128 devices in a mesh: line: 4 (over y), xline: 32 (over z, x, core).
Axes of the slice: x: 4, y: 4, z: 4, core: 2. Of those that a mesh axis runs over, the one named last changes fastest.
Arguments:
- traces: bfloat16 [4, 8192, 1024], P('line', 'xline'), may hold values from -6 to 6
- taper: float32 [128], replicated, may hold values from 0.3 to 1
- ray_param: float32 [64], replicated, may hold values from -0.4 to 0.4
- reach: int32 [4, 8192, 4], P('line', 'xline'), may hold values from 0 to 127, all different within a row; in each aligned block of 256 rows (0 to 255, 256 to 511, ..., all dimensions but the last counted through in order) at most 9 rows name the same one
- landing: int32 [4, 8192, 4], P('line', 'xline'), may hold values from 0 to 127
- travel_time: float32 [64, 1024], P('xline'), may hold values from 2 to 40
- amplitude: float32 [64, 1024], P('xline'), may hold values from 0.3 to 3
Outputs:
- image: float32 [4, 1024, 4096], P('line', None, 'xline')
The draws below stay inside these ranges and needn't reach their ends.
Inputs may be any that keep to these rules, and one draw needn't show every extreme that they name: `reach`: in the rows of one device no tile is named more than 9 times, a bound that some block reaches.
All inputs are finite; a program needn't handle non-finite values.
Results may differ from the reference program's by a relative error of at most 0.0057.
Values may be sent and summed in bfloat16 or wider, within the bound.
No kernel may reach another device: no remote copies, remote signals or barrier semaphores. Data moves between devices by JAX's collectives and lax.ppermute only.
A program may use at most 64 MiB of HBM per device.

```python
import math
import jax
import jax.numpy as jnp
import numpy as np
from jax import lax

F = 512
P_SIZE = 64
K = 128
X = 128
Z = 1024
C_DEV = 4
TOP = 4
CAP = 9
NC = 128
TRACES = 8192
N_LINE = 4
N_XLINE = 32
DEVICES = 128


def touch_ends(values, rng, smallest, top_value):
    dims = values.shape
    place = [jax.random.randint(jax.random.fold_in(rng, axis), (), 0, dims[axis]) for axis in range(len(dims))]
    values = values.at[tuple(place)].set(smallest)
    longest = dims.index(max(dims))
    place[longest] = (place[longest] + 1) % dims[longest]
    return values.at[tuple(place)].set(top_value)


def shard_levels(key, dims, cuts, low, high):
    gain, own = 1.0, jax.random.fold_in(key, 6)
    for dim, parts in cuts:
        draws = jnp.exp(jax.random.uniform(jax.random.fold_in(own, dim), (parts,), jnp.float32, low / len(cuts), high / len(cuts)))
        gain = gain * jnp.repeat(draws, dims[dim] // parts).reshape([-1 if axis == dim else 1 for axis in range(len(dims))])
    return gain


def shared_out(stream_key, own, number, rows, number_of, top, limit, skew):
    ranking = jax.random.permutation(stream_key, number_of)
    heavy_load, ordinary = load_shares(number_of, rows * top, limit, skew, True), load_shares(number_of, rows * top, limit, skew, False)
    places = jnp.arange(number_of)

    def named(sizes, offset_by):
        used = int((sizes > 0).sum())
        fixed = max(1, used // 4)
        moved = fixed + (places - fixed + offset_by * (used - fixed)) % max(1, number_of - fixed)
        return jnp.zeros((number_of,), jnp.int32).at[ranking[jnp.where(places < fixed, places, moved)]].set(jnp.asarray(sizes, jnp.int32))

    sizes = jnp.where(number % 4 == 0, named(heavy_load, number // 4), named(ordinary, number - number // 4 - 1))
    mixed = jax.random.permutation(jax.random.fold_in(own, 3), number_of)
    giver, receiver = mixed[0:number_of // 2 * 2:2], mixed[1:number_of // 2 * 2:2]
    slack = jnp.minimum(sizes[giver] - 1, limit - sizes[receiver]) // 2
    slack = jnp.where((giver == ranking[0]) | (receiver == ranking[0]) | (sizes[receiver] == 0), 0, jnp.maximum(slack, 0))
    moved = jax.random.randint(jax.random.fold_in(own, 4), (number_of // 2,), 0, 1 << 20) % (slack + 1)
    sizes = sizes.at[giver].add(-moved).at[receiver].add(moved)
    items = jnp.searchsorted(jnp.cumsum(sizes), jnp.arange(rows * top), side="right").astype(jnp.int32)
    listing = items.reshape(top, rows).T
    listing = listing[jax.random.permutation(jax.random.fold_in(own, 1), rows)]
    offset_by = jax.random.randint(jax.random.fold_in(own, 2), (rows, 1), 0, top)
    return jnp.take_along_axis(listing, (jnp.arange(top)[None, :] + offset_by) % top, axis=1)


def load_shares(count, total, limit, lean, full):
    weights = [(1 << 20) // math.isqrt(grade ** lean) + 1 for grade in range(1, count + 1)]
    largest = limit if full else min(limit, max(-(-total // count), total * weights[0] // sum(weights)))
    least = 1 if total - largest >= count - 1 else 0
    holding, rest = [largest] + [least] * (count - 1), total - largest - least * (count - 1)
    while rest > 0:
        free = [i for i in range(1, count) if holding[i] < largest] or [i for i in range(1, count) if holding[i] < limit]
        whole, remaining = sum([weights[i] for i in free]), rest
        for i in free:
            addition = min(limit - holding[i], max(1, remaining * weights[i] // whole), rest)
            holding[i] = holding[i] + addition
            rest = rest - addition
    return np.array(holding)


def centred(rng, dims, scale, bound, cuts=(), kind=jnp.bfloat16):
    result = scale * jax.random.normal(rng, dims, jnp.float32)
    if cuts:
        result = result * shard_levels(rng, dims, cuts, -0.22, 0.18)
    return jnp.clip(result, -bound, bound).astype(kind)


def setup_inputs(seed: int = 0) -> dict:
    arg_keys = jax.random.split(jax.random.key(seed), 8)
    traces = centred(arg_keys[0], (N_LINE, TRACES, 2 * F), 1.0, 6.0, ((0, 4), (1, 32)))
    taper = jnp.clip(jax.random.uniform(arg_keys[1], (K,), jnp.float32, 0.3, 1.0), 0.3, 1.0)
    ray_param = jnp.clip(jax.random.uniform(arg_keys[2], (P_SIZE,), jnp.float32, -0.4, 0.4), -0.4, 0.4)
    reach_keys = jax.random.split(jax.random.fold_in(arg_keys[3], 1), N_LINE * (NC * P_SIZE) // (C_DEV * P_SIZE))
    reach_turns = jax.random.permutation(jax.random.fold_in(arg_keys[3], 3), N_LINE * (NC * P_SIZE) // (C_DEV * P_SIZE))
    reach = jax.vmap(lambda own, number: shared_out(jax.random.fold_in(arg_keys[3], 2), own, number, C_DEV * P_SIZE, DEVICES, TOP, CAP, 1))(reach_keys, reach_turns).reshape((N_LINE, NC * P_SIZE, TOP))
    landing = touch_ends(jax.random.randint(arg_keys[4], (N_LINE, NC * P_SIZE, TOP), 0, X), jax.random.fold_in(arg_keys[4], 1), 0, X - 1).astype(jnp.int32)
    travel_time = jnp.clip(2.0 + 38.0 * jax.random.uniform(arg_keys[5], (P_SIZE, Z), jnp.float32) ** shard_levels(arg_keys[5], (P_SIZE, Z), ((0, 32),), -0.2, 0.2), 2.0, 40.0)
    amplitude = jnp.clip(jnp.exp(math.log(3.0) - 2.3025851 * jax.random.uniform(arg_keys[6], (P_SIZE, Z), jnp.float32) ** shard_levels(arg_keys[6], (P_SIZE, Z), ((0, 32),), -0.2, 0.2)), 0.3, 3.0)
    return dict(traces=traces, taper=taper, ray_param=ray_param, reach=reach, landing=landing, travel_time=travel_time, amplitude=amplitude)


def steering(taper, ray_param, window, freq_count):
    offsets = jnp.arange(window, dtype=jnp.float32) - (window - 1) / 2.0
    angular = (jnp.arange(freq_count, dtype=jnp.float32) + 1.0) * (math.pi / freq_count)
    phase = ray_param[:, None, None] * offsets[None, :, None] * angular[None, None, :]
    weight = taper[None, :, None] / math.sqrt(window)
    return ((weight * jnp.cos(phase)).astype(jnp.bfloat16), (weight * jnp.sin(phase)).astype(jnp.bfloat16))

def kernel_slab(time_row, amp_row, freq_count, factor):
    angular = (jnp.arange(freq_count, dtype=jnp.float32) + 1.0) * (math.pi / freq_count)
    phase = time_row[..., None] * angular
    weight = amp_row[..., None] * factor
    return jnp.concatenate([weight * jnp.cos(phase), weight * jnp.sin(phase)], axis=-1).astype(jnp.bfloat16)

def slant_line(halves, cos_weight, sin_weight, half_window, freq_count):
    lower_half = halves[:-1]
    upper_half = halves[1:]
    real_part = jnp.zeros((lower_half.shape[0], cos_weight.shape[0], freq_count), jnp.float32)
    imag_part = jnp.zeros((lower_half.shape[0], cos_weight.shape[0], freq_count), jnp.float32)
    for section, lower in ((lower_half, 0), (upper_half, half_window)):
        cos_part = cos_weight[:, lower:lower + half_window, :].astype(jnp.float32)
        sin_part = sin_weight[:, lower:lower + half_window, :].astype(jnp.float32)
        data_real = section[..., :freq_count].astype(jnp.float32)
        data_imag = section[..., freq_count:].astype(jnp.float32)
        real_part = real_part + jnp.einsum('nkf,pkf->npf', data_real, cos_part) + jnp.einsum('nkf,pkf->npf', data_imag, sin_part)
        imag_part = imag_part + jnp.einsum('nkf,pkf->npf', data_imag, cos_part) - jnp.einsum('nkf,pkf->npf', data_real, sin_part)
    return jnp.concatenate([real_part, imag_part], axis=-1).astype(jnp.bfloat16)

def reference(traces, taper, ray_param, reach, landing, travel_time, amplitude):
    cos_weight, sin_weight = steering(taper, ray_param, K, F)
    half_window = K // 2
    padded = jnp.pad(traces, ((0, 0), (K // 4, K // 4), (0, 0)))
    halves = padded.reshape(N_LINE, NC + 1, half_window, 2 * F)
    beam_block = lax.map(lambda line_halves: slant_line(line_halves, cos_weight, sin_weight, half_window, F), halves)
    column_keys = (reach * X + landing).reshape(N_LINE, NC, P_SIZE, TOP)
    tiles = N_LINE * N_XLINE
    factor = 1.0 / math.sqrt(2.0 * F * C_DEV * P_SIZE * TOP / X)

    def one_bin(running, bin_index):
        beam_rows = lax.dynamic_index_in_dim(beam_block, bin_index, 2, keepdims=False)
        beam_rows = beam_rows.reshape(N_LINE * NC, 2 * F)
        time_row = lax.dynamic_index_in_dim(travel_time, bin_index, 0, keepdims=False)
        amp_row = lax.dynamic_index_in_dim(amplitude, bin_index, 0, keepdims=False)
        kernel = kernel_slab(time_row, amp_row, F, factor)
        projected = lax.dot_general(beam_rows, kernel, (((1,), (1,)), ((), ())), preferred_element_type=jnp.float32)
        projected = projected.astype(jnp.bfloat16).astype(jnp.float32)
        landing_keys = lax.dynamic_index_in_dim(column_keys, bin_index, 2, keepdims=False)
        landing_keys = landing_keys.reshape(N_LINE * NC, TOP)
        for reach_slot in range(TOP):
            running = running.at[landing_keys[:, reach_slot]].add(projected)
        return (running, None)
    summed, unused = lax.scan(one_bin, jnp.zeros((tiles * X, Z), jnp.float32), jnp.arange(P_SIZE, dtype=jnp.int32))
    return summed.reshape(N_LINE, N_XLINE, X, Z).transpose(0, 3, 1, 2).reshape(N_LINE, Z, N_XLINE * X)
```

```python
import functools
import math

import jax
import jax.numpy as jnp
import numpy as np
from jax import lax
from jax.experimental import pallas as pl
from jax.experimental.pallas import tpu as pltpu
from jax.sharding import PartitionSpec as P

X = 128
FINE = 128
SLOTS = 9


def iota(shape, dim):
    return lax.broadcasted_iota(jnp.int32, shape, dim)


def fold_matrix():
    half = FINE // 2
    plus = np.zeros((FINE, half), np.float32)
    minus = np.zeros((FINE, half), np.float32)
    for m in range(half):
        plus[half + m, m] = plus[half - 1 - m, m] = 1.0
        minus[half + m, m], minus[half - 1 - m, m] = 1.0, -1.0
    zero = np.zeros_like(plus)
    real = np.concatenate([plus, zero, zero, -minus], 1)
    imag = np.concatenate([zero, minus, plus, zero], 1)
    return np.concatenate([real, imag], 0)


def slant_kernel(before, own, after, tap, ray, flip, fold, out, combos, beams):
    freqs = combos.shape[0] * 128
    half = combos.shape[1]
    centres = combos.shape[2] // 4
    flat = combos.reshape(freqs // 128, half * 4 * centres, 128)
    for n in range(centres):
        start = n * half - half // 2
        if n == 0:
            low = jnp.concatenate([before[...], own[: half // 2]], 0)
        else:
            low = own[start : start + half]
        if n == centres - 1:
            high = jnp.concatenate([own[start + half :], after[...]], 0)
        else:
            high = own[start + half : start + 2 * half]
        turned = jnp.dot(flip[...], low, preferred_element_type=jnp.float32) * tap[0]
        high = high.astype(jnp.float32) * tap[1]
        total, diff = high + turned, high - turned
        for block in range(freqs // 128):
            for q in range(4):
                value = (total, diff)[q // 2]
                cut = (q % 2) * freqs + block * 128
                rows = pl.ds(q * centres + n, half, stride=4 * centres)
                flat[block, rows, :] = value[:, cut : cut + 128]

    rays = ray.shape[0]
    group = 2
    blocks = rays // (8 * group)

    def one_tile(tile, carry):
        block, first = tile // blocks, (tile % blocks) * 8 * group
        angular = (iota((8, 128), 1) + (block * 128 + 1)).astype(jnp.float32) * (math.pi / freqs)
        state = []
        steps = []
        for g in range(group):
            rows = pl.ds(pl.multiple_of(first + 8 * g, 8), 8)
            angle = ray[rows, :] * 0.5 * angular
            c, s = jnp.cos(angle), jnp.sin(angle)
            state += [c, s]
            steps += [(1.0 - 2.0 * s * s, 2.0 * s * c)]
        zero = jnp.zeros((8, 128), jnp.float32)
        sums = [zero] * (2 * group * centres)

        def one_offset(j, current):
            state, sums = list(current[0]), list(current[1])
            for n in range(centres):
                pr, pi, mr, mi = (
                    jnp.broadcast_to(combos[block, j, q * centres + n : q * centres + n + 1, :], (8, 128))
                    for q in range(4)
                )
                for g in range(group):
                    c, s = state[2 * g], state[2 * g + 1]
                    at = 2 * (g * centres + n)
                    sums[at] = sums[at] + (c * pr + s * mi)
                    sums[at + 1] = sums[at + 1] + (c * pi - s * mr)
            for g in range(group):
                c, s = state[2 * g], state[2 * g + 1]
                cs, ss = steps[g]
                state[2 * g], state[2 * g + 1] = c * cs - s * ss, s * cs + c * ss
            return tuple(state), tuple(sums)

        state, sums = lax.fori_loop(0, half, one_offset, (tuple(state), tuple(sums)), unroll=4)
        for g in range(group):
            for n in range(centres):
                at = 2 * (g * centres + n)
                row = pl.multiple_of((block * centres + n) * rays + first + 8 * g, 8)
                beams[pl.ds(row, 8), 0:128] = sums[at]
                beams[pl.ds(row, 8), 128:256] = sums[at + 1]
        return carry

    lax.fori_loop(0, (freqs // 128) * blocks, one_tile, 0)
    rows = centres * rays
    flat = out.reshape(rays * out.shape[1], 128)
    for block in range(freqs // 128):
        folded = jnp.dot(
            beams[block * rows : (block + 1) * rows].astype(jnp.bfloat16),
            fold[...],
            preferred_element_type=jnp.float32,
        )
        for n in range(centres):
            for v in range(2):
                row = (2 * block + v) * centres + n
                value = folded[n * rays : (n + 1) * rays, 128 * v : 128 * (v + 1)]
                flat[pl.ds(row, rays, stride=out.shape[1]), :] = value


def project_kernel(factor, coarse, centres, times, folded, rank, keys, out, fine, outer, proj):
    half = FINE // 2
    blocks = fine.shape[0]
    bases = times.shape[0]
    upper = iota((2 * centres, 128 * blocks), 0) < centres

    def one_group(base, r):
        c0s, s0s, c1s, s1s = [], [], [], []
        for zb in range(blocks):
            cols = slice(zb * 128, zb * 128 + 128)
            t = times[base, pl.ds(8 * r + zb, 8, stride=32), :]
            amp = times[base, pl.ds(16 + 8 * r + zb, 8, stride=32), :] * factor
            angle = t * (math.pi / (2 * coarse * FINE))
            c0, s0 = jnp.cos(angle), jnp.sin(angle)
            c1, s1 = 1.0 - 2.0 * s0 * s0, 2.0 * s0 * c0
            c, s = c1, s1
            for _ in range(6):
                c, s = 1.0 - 2.0 * s * s, 2.0 * s * c
            ca, sa = (c * c0 - s * s0) * amp, (s * c0 + c * s0) * amp
            cb, sb = 1.0 - 2.0 * s * s, 2.0 * s * c
            for a in range(coarse):
                outer[16 * a : 16 * a + 8, cols] = ca
                outer[16 * a + 8 : 16 * a + 16, cols] = sa
                ca, sa = ca * cb - sa * sb, sa * cb + ca * sb
            c0s, s0s, c1s, s1s = c0s + [c0], s0s + [s0], c1s + [c1], s1s + [s1]

        def one_step(m, state):
            cs, ss = state
            row, low = pl.multiple_of(m * 8, 8), pl.multiple_of((half + m) * 8, 8)
            for zb in range(blocks):
                fine[zb, pl.ds(row, 8), :] = cs[zb]
                fine[zb, pl.ds(low, 8), :] = ss[zb]
            turned = [
                (c * c1 - s * s1, s * c1 + c * s1) for c, s, c1, s1 in zip(cs, ss, c1s, s1s)
            ]
            return tuple(c for c, _ in turned), tuple(s for _, s in turned)

        lax.fori_loop(0, half, one_step, (tuple(c0s), tuple(s0s)), unroll=4)
        for i in range(8):
            p = base * 16 + 2 * i + r
            weights = jnp.concatenate(
                [fine[zb, pl.ds(i, FINE, stride=8), :].astype(jnp.bfloat16) for zb in range(blocks)],
                1,
            )
            rows = folded[p].astype(jnp.bfloat16)
            parts = jnp.dot(rows, weights, preferred_element_type=jnp.float32)
            total = jnp.zeros(upper.shape, jnp.float32)
            for a in range(coarse):
                turn = jnp.where(
                    upper,
                    jnp.broadcast_to(outer[16 * a + i : 16 * a + i + 1, :], upper.shape),
                    jnp.broadcast_to(outer[16 * a + 8 + i : 16 * a + 9 + i, :], upper.shape),
                )
                total = total + parts[2 * centres * a : 2 * centres * (a + 1)] * turn
            total = total + pltpu.roll(total, centres, 0)
            if i % 2 == 0:
                held = total
            else:
                proj[(r * bases + base) * 4 + i // 2] = jnp.where(upper, held, total)

    def one_base(base, carry):
        one_group(base, 0)
        one_group(base, 1)
        return carry

    lax.fori_loop(0, bases, one_base, 0)

    sends = proj[...].reshape(-1, 128 * blocks).astype(jnp.bfloat16)
    devices, rows = rank.shape
    ranks = jnp.broadcast_to(rank[...][:, None, :], (devices, 8, rows)).reshape(devices * 8, rows)
    lane8 = iota((devices * 8, rows), 0) % 8
    pick = (ranks == lane8.astype(jnp.float32)).astype(jnp.bfloat16)
    for k in range(4):
        y = jnp.dot(pick, sends[:, 256 * k : 256 * (k + 1)], preferred_element_type=jnp.float32)
        pair = [y[:, :128].reshape(devices, 8, 128), y[:, 128:].reshape(devices, 8, 128)]
        out[:, 16 * k : 16 * (k + 1), :] = jnp.concatenate(pair, 1).astype(jnp.bfloat16)
    last = jnp.zeros((devices * 8, 128), jnp.float32)
    for k in range(8):
        pick = ((ranks == 8.0) & (lane8 == k)).astype(jnp.bfloat16)
        last += jnp.dot(pick, sends[:, 128 * k : 128 * (k + 1)], preferred_element_type=jnp.float32)
    tags = jnp.broadcast_to(keys[...][:, None, :], (devices, 8, 128))
    pair = [last.reshape(devices, 8, 128), tags]
    out[:, 64:80, :] = jnp.concatenate(pair, 1).astype(jnp.bfloat16)


def route_kernel(reach, landing, earlier, rank, keys):
    devices, rows = rank.shape
    tile = iota((devices, rows), 0)
    named = jnp.zeros((devices, rows), jnp.float32)
    column = jnp.zeros((devices, rows), jnp.float32)
    for t in range(reach.shape[0]):
        hit = jnp.broadcast_to(reach[t : t + 1, :], (devices, rows)) == tile
        land = jnp.broadcast_to(landing[t : t + 1, :], (devices, rows)).astype(jnp.float32)
        named = named + jnp.where(hit, 1.0, 0.0)
        column = column + jnp.where(hit, land + 1.0, 0.0)
    count = jnp.dot(named.astype(jnp.bfloat16), earlier[...], preferred_element_type=jnp.float32)
    slot = jnp.where(named > 0.0, count, -1.0)
    rank[...] = slot
    lane = iota((devices, 128), 1)
    table = jnp.zeros((devices, 128), jnp.float32)
    for k in range(SLOTS):
        value = jnp.sum(jnp.where(slot == k, column, 0.0), axis=1, keepdims=True)
        table = jnp.where(lane == k, value, table)
    keys[...] = table - 1.0


def place_kernel(incoming, image):
    devices = incoming.shape[0]
    tags = incoming[:, 64:80, :].astype(jnp.float32)[:, 8:16, :]
    tags = jnp.concatenate([tags, tags], 1).reshape(devices * 16, 128)
    lane = iota((devices * 16, 128), 1)
    row = iota((devices * 16, 128), 0) % 16
    key = jnp.sum(jnp.where(lane == row % 8, tags, 0.0), axis=1, keepdims=True)
    key9 = jnp.sum(jnp.where(lane == 8, tags, 0.0), axis=1, keepdims=True)
    lanes = lane.astype(jnp.float32)
    hit = key == lanes
    both = jnp.concatenate(
        [
            (hit & (row < 8)).astype(jnp.bfloat16),
            (hit & (row >= 8)).astype(jnp.bfloat16),
        ],
        1,
    )
    hit9 = key9 == lanes
    contract = (((0,), (0,)), ((), ()))
    tail = incoming[:, 64:80, :].reshape(devices * 16, 128)
    for k in range(4):
        rows = incoming[:, 16 * k : 16 * (k + 1), :].reshape(devices * 16, 128)
        y = lax.dot_general(rows, both, contract, preferred_element_type=jnp.float32)
        nine = jnp.concatenate(
            [(hit9 & (row == 2 * k + q)).astype(jnp.bfloat16) for q in range(2)], 1
        )
        y += lax.dot_general(tail, nine, contract, preferred_element_type=jnp.float32)
        image[256 * k : 256 * k + 128, :] = y[:, :128]
        image[256 * k + 128 : 256 * (k + 1), :] = y[:, 128:]


def vmem(count):
    return [pl.BlockSpec(memory_space=pltpu.VMEM)] * count


def call(kernel, shapes, args, scratch=()):
    return pl.pallas_call(
        kernel,
        out_shape=shapes,
        in_specs=vmem(len(args)),
        out_specs=jax.tree.map(lambda _: pl.BlockSpec(memory_space=pltpu.VMEM), shapes),
        scratch_shapes=list(scratch),
        compiler_params=pltpu.CompilerParams(vmem_limit_bytes=56 * 1024 * 1024),
    )(*args)


def on_device(traces, taper, ray_param, reach, landing, travel_time, amplitude):
    f32, bf16 = jnp.float32, jnp.bfloat16
    freqs = traces.shape[2] // 2
    window = taper.shape[0]
    half = window // 2
    rays = ray_param.shape[0]
    rows = traces.shape[1]
    centres = rows // half
    depth = travel_time.shape[1]
    reach_count = reach.shape[2]
    line_count, size = lax.axis_size("line"), lax.axis_size("xline")
    devices = line_count * size
    coarse = freqs // FINE
    factor = 1.0 / math.sqrt(2.0 * freqs * centres * rays * reach_count / X)

    own = traces[0]
    up = [(i, i + 1) for i in range(size - 1)]
    down = [(j, i) for i, j in up]
    before = lax.ppermute(own[rows - half // 2 :], "xline", up)
    after = lax.ppermute(own[: half // 2], "xline", down)
    mine = jnp.concatenate([travel_time.reshape(-1, 128), amplitude.reshape(-1, 128)], 0)
    mine = jnp.broadcast_to(mine[None], (size,) + mine.shape)
    times = lax.all_to_all(mine, "xline", split_axis=0, concat_axis=0, tiled=True)
    times = times.reshape(size // 8, 8 * mine.shape[1], 128)

    def beam_order(table):
        table = table.reshape(centres, rays // 16, 4, 2, 2, reach_count)
        return table.transpose(5, 4, 1, 2, 3, 0).reshape(reach_count, centres * rays)


    beam_count = centres * rays
    earlier = np.triu(np.ones((beam_count, beam_count), np.float32), 1)
    rank, keys = call(
        route_kernel,
        (
            jax.ShapeDtypeStruct((devices, beam_count), f32),
            jax.ShapeDtypeStruct((devices, 128), f32),
        ),
        (beam_order(reach[0]), beam_order(landing[0]), jnp.asarray(earlier, bf16)),
    )

    weight = taper * (1.0 / math.sqrt(window))
    tap = jnp.stack([weight[:half][::-1], weight[half:]])[:, :, None]
    flip = jnp.asarray(np.eye(half, dtype=np.float32)[::-1], bf16)
    folded = call(
        slant_kernel,
        jax.ShapeDtypeStruct((rays, 2 * coarse * centres, FINE), f32),
        (before, own, after, tap, ray_param[:, None], flip, jnp.asarray(fold_matrix(), bf16)),
        [
            pltpu.VMEM((freqs // 128, half, 4 * centres, 128), f32),
            pltpu.VMEM((coarse * beam_count, 2 * FINE), f32),
        ],
    )
    outgoing = call(
        functools.partial(project_kernel, factor, coarse, centres),
        jax.ShapeDtypeStruct((devices, 80, 128), bf16),
        (times, folded, rank, keys),
        [
            pltpu.VMEM((depth // 128, 8 * FINE, 128), f32),
            pltpu.VMEM((16 * coarse, depth), f32),
            pltpu.VMEM((beam_count // (2 * centres), 2 * centres, depth), f32),
        ],
    )
    incoming = lax.all_to_all(
        outgoing, ("line", "xline"), split_axis=0, concat_axis=0, tiled=True
    )
    image = call(place_kernel, jax.ShapeDtypeStruct((depth, X), f32), (incoming,))
    return image[None]


def solution(mesh):
    placed = (
        P("line", "xline", None),
        P(),
        P(),
        P("line", "xline", None),
        P("line", "xline", None),
        P("xline", None),
        P("xline", None),
    )
    return jax.shard_map(
        on_device, mesh=mesh, in_specs=placed, out_specs=P("line", None, "xline"), check_vma=False
    )
```

```python
import functools
import math

import jax
import jax.numpy as jnp
import numpy as np
from jax import lax
from jax.experimental import pallas as pl
from jax.experimental.pallas import tpu as pltpu
from jax.sharding import PartitionSpec as P

X = 128
FINE = 128
SLOTS = 9


def iota(shape, dim):
    return lax.broadcasted_iota(jnp.int32, shape, dim)


def fold_matrix():
    half = FINE // 2
    plus = np.zeros((FINE, half), np.float32)
    minus = np.zeros((FINE, half), np.float32)
    for m in range(half):
        plus[half + m, m] = plus[half - 1 - m, m] = 1.0
        minus[half + m, m], minus[half - 1 - m, m] = 1.0, -1.0
    zero = np.zeros_like(plus)
    real = np.concatenate([plus, zero, zero, -minus], 1)
    imag = np.concatenate([zero, minus, plus, zero], 1)
    return np.concatenate([real, imag], 0)


def slant_kernel(before, own, after, tap, ray, flip, fold, out, combos, beams):
    freqs = combos.shape[0] * 128
    half = combos.shape[1]
    centres = combos.shape[2] // 4
    flat = combos.reshape(freqs // 128, half * 4 * centres, 128)
    for n in range(centres):
        start = n * half - half // 2
        if n == 0:
            low = jnp.concatenate([before[...], own[: half // 2]], 0)
        else:
            low = own[start : start + half]
        if n == centres - 1:
            high = jnp.concatenate([own[start + half :], after[...]], 0)
        else:
            high = own[start + half : start + 2 * half]
        turned = jnp.dot(flip[...], low, preferred_element_type=jnp.float32) * tap[0]
        high = high.astype(jnp.float32) * tap[1]
        total, diff = high + turned, high - turned
        for block in range(freqs // 128):
            for q in range(4):
                value = (total, diff)[q // 2]
                cut = (q % 2) * freqs + block * 128
                rows = pl.ds(q * centres + n, half, stride=4 * centres)
                flat[block, rows, :] = value[:, cut : cut + 128]

    rays = ray.shape[0]
    group = 2
    blocks = rays // (8 * group)

    def one_tile(tile, carry):
        block, first = tile // blocks, (tile % blocks) * 8 * group
        angular = (iota((8, 128), 1) + (block * 128 + 1)).astype(jnp.float32) * (math.pi / freqs)
        state = []
        steps = []
        for g in range(group):
            rows = pl.ds(pl.multiple_of(first + 8 * g, 8), 8)
            angle = ray[rows, :] * 0.5 * angular
            c, s = jnp.cos(angle), jnp.sin(angle)
            state += [c, s]
            steps += [(1.0 - 2.0 * s * s, 2.0 * s * c)]
        zero = jnp.zeros((8, 128), jnp.float32)
        sums = [zero] * (2 * group * centres)

        def one_offset(j, current):
            state, sums = list(current[0]), list(current[1])
            for n in range(centres):
                pr, pi, mr, mi = (
                    jnp.broadcast_to(combos[block, j, q * centres + n : q * centres + n + 1, :], (8, 128))
                    for q in range(4)
                )
                for g in range(group):
                    c, s = state[2 * g], state[2 * g + 1]
                    at = 2 * (g * centres + n)
                    sums[at] = sums[at] + (c * pr + s * mi)
                    sums[at + 1] = sums[at + 1] + (c * pi - s * mr)
            for g in range(group):
                c, s = state[2 * g], state[2 * g + 1]
                cs, ss = steps[g]
                state[2 * g], state[2 * g + 1] = c * cs - s * ss, s * cs + c * ss
            return tuple(state), tuple(sums)

        state, sums = lax.fori_loop(0, half, one_offset, (tuple(state), tuple(sums)), unroll=4)
        for g in range(group):
            for n in range(centres):
                at = 2 * (g * centres + n)
                row = pl.multiple_of((block * centres + n) * rays + first + 8 * g, 8)
                beams[pl.ds(row, 8), 0:128] = sums[at]
                beams[pl.ds(row, 8), 128:256] = sums[at + 1]
        return carry

    lax.fori_loop(0, (freqs // 128) * blocks, one_tile, 0)
    rows = centres * rays
    flat = out.reshape(rays * out.shape[1], 128)
    for block in range(freqs // 128):
        folded = jnp.dot(
            beams[block * rows : (block + 1) * rows].astype(jnp.bfloat16),
            fold[...],
            preferred_element_type=jnp.float32,
        )
        for n in range(centres):
            for v in range(2):
                row = (2 * block + v) * centres + n
                value = folded[n * rays : (n + 1) * rays, 128 * v : 128 * (v + 1)]
                flat[pl.ds(row, rays, stride=out.shape[1]), :] = value


def project_kernel(factor, coarse, centres, times, folded, rank, keys, out, seed, step, outer, proj, ninth):
    half = FINE // 2
    blocks = seed.shape[0]
    bases = times.shape[0]
    upper = iota((2 * centres, 128 * blocks), 0) < centres

    def one_group(base, r):
        for zb in range(blocks):
            cols = slice(zb * 128, zb * 128 + 128)
            t = times[base, pl.ds(8 * r + zb, 8, stride=32), :]
            amp = times[base, pl.ds(16 + 8 * r + zb, 8, stride=32), :] * factor
            angle = t * (math.pi / (2 * coarse * FINE))
            c0, s0 = jnp.cos(angle), jnp.sin(angle)
            c1, s1 = 1.0 - 2.0 * s0 * s0, 2.0 * s0 * c0
            c, s = c0, s0
            for m in range(8):
                seed[zb, m * 8 : m * 8 + 8, :] = c
                seed[zb, 64 + m * 8 : 72 + m * 8, :] = s
                if m < 7:
                    c, s = c * c1 - s * s1, s * c1 + c * s1
            c, s = c1, s1
            for power in range(6):
                c, s = 1.0 - 2.0 * s * s, 2.0 * s * c
                if power == 2:
                    step[0:8, cols] = c
                    step[8:16, cols] = s
            ca, sa = (c * c0 - s * s0) * amp, (s * c0 + c * s0) * amp
            cb, sb = 1.0 - 2.0 * s * s, 2.0 * s * c
            for a in range(coarse):
                outer[16 * a : 16 * a + 8, cols] = ca
                outer[16 * a + 8 : 16 * a + 16, cols] = sa
                ca, sa = ca * cb - sa * sb, sa * cb + ca * sb
        for i in range(8):
            p = base * 16 + 2 * i + r
            rows = folded[p].astype(jnp.bfloat16)
            weights = []
            for zb in range(blocks):
                cols = slice(zb * 128, zb * 128 + 128)
                c = seed[zb, pl.ds(i, 8, stride=8), :]
                s = seed[zb, pl.ds(64 + i, 8, stride=8), :]
                cs = jnp.broadcast_to(step[i : i + 1, cols], (8, 128))
                ss = jnp.broadcast_to(step[8 + i : 9 + i, cols], (8, 128))
                real, imag = [c], [s]
                for _ in range(half // 8 - 1):
                    c, s = c * cs - s * ss, s * cs + c * ss
                    real.append(c)
                    imag.append(s)
                weights.append(jnp.concatenate(real + imag, 0).astype(jnp.bfloat16))
            parts = jnp.dot(
                rows, jnp.concatenate(weights, 1), preferred_element_type=jnp.float32
            )
            total = jnp.zeros(upper.shape, jnp.float32)
            for a in range(coarse):
                turn = jnp.where(
                    upper,
                    jnp.broadcast_to(outer[16 * a + i : 16 * a + i + 1, :], upper.shape),
                    jnp.broadcast_to(outer[16 * a + 8 + i : 16 * a + 9 + i, :], upper.shape),
                )
                total = total + parts[2 * centres * a : 2 * centres * (a + 1)] * turn
            total = total + pltpu.roll(total, centres, 0)
            if i % 2 == 0:
                held = total
            else:
                proj[(r * bases + base) * 4 + i // 2] = jnp.where(upper, held, total)

    def one_base(base, carry):
        one_group(base, 0)
        one_group(base, 1)
        return carry

    lax.fori_loop(0, bases, one_base, 0)

    sends = proj[...].reshape(-1, 128 * blocks).astype(jnp.bfloat16)
    devices, rows = rank.shape
    ranks = jnp.broadcast_to(rank[...][:, None, :], (devices, 8, rows)).reshape(devices * 8, rows)
    lane8 = iota((devices * 8, rows), 0) % 8
    pick = (ranks == lane8.astype(jnp.float32)).astype(jnp.bfloat16)
    for k in range(4):
        y = jnp.dot(pick, sends[:, 256 * k : 256 * (k + 1)], preferred_element_type=jnp.float32)
        pair = [y[:, :128].reshape(devices, 8, 128), y[:, 128:].reshape(devices, 8, 128)]
        out[:, 16 * k : 16 * (k + 1), :] = jnp.concatenate(pair, 1).astype(jnp.bfloat16)
    last = jnp.dot(
        (rank[...] == 8.0).astype(jnp.bfloat16), sends, preferred_element_type=jnp.float32
    )
    for k in range(8):
        ninth[pl.ds(k, devices, stride=8), :] = last[:, 128 * k : 128 * (k + 1)]
    tags = jnp.broadcast_to(keys[...][:, None, :], (devices, 8, 128))
    pair = [ninth[...].reshape(devices, 8, 128), tags]
    out[:, 64:80, :] = jnp.concatenate(pair, 1).astype(jnp.bfloat16)


def route_kernel(reach, landing, earlier, order, rank, keys):
    devices, rows = rank.shape
    tile = iota((devices, rows), 0)
    named = jnp.zeros((devices, rows), jnp.float32)
    column = jnp.zeros((devices, rows), jnp.float32)
    for t in range(reach.shape[0]):
        hit = jnp.broadcast_to(reach[t : t + 1, :], (devices, rows)) == tile
        land = jnp.broadcast_to(landing[t : t + 1, :], (devices, rows)).astype(jnp.float32)
        named = named + jnp.where(hit, 1.0, 0.0)
        column = column + jnp.where(hit, land + 1.0, 0.0)
    count = jnp.dot(named.astype(jnp.bfloat16), earlier[...], preferred_element_type=jnp.float32)
    slot = jnp.where(named > 0.0, count, -1.0)
    rank[...] = jnp.dot(
        slot.astype(jnp.bfloat16), order[...], preferred_element_type=jnp.float32
    )
    lane = iota((devices, 128), 1)
    table = jnp.zeros((devices, 128), jnp.float32)
    for k in range(SLOTS):
        value = jnp.sum(jnp.where(slot == k, column, 0.0), axis=1, keepdims=True)
        table = jnp.where(lane == k, value, table)
    keys[...] = table - 1.0


def spread_kernel(times, amps, out):
    rows = [table[r : r + 1, :] for table in (times, amps) for r in range(table.shape[0])]
    lanes = range(0, times.shape[1], 128)
    tile = jnp.concatenate([row[:, at : at + 128] for row in rows for at in lanes], 0)
    out[...] = jnp.broadcast_to(tile[None], out.shape)


def place_kernel(incoming, image):
    devices = incoming.shape[0]
    tags = incoming[:, 64:80, :].astype(jnp.float32)[:, 8:16, :]
    tags = jnp.concatenate([tags, tags], 1).reshape(devices * 16, 128)
    lane = iota((devices * 16, 128), 1)
    row = iota((devices * 16, 128), 0) % 16
    key = jnp.sum(jnp.where(lane == row % 8, tags, 0.0), axis=1, keepdims=True)
    key9 = jnp.sum(jnp.where(lane == 8, tags, 0.0), axis=1, keepdims=True)
    lanes = lane.astype(jnp.float32)
    hit = key == lanes
    both = jnp.concatenate(
        [
            (hit & (row < 8)).astype(jnp.bfloat16),
            (hit & (row >= 8)).astype(jnp.bfloat16),
        ],
        1,
    )
    hit9 = key9 == lanes
    contract = (((0,), (0,)), ((), ()))
    tail = incoming[:, 64:80, :].reshape(devices * 16, 128)
    for k in range(4):
        rows = incoming[:, 16 * k : 16 * (k + 1), :].reshape(devices * 16, 128)
        y = lax.dot_general(rows, both, contract, preferred_element_type=jnp.float32)
        nine = jnp.concatenate(
            [(hit9 & (row == 2 * k + q)).astype(jnp.bfloat16) for q in range(2)], 1
        )
        y += lax.dot_general(tail, nine, contract, preferred_element_type=jnp.float32)
        image[256 * k : 256 * k + 128, :] = y[:, :128]
        image[256 * k + 128 : 256 * (k + 1), :] = y[:, 128:]


def vmem(count):
    return [pl.BlockSpec(memory_space=pltpu.VMEM)] * count


def call(kernel, shapes, args, scratch=()):
    return pl.pallas_call(
        kernel,
        out_shape=shapes,
        in_specs=vmem(len(args)),
        out_specs=jax.tree.map(lambda _: pl.BlockSpec(memory_space=pltpu.VMEM), shapes),
        scratch_shapes=list(scratch),
        compiler_params=pltpu.CompilerParams(vmem_limit_bytes=56 * 1024 * 1024),
    )(*args)


def on_device(traces, taper, ray_param, reach, landing, travel_time, amplitude):
    f32, bf16 = jnp.float32, jnp.bfloat16
    freqs = traces.shape[2] // 2
    window = taper.shape[0]
    half = window // 2
    rays = ray_param.shape[0]
    rows = traces.shape[1]
    centres = rows // half
    depth = travel_time.shape[1]
    reach_count = reach.shape[2]
    line_count, size = lax.axis_size("line"), lax.axis_size("xline")
    devices = line_count * size
    coarse = freqs // FINE
    factor = 1.0 / math.sqrt(2.0 * freqs * centres * rays * reach_count / X)

    own = traces[0]
    up = [(i, i + 1) for i in range(size - 1)]
    down = [(j, i) for i, j in up]
    before = lax.ppermute(own[rows - half // 2 :], "xline", up)
    after = lax.ppermute(own[: half // 2], "xline", down)
    mine = call(
        spread_kernel,
        jax.ShapeDtypeStruct((size, 4 * depth // 128, 128), f32),
        (travel_time, amplitude),
    )
    times = lax.all_to_all(mine, "xline", split_axis=0, concat_axis=0, tiled=True)
    times = times.reshape(size // 8, 8 * mine.shape[1], 128)

    beam_count = centres * rays
    earlier = np.triu(np.ones((beam_count, beam_count), np.float32), 1)
    order = np.arange(beam_count).reshape(centres, rays // 16, 4, 2, 2)
    order = np.eye(beam_count, dtype=np.float32)[:, order.transpose(4, 1, 2, 3, 0).reshape(-1)]
    rank, keys = call(
        route_kernel,
        (
            jax.ShapeDtypeStruct((devices, beam_count), f32),
            jax.ShapeDtypeStruct((devices, 128), f32),
        ),
        (
            reach[0].T,
            landing[0].T,
            jnp.asarray(earlier, bf16),
            jnp.asarray(order, bf16),
        ),
    )

    weight = taper * (1.0 / math.sqrt(window))
    tap = jnp.stack([weight[:half][::-1], weight[half:]])[:, :, None]
    flip = jnp.asarray(np.eye(half, dtype=np.float32)[::-1], bf16)
    folded = call(
        slant_kernel,
        jax.ShapeDtypeStruct((rays, 2 * coarse * centres, FINE), f32),
        (before, own, after, tap, ray_param[:, None], flip, jnp.asarray(fold_matrix(), bf16)),
        [
            pltpu.VMEM((freqs // 128, half, 4 * centres, 128), f32),
            pltpu.VMEM((coarse * beam_count, 2 * FINE), f32),
        ],
    )
    outgoing = call(
        functools.partial(project_kernel, factor, coarse, centres),
        jax.ShapeDtypeStruct((devices, 80, 128), bf16),
        (times, folded, rank, keys),
        [
            pltpu.VMEM((depth // 128, 128, 128), f32),
            pltpu.VMEM((16, depth), f32),
            pltpu.VMEM((16 * coarse, depth), f32),
            pltpu.VMEM((beam_count // (2 * centres), 2 * centres, depth), f32),
            pltpu.VMEM((devices * 8, 128), f32),
        ],
    )
    incoming = lax.all_to_all(
        outgoing, ("line", "xline"), split_axis=0, concat_axis=0, tiled=True
    )
    image = call(place_kernel, jax.ShapeDtypeStruct((depth, X), f32), (incoming,))
    return image[None]


def solution(mesh):
    placed = (
        P("line", "xline", None),
        P(),
        P(),
        P("line", "xline", None),
        P("line", "xline", None),
        P("xline", None),
        P("xline", None),
    )
    return jax.shard_map(
        on_device, mesh=mesh, in_specs=placed, out_specs=P("line", None, "xline"), check_vma=False
    )
```

```python
import functools
import math

import jax
import jax.numpy as jnp
import numpy as np
from jax import lax
from jax.experimental import pallas as pl
from jax.experimental.pallas import tpu as pltpu
from jax.sharding import PartitionSpec as P

X = 128
FINE = 128
SLOTS = 9
BATCH = 8


def iota(shape, dim):
    return lax.broadcasted_iota(jnp.int32, shape, dim)


def fold_matrix():
    half = FINE // 2
    plus = np.zeros((FINE, half), np.float32)
    minus = np.zeros((FINE, half), np.float32)
    for m in range(half):
        plus[half + m, m] = plus[half - 1 - m, m] = 1.0
        minus[half + m, m], minus[half - 1 - m, m] = 1.0, -1.0
    zero = np.zeros_like(plus)
    real = np.concatenate([plus, zero, zero, -minus], 1)
    imag = np.concatenate([zero, minus, plus, zero], 1)
    return np.concatenate([real, imag], 0)


def pick_column(row, at):
    hit = iota((at.shape[0], row.shape[1]), 1) == at
    return jnp.sum(jnp.where(hit, row, 0.0), axis=1, keepdims=True)


def slant_kernel(before, own, after, taper, ray, fold, out, data, order, rows, beams):
    half = before.shape[0] * 2
    window = 2 * half
    rays = ray.shape[1]
    freqs = own.shape[1] // 2
    centres = own.shape[0] // half
    blocks = freqs // 128
    data[: half // 2] = before[...]
    data[half // 2 : half // 2 + own.shape[0]] = own[...]
    data[half // 2 + own.shape[0] :] = after[...]

    column = iota((1, order.shape[1]), 1)
    source = column // 16 % 8 * 128 + column // 128 * 16 + column % 16
    order[...] = (iota(order.shape, 0) == source).astype(jnp.bfloat16)

    weight = taper[...] * (1.0 / math.sqrt(window))
    place = iota((half, 1), 0)
    high_weight = pick_column(weight, half + place)
    low_weight = pick_column(weight, half - 1 - place)
    flip = (iota((half, half), 0) + iota((half, half), 1) == half - 1).astype(jnp.bfloat16)
    lane = iota((half, 128), 1)
    even = lane % 2 == 0
    for block in range(blocks):
        parts = [
            data[n * half : n * half + window, part * freqs + block * 128 :][:, :128]
            for n in range(centres)
            for part in range(2)
        ]
        moved = jnp.dot(
            jnp.concatenate(parts, 1), order[...], preferred_element_type=jnp.float32
        )
        low = jnp.dot(flip, moved[:half].astype(jnp.bfloat16), preferred_element_type=jnp.float32)
        low, high = low * low_weight, moved[half:] * high_weight
        total, diff = high + low, high - low
        for g in range(8):
            plus = total[:, 128 * g : 128 * (g + 1)]
            minus = diff[:, 128 * g : 128 * (g + 1)]
            minus = jnp.where(
                lane % 32 < 16, pltpu.roll(minus, 112, 1), -pltpu.roll(minus, 16, 1)
            )
            stack = [
                jnp.where(even, plus, 0.0),
                jnp.where(even, 0.0, plus),
                jnp.where(even, minus, 0.0),
                jnp.where(even, 0.0, minus),
            ]
            rows[block * 8 + g] = jnp.concatenate(stack, 0).astype(jnp.bfloat16)

    slow = pick_column(ray[...], iota((rays, 1), 0))
    lane = iota((rays, 128), 1)
    offset = (lane % half).astype(jnp.float32) + 0.5
    angle = slow * offset * (math.pi / freqs)
    c1, s1 = jnp.cos(angle), jnp.sin(angle)
    cs, ss = 1.0 - 2.0 * s1 * s1, 2.0 * s1 * c1
    first = lane < half
    pair = lane % 16 // 2

    def one_group(g, state):
        c, s = state
        total = jnp.zeros((rays, 128), jnp.float32)
        for start in range(0, 8, BATCH):
            steer = []
            for _ in range(BATCH):
                steer.append(jnp.concatenate([c, s], 1).astype(jnp.bfloat16))
                c, s = c * cs - s * ss, s * cs + c * ss
            y = jnp.dot(
                jnp.concatenate(steer, 0), rows[g], preferred_element_type=jnp.float32
            )
            for q in range(BATCH):
                total = jnp.where(pair == start + q, y[q * rays : (q + 1) * rays], total)
        beams[g] = total
        return c, s

    begin = (jnp.where(first, c1, cs), jnp.where(first, s1, ss))
    lax.fori_loop(0, 8 * blocks, one_group, begin, unroll=8)

    flat = out.reshape(rays * out.shape[1], 128)
    centre = lane // 32
    for block in range(blocks):
        fine, rest = [], []
        for g in range(8):
            value = beams[block * 8 + g]
            fine.append(value.astype(jnp.bfloat16).astype(jnp.float32))
            rest.append(value - fine[-1])
        stack = [
            jnp.concatenate([jnp.where(centre == n, v, 0.0) for v in piece], 1)
            for piece in (fine, rest)
            for n in range(centres)
        ]
        folded = jnp.dot(
            jnp.concatenate(stack, 0).astype(jnp.bfloat16),
            fold[...],
            preferred_element_type=jnp.float32,
        )
        folded = folded[: centres * rays] + folded[centres * rays :]
        for n in range(centres):
            for v in range(2):
                row = (2 * block + v) * centres + n
                value = folded[n * rays : (n + 1) * rays, 128 * v : 128 * (v + 1)]
                flat[pl.ds(row, rays, stride=out.shape[1]), :] = value


def project_kernel(factor, coarse, centres, times, folded, rank, keys, out, seed, step, outer, proj, ninth):
    half = FINE // 2
    blocks = seed.shape[0]
    bases = times.shape[0]
    upper = iota((2 * centres, 128 * blocks), 0) < centres

    def one_group(base, r):
        for zb in range(blocks):
            cols = slice(zb * 128, zb * 128 + 128)
            t = times[base, pl.ds(8 * r + zb, 8, stride=32), :]
            amp = times[base, pl.ds(16 + 8 * r + zb, 8, stride=32), :] * factor
            angle = t * (math.pi / (2 * coarse * FINE))
            c0, s0 = jnp.cos(angle), jnp.sin(angle)
            c1, s1 = 1.0 - 2.0 * s0 * s0, 2.0 * s0 * c0
            c, s = c0, s0
            for m in range(8):
                seed[zb, m * 8 : m * 8 + 8, :] = c
                seed[zb, 64 + m * 8 : 72 + m * 8, :] = s
                if m < 7:
                    c, s = c * c1 - s * s1, s * c1 + c * s1
            c, s = c1, s1
            for power in range(6):
                c, s = 1.0 - 2.0 * s * s, 2.0 * s * c
                if power == 2:
                    step[0:8, cols] = c
                    step[8:16, cols] = s
            ca, sa = (c * c0 - s * s0) * amp, (s * c0 + c * s0) * amp
            cb, sb = 1.0 - 2.0 * s * s, 2.0 * s * c
            for a in range(coarse):
                outer[16 * a : 16 * a + 8, cols] = ca
                outer[16 * a + 8 : 16 * a + 16, cols] = sa
                ca, sa = ca * cb - sa * sb, sa * cb + ca * sb
        for i in range(8):
            p = base * 16 + 2 * i + r
            rows = folded[p].astype(jnp.bfloat16)
            weights = []
            for zb in range(blocks):
                cols = slice(zb * 128, zb * 128 + 128)
                c = seed[zb, pl.ds(i, 8, stride=8), :]
                s = seed[zb, pl.ds(64 + i, 8, stride=8), :]
                cs = jnp.broadcast_to(step[i : i + 1, cols], (8, 128))
                ss = jnp.broadcast_to(step[8 + i : 9 + i, cols], (8, 128))
                real, imag = [c], [s]
                for _ in range(half // 8 - 1):
                    c, s = c * cs - s * ss, s * cs + c * ss
                    real.append(c)
                    imag.append(s)
                weights.append(jnp.concatenate(real + imag, 0).astype(jnp.bfloat16))
            parts = jnp.dot(
                rows, jnp.concatenate(weights, 1), preferred_element_type=jnp.float32
            )
            total = jnp.zeros(upper.shape, jnp.float32)
            for a in range(coarse):
                turn = jnp.where(
                    upper,
                    jnp.broadcast_to(outer[16 * a + i : 16 * a + i + 1, :], upper.shape),
                    jnp.broadcast_to(outer[16 * a + 8 + i : 16 * a + 9 + i, :], upper.shape),
                )
                total = total + parts[2 * centres * a : 2 * centres * (a + 1)] * turn
            total = total + pltpu.roll(total, centres, 0)
            if i % 2 == 0:
                held = total
            else:
                proj[(r * bases + base) * 4 + i // 2] = jnp.where(upper, held, total)

    def one_base(base, carry):
        one_group(base, 0)
        one_group(base, 1)
        return carry

    lax.fori_loop(0, bases, one_base, 0)

    sends = proj[...].reshape(-1, 128 * blocks).astype(jnp.bfloat16)
    devices, rows = rank.shape
    ranks = jnp.broadcast_to(rank[...][:, None, :], (devices, 8, rows)).reshape(devices * 8, rows)
    lane8 = iota((devices * 8, rows), 0) % 8
    pick = (ranks == lane8.astype(jnp.float32)).astype(jnp.bfloat16)
    for k in range(4):
        y = jnp.dot(pick, sends[:, 256 * k : 256 * (k + 1)], preferred_element_type=jnp.float32)
        pair = [y[:, :128].reshape(devices, 8, 128), y[:, 128:].reshape(devices, 8, 128)]
        out[:, 16 * k : 16 * (k + 1), :] = jnp.concatenate(pair, 1).astype(jnp.bfloat16)
    last = jnp.dot(
        (rank[...] == 8.0).astype(jnp.bfloat16), sends, preferred_element_type=jnp.float32
    )
    for k in range(8):
        ninth[pl.ds(k, devices, stride=8), :] = last[:, 128 * k : 128 * (k + 1)]
    tags = jnp.broadcast_to(keys[...][:, None, :], (devices, 8, 128))
    pair = [ninth[...].reshape(devices, 8, 128), tags]
    out[:, 64:80, :] = jnp.concatenate(pair, 1).astype(jnp.bfloat16)


def route_kernel(reach, landing, earlier, order, rank, keys):
    devices, rows = rank.shape
    tile = iota((devices, rows), 0)
    named = jnp.zeros((devices, rows), jnp.float32)
    column = jnp.zeros((devices, rows), jnp.float32)
    for t in range(reach.shape[0]):
        hit = jnp.broadcast_to(reach[t : t + 1, :], (devices, rows)) == tile
        land = jnp.broadcast_to(landing[t : t + 1, :], (devices, rows)).astype(jnp.float32)
        named = named + jnp.where(hit, 1.0, 0.0)
        column = column + jnp.where(hit, land + 1.0, 0.0)
    count = jnp.dot(named.astype(jnp.bfloat16), earlier[...], preferred_element_type=jnp.float32)
    slot = jnp.where(named > 0.0, count, -1.0)
    rank[...] = jnp.dot(
        slot.astype(jnp.bfloat16), order[...], preferred_element_type=jnp.float32
    )
    lane = iota((devices, 128), 1)
    table = jnp.zeros((devices, 128), jnp.float32)
    for k in range(SLOTS):
        value = jnp.sum(jnp.where(slot == k, column, 0.0), axis=1, keepdims=True)
        table = jnp.where(lane == k, value, table)
    keys[...] = table - 1.0


def spread_kernel(times, amps, out):
    rows = [table[r : r + 1, :] for table in (times, amps) for r in range(table.shape[0])]
    lanes = range(0, times.shape[1], 128)
    tile = jnp.concatenate([row[:, at : at + 128] for row in rows for at in lanes], 0)
    out[...] = jnp.broadcast_to(tile[None], out.shape)


def place_kernel(incoming, image):
    devices = incoming.shape[0]
    tags = incoming[:, 64:80, :].astype(jnp.float32)[:, 8:16, :]
    tags = jnp.concatenate([tags, tags], 1).reshape(devices * 16, 128)
    lane = iota((devices * 16, 128), 1)
    row = iota((devices * 16, 128), 0) % 16
    key = jnp.sum(jnp.where(lane == row % 8, tags, 0.0), axis=1, keepdims=True)
    key9 = jnp.sum(jnp.where(lane == 8, tags, 0.0), axis=1, keepdims=True)
    lanes = lane.astype(jnp.float32)
    hit = key == lanes
    both = jnp.concatenate(
        [
            (hit & (row < 8)).astype(jnp.bfloat16),
            (hit & (row >= 8)).astype(jnp.bfloat16),
        ],
        1,
    )
    hit9 = key9 == lanes
    contract = (((0,), (0,)), ((), ()))
    tail = incoming[:, 64:80, :].reshape(devices * 16, 128)
    for k in range(4):
        rows = incoming[:, 16 * k : 16 * (k + 1), :].reshape(devices * 16, 128)
        y = lax.dot_general(rows, both, contract, preferred_element_type=jnp.float32)
        nine = jnp.concatenate(
            [(hit9 & (row == 2 * k + q)).astype(jnp.bfloat16) for q in range(2)], 1
        )
        y += lax.dot_general(tail, nine, contract, preferred_element_type=jnp.float32)
        image[256 * k : 256 * k + 128, :] = y[:, :128]
        image[256 * k + 128 : 256 * (k + 1), :] = y[:, 128:]


def vmem(count):
    return [pl.BlockSpec(memory_space=pltpu.VMEM)] * count


def call(kernel, shapes, args, scratch=()):
    return pl.pallas_call(
        kernel,
        out_shape=shapes,
        in_specs=vmem(len(args)),
        out_specs=jax.tree.map(lambda _: pl.BlockSpec(memory_space=pltpu.VMEM), shapes),
        scratch_shapes=list(scratch),
        compiler_params=pltpu.CompilerParams(vmem_limit_bytes=56 * 1024 * 1024),
    )(*args)


def on_device(traces, taper, ray_param, reach, landing, travel_time, amplitude):
    f32, bf16 = jnp.float32, jnp.bfloat16
    freqs = traces.shape[2] // 2
    window = taper.shape[0]
    half = window // 2
    rays = ray_param.shape[0]
    rows = traces.shape[1]
    centres = rows // half
    depth = travel_time.shape[1]
    reach_count = reach.shape[2]
    line_count, size = lax.axis_size("line"), lax.axis_size("xline")
    devices = line_count * size
    coarse = freqs // FINE
    factor = 1.0 / math.sqrt(2.0 * freqs * centres * rays * reach_count / X)

    own = traces[0]
    up = [(i, i + 1) for i in range(size - 1)]
    down = [(j, i) for i, j in up]
    before = lax.ppermute(own[rows - half // 2 :], "xline", up)
    after = lax.ppermute(own[: half // 2], "xline", down)
    mine = call(
        spread_kernel,
        jax.ShapeDtypeStruct((size, 4 * depth // 128, 128), f32),
        (travel_time, amplitude),
    )
    times = lax.all_to_all(mine, "xline", split_axis=0, concat_axis=0, tiled=True)
    times = times.reshape(size // 8, 8 * mine.shape[1], 128)

    beam_count = centres * rays
    earlier = np.triu(np.ones((beam_count, beam_count), np.float32), 1)
    order = np.arange(beam_count).reshape(centres, rays // 16, 4, 2, 2)
    order = np.eye(beam_count, dtype=np.float32)[:, order.transpose(4, 1, 2, 3, 0).reshape(-1)]
    rank, keys = call(
        route_kernel,
        (
            jax.ShapeDtypeStruct((devices, beam_count), f32),
            jax.ShapeDtypeStruct((devices, 128), f32),
        ),
        (
            reach[0].T,
            landing[0].T,
            jnp.asarray(earlier, bf16),
            jnp.asarray(order, bf16),
        ),
    )

    at = np.arange(8 * 128)
    fold = fold_matrix()[at // 16 % 2 * 128 + at // 128 * 16 + at % 16]
    folded = call(
        slant_kernel,
        jax.ShapeDtypeStruct((rays, 2 * coarse * centres, FINE), f32),
        (before, own, after, taper[None], ray_param[None], jnp.asarray(fold, bf16)),
        [
            pltpu.VMEM((rows + half, 2 * freqs), bf16),
            pltpu.VMEM((256 * centres, 256 * centres), bf16),
            pltpu.VMEM((freqs // 16, 4 * half, 128), bf16),
            pltpu.VMEM((freqs // 16, rays, 128), f32),
        ],
    )
    outgoing = call(
        functools.partial(project_kernel, factor, coarse, centres),
        jax.ShapeDtypeStruct((devices, 80, 128), bf16),
        (times, folded, rank, keys),
        [
            pltpu.VMEM((depth // 128, 128, 128), f32),
            pltpu.VMEM((16, depth), f32),
            pltpu.VMEM((16 * coarse, depth), f32),
            pltpu.VMEM((beam_count // (2 * centres), 2 * centres, depth), f32),
            pltpu.VMEM((devices * 8, 128), f32),
        ],
    )
    incoming = lax.all_to_all(
        outgoing, ("line", "xline"), split_axis=0, concat_axis=0, tiled=True
    )
    image = call(place_kernel, jax.ShapeDtypeStruct((depth, X), f32), (incoming,))
    return image[None]


def solution(mesh):
    placed = (
        P("line", "xline", None),
        P(),
        P(),
        P("line", "xline", None),
        P("line", "xline", None),
        P("xline", None),
        P("xline", None),
    )
    return jax.shard_map(
        on_device, mesh=mesh, in_specs=placed, out_specs=P("line", None, "xline"), check_vma=False
    )
```

```python
import functools
import math

import jax
import jax.numpy as jnp
import numpy as np
from jax import lax
from jax.experimental import pallas as pl
from jax.experimental.pallas import tpu as pltpu
from jax.sharding import PartitionSpec as P

X = 128
FINE = 128
SLOTS = 9
BATCH = 8


def iota(shape, dim):
    return lax.broadcasted_iota(jnp.int32, shape, dim)


def fold_matrix():
    half = FINE // 2
    plus = np.zeros((FINE, half), np.float32)
    minus = np.zeros((FINE, half), np.float32)
    for m in range(half):
        plus[half + m, m] = plus[half - 1 - m, m] = 1.0
        minus[half + m, m], minus[half - 1 - m, m] = 1.0, -1.0
    zero = np.zeros_like(plus)
    real = np.concatenate([plus, zero, zero, -minus], 1)
    imag = np.concatenate([zero, minus, plus, zero], 1)
    return np.concatenate([real, imag], 0)


def pick_column(row, at):
    hit = iota((at.shape[0], row.shape[1]), 1) == at
    return jnp.sum(jnp.where(hit, row, 0.0), axis=1, keepdims=True)


def slant_kernel(before, own, after, taper, ray, fold, out, data, order, rows, beams):
    half = before.shape[0] * 2
    window = 2 * half
    rays = ray.shape[1]
    freqs = own.shape[1] // 2
    centres = own.shape[0] // half
    blocks = freqs // 128
    data[: half // 2] = before[...]
    data[half // 2 : half // 2 + own.shape[0]] = own[...]
    data[half // 2 + own.shape[0] :] = after[...]

    column = iota((1, order.shape[1]), 1)
    source = column // 16 % 8 * 128 + column // 128 * 16 + column % 16
    order[...] = (iota(order.shape, 0) == source).astype(jnp.bfloat16)

    weight = taper[...] * (1.0 / math.sqrt(window))
    place = iota((half, 1), 0)
    high_weight = pick_column(weight, half + place)
    low_weight = pick_column(weight, half - 1 - place)
    flip = (iota((half, half), 0) + iota((half, half), 1) == half - 1).astype(jnp.bfloat16)
    lane = iota((half, 128), 1)
    even = lane % 2 == 0
    for block in range(blocks):
        parts = [
            data[n * half : n * half + window, part * freqs + block * 128 :][:, :128]
            for n in range(centres)
            for part in range(2)
        ]
        moved = jnp.dot(
            jnp.concatenate(parts, 1), order[...], preferred_element_type=jnp.float32
        )
        low = jnp.dot(flip, moved[:half].astype(jnp.bfloat16), preferred_element_type=jnp.float32)
        low, high = low * low_weight, moved[half:] * high_weight
        total, diff = high + low, high - low
        for g in range(8):
            plus = total[:, 128 * g : 128 * (g + 1)]
            minus = diff[:, 128 * g : 128 * (g + 1)]
            minus = jnp.where(
                lane % 32 < 16, pltpu.roll(minus, 112, 1), -pltpu.roll(minus, 16, 1)
            )
            stack = [
                jnp.where(even, plus, 0.0),
                jnp.where(even, 0.0, plus),
                jnp.where(even, minus, 0.0),
                jnp.where(even, 0.0, minus),
            ]
            rows[block * 8 + g] = jnp.concatenate(stack, 0).astype(jnp.bfloat16)

    slow = pick_column(ray[...], iota((rays, 1), 0))
    lane = iota((rays, 128), 1)
    offset = (lane % half).astype(jnp.float32) + 0.5
    angle = slow * offset * (math.pi / freqs)
    c1, s1 = jnp.cos(angle), jnp.sin(angle)
    cs, ss = 1.0 - 2.0 * s1 * s1, 2.0 * s1 * c1
    first = lane < half
    pair = lane % 16 // 2

    def one_group(g, state):
        c, s = state
        total = jnp.zeros((rays, 128), jnp.float32)
        for start in range(0, 8, BATCH):
            steer = []
            for _ in range(BATCH):
                steer.append(jnp.concatenate([c, s], 1).astype(jnp.bfloat16))
                c, s = c * cs - s * ss, s * cs + c * ss
            y = jnp.dot(
                jnp.concatenate(steer, 0), rows[g], preferred_element_type=jnp.float32
            )
            for q in range(BATCH):
                total = jnp.where(pair == start + q, y[q * rays : (q + 1) * rays], total)
        beams[g] = total
        return c, s

    begin = (jnp.where(first, c1, cs), jnp.where(first, s1, ss))
    lax.fori_loop(0, 8 * blocks, one_group, begin, unroll=8)

    flat = out.reshape(rays * out.shape[1], 128)
    centre = lane // 32
    for block in range(blocks):
        fine, rest = [], []
        for g in range(8):
            value = beams[block * 8 + g]
            fine.append(value.astype(jnp.bfloat16).astype(jnp.float32))
            rest.append(value - fine[-1])
        stack = [
            jnp.concatenate([jnp.where(centre == n, v, 0.0) for v in piece], 1)
            for piece in (fine, rest)
            for n in range(centres)
        ]
        folded = jnp.dot(
            jnp.concatenate(stack, 0).astype(jnp.bfloat16),
            fold[...],
            preferred_element_type=jnp.float32,
        )
        folded = folded[: centres * rays] + folded[centres * rays :]
        for n in range(centres):
            for v in range(2):
                row = (2 * block + v) * centres + n
                value = folded[n * rays : (n + 1) * rays, 128 * v : 128 * (v + 1)]
                flat[pl.ds(row, rays, stride=out.shape[1]), :] = value


def project_kernel(factor, coarse, centres, times, folded, rank, keys, out, seed, step, outer, proj, ninth):
    half = FINE // 2
    blocks = seed.shape[0]
    bases = times.shape[0]
    upper = iota((2 * centres, 128), 0) < centres

    def one_group(base, r):
        for zb in range(blocks):
            cols = slice(zb * 128, zb * 128 + 128)
            t = times[base, pl.ds(8 * r + zb, 8, stride=32), :]
            amp = times[base, pl.ds(16 + 8 * r + zb, 8, stride=32), :] * factor
            angle = t * (math.pi / (2 * coarse * FINE))
            c0, s0 = jnp.cos(angle), jnp.sin(angle)
            c1, s1 = 1.0 - 2.0 * s0 * s0, 2.0 * s0 * c0
            c, s = c0, s0
            for m in range(8):
                seed[zb, m * 8 : m * 8 + 8, :] = c
                seed[zb, 64 + m * 8 : 72 + m * 8, :] = s
                if m < 7:
                    c, s = c * c1 - s * s1, s * c1 + c * s1
            c, s = c1, s1
            for power in range(6):
                c, s = 1.0 - 2.0 * s * s, 2.0 * s * c
                if power == 2:
                    step[0:8, cols] = c
                    step[8:16, cols] = s
            ca, sa = (c * c0 - s * s0) * amp, (s * c0 + c * s0) * amp
            cb, sb = 1.0 - 2.0 * s * s, 2.0 * s * c
            for a in range(coarse):
                outer[16 * a : 16 * a + 8, cols] = ca
                outer[16 * a + 8 : 16 * a + 16, cols] = sa
                ca, sa = ca * cb - sa * sb, sa * cb + ca * sb
        held = [None] * blocks
        for i in range(8):
            p = base * 16 + 2 * i + r
            rows = folded[p].astype(jnp.bfloat16)
            for zb in range(blocks):
                cols = slice(zb * 128, zb * 128 + 128)
                c = seed[zb, pl.ds(i, 8, stride=8), :]
                s = seed[zb, pl.ds(64 + i, 8, stride=8), :]
                cs = jnp.broadcast_to(step[i : i + 1, cols], (8, 128))
                ss = jnp.broadcast_to(step[8 + i : 9 + i, cols], (8, 128))
                real, imag = [c], [s]
                for _ in range(half // 8 - 1):
                    c, s = c * cs - s * ss, s * cs + c * ss
                    real.append(c)
                    imag.append(s)
                weights = jnp.concatenate(real + imag, 0).astype(jnp.bfloat16)
                parts = jnp.dot(rows, weights, preferred_element_type=jnp.float32)
                total = jnp.zeros(upper.shape, jnp.float32)
                for a in range(coarse):
                    turn = jnp.where(
                        upper,
                        jnp.broadcast_to(outer[16 * a + i : 16 * a + i + 1, cols], upper.shape),
                        jnp.broadcast_to(outer[16 * a + 8 + i : 16 * a + 9 + i, cols], upper.shape),
                    )
                    total = total + parts[2 * centres * a : 2 * centres * (a + 1)] * turn
                total = total + pltpu.roll(total, centres, 0)
                if i % 2 == 0:
                    held[zb] = total
                else:
                    tile = (r * bases + base) * 4 + i // 2
                    proj[tile, :, cols] = jnp.where(upper, held[zb], total)

    def one_base(base, carry):
        one_group(base, 0)
        one_group(base, 1)
        return carry

    lax.fori_loop(0, bases, one_base, 0)

    sends = proj[...].reshape(-1, 128 * blocks).astype(jnp.bfloat16)
    devices, rows = rank.shape
    ranks = jnp.broadcast_to(rank[...][:, None, :], (devices, 8, rows)).reshape(devices * 8, rows)
    lane8 = iota((devices * 8, rows), 0) % 8
    pick = (ranks == lane8.astype(jnp.float32)).astype(jnp.bfloat16)
    for k in range(4):
        y = jnp.dot(pick, sends[:, 256 * k : 256 * (k + 1)], preferred_element_type=jnp.float32)
        pair = [y[:, :128].reshape(devices, 8, 128), y[:, 128:].reshape(devices, 8, 128)]
        out[:, 16 * k : 16 * (k + 1), :] = jnp.concatenate(pair, 1).astype(jnp.bfloat16)
    last = jnp.dot(
        (rank[...] == 8.0).astype(jnp.bfloat16), sends, preferred_element_type=jnp.float32
    )
    for k in range(8):
        ninth[pl.ds(k, devices, stride=8), :] = last[:, 128 * k : 128 * (k + 1)]
    tags = jnp.broadcast_to(keys[...][:, None, :], (devices, 8, 128))
    pair = [ninth[...].reshape(devices, 8, 128), tags]
    out[:, 64:80, :] = jnp.concatenate(pair, 1).astype(jnp.bfloat16)


def open_kernel(own, times, amps, reach, landing, earlier, order, up, down, mine, rank, keys, sems):
    edge = up.shape[0]
    copies = [
        pltpu.make_async_copy(own.at[own.shape[0] - edge :], up, sems.at[0]),
        pltpu.make_async_copy(own.at[:edge], down, sems.at[1]),
    ]
    for copy in copies:
        copy.start()
    rows = [table[r : r + 1, :] for table in (times, amps) for r in range(table.shape[0])]
    lanes = range(0, times.shape[1], 128)
    tile = jnp.concatenate([row[:, at : at + 128] for row in rows for at in lanes], 0)
    mine[...] = jnp.broadcast_to(tile[None], mine.shape)

    devices, rows = rank.shape
    tile = iota((devices, rows), 0)
    named = jnp.zeros((devices, rows), jnp.float32)
    column = jnp.zeros((devices, rows), jnp.float32)
    for t in range(reach.shape[0]):
        hit = jnp.broadcast_to(reach[t : t + 1, :], (devices, rows)) == tile
        land = jnp.broadcast_to(landing[t : t + 1, :], (devices, rows)).astype(jnp.float32)
        named = named + jnp.where(hit, 1.0, 0.0)
        column = column + jnp.where(hit, land + 1.0, 0.0)
    count = jnp.dot(named.astype(jnp.bfloat16), earlier[...], preferred_element_type=jnp.float32)
    slot = jnp.where(named > 0.0, count, -1.0)
    rank[...] = jnp.dot(
        slot.astype(jnp.bfloat16), order[...], preferred_element_type=jnp.float32
    )
    lane = iota((devices, 128), 1)
    table = jnp.zeros((devices, 128), jnp.float32)
    for k in range(SLOTS):
        value = jnp.sum(jnp.where(slot == k, column, 0.0), axis=1, keepdims=True)
        table = jnp.where(lane == k, value, table)
    keys[...] = table - 1.0
    for copy in copies:
        copy.wait()


def place_kernel(incoming, image, ninth):
    devices = incoming.shape[0]
    tail = incoming[:, 64:80, :].astype(jnp.float32)
    tags = tail[:, 8:16, :]
    ninth[...] = tail[:, 0:8, :].reshape(devices * 8, 128)
    lane = iota((devices, 128), 1)
    hit9 = (tags[:, 0, :][:, 8:9] == lane.astype(jnp.float32)).astype(jnp.bfloat16)
    tags = jnp.concatenate([tags, tags], 1).reshape(devices * 16, 128)
    lane = iota((devices * 16, 128), 1)
    row = iota((devices * 16, 128), 0) % 16
    key = jnp.sum(jnp.where(lane == row % 8, tags, 0.0), axis=1, keepdims=True)
    hit = key == lane.astype(jnp.float32)
    both = jnp.concatenate(
        [
            (hit & (row < 8)).astype(jnp.bfloat16),
            (hit & (row >= 8)).astype(jnp.bfloat16),
        ],
        1,
    )
    contract = (((0,), (0,)), ((), ()))
    for k in range(4):
        rows = incoming[:, 16 * k : 16 * (k + 1), :].reshape(devices * 16, 128)
        y = lax.dot_general(rows, both, contract, preferred_element_type=jnp.float32)
        for q in range(2):
            last = ninth[pl.ds(2 * k + q, devices, stride=8), :].astype(jnp.bfloat16)
            last = lax.dot_general(last, hit9, contract, preferred_element_type=jnp.float32)
            cut = 256 * k + 128 * q
            image[cut : cut + 128, :] = y[:, 128 * q : 128 * (q + 1)] + last


def vmem(count):
    return [pl.BlockSpec(memory_space=pltpu.VMEM)] * count


def call(kernel, shapes, args, scratch=(), specs=()):
    return pl.pallas_call(
        kernel,
        out_shape=shapes,
        in_specs=list(specs) + vmem(len(args) - len(specs)),
        out_specs=jax.tree.map(lambda _: pl.BlockSpec(memory_space=pltpu.VMEM), shapes),
        scratch_shapes=list(scratch),
        compiler_params=pltpu.CompilerParams(vmem_limit_bytes=56 * 1024 * 1024),
    )(*args)


def on_device(traces, taper, ray_param, reach, landing, travel_time, amplitude):
    f32, bf16 = jnp.float32, jnp.bfloat16
    freqs = traces.shape[2] // 2
    window = taper.shape[0]
    half = window // 2
    rays = ray_param.shape[0]
    rows = traces.shape[1]
    centres = rows // half
    depth = travel_time.shape[1]
    reach_count = reach.shape[2]
    line_count, size = lax.axis_size("line"), lax.axis_size("xline")
    devices = line_count * size
    coarse = freqs // FINE
    factor = 1.0 / math.sqrt(2.0 * freqs * centres * rays * reach_count / X)

    own = traces[0]
    beam_count = centres * rays
    earlier = np.triu(np.ones((beam_count, beam_count), np.float32), 1)
    order = np.arange(beam_count).reshape(centres, rays // 16, 4, 2, 2)
    order = np.eye(beam_count, dtype=np.float32)[:, order.transpose(4, 1, 2, 3, 0).reshape(-1)]
    edge = (half // 2, 2 * freqs)
    last, first, mine, rank, keys = call(
        open_kernel,
        (
            jax.ShapeDtypeStruct(edge, bf16),
            jax.ShapeDtypeStruct(edge, bf16),
            jax.ShapeDtypeStruct((size, 4 * depth // 128, 128), f32),
            jax.ShapeDtypeStruct((devices, beam_count), f32),
            jax.ShapeDtypeStruct((devices, 128), f32),
        ),
        (
            own,
            travel_time,
            amplitude,
            reach[0].T,
            landing[0].T,
            jnp.asarray(earlier, bf16),
            jnp.asarray(order, bf16),
        ),
        [pltpu.SemaphoreType.DMA((2,))],
        [pl.BlockSpec(memory_space=pl.ANY)],
    )
    up = [(i, i + 1) for i in range(size - 1)]
    down = [(j, i) for i, j in up]
    before = lax.ppermute(last, "xline", up)
    after = lax.ppermute(first, "xline", down)
    times = lax.all_to_all(mine, "xline", split_axis=0, concat_axis=0, tiled=True)
    times = times.reshape(size // 8, 8 * mine.shape[1], 128)

    at = np.arange(8 * 128)
    fold = fold_matrix()[at // 16 % 2 * 128 + at // 128 * 16 + at % 16]
    folded = call(
        slant_kernel,
        jax.ShapeDtypeStruct((rays, 2 * coarse * centres, FINE), f32),
        (before, own, after, taper[None], ray_param[None], jnp.asarray(fold, bf16)),
        [
            pltpu.VMEM((rows + half, 2 * freqs), bf16),
            pltpu.VMEM((256 * centres, 256 * centres), bf16),
            pltpu.VMEM((freqs // 16, 4 * half, 128), bf16),
            pltpu.VMEM((freqs // 16, rays, 128), f32),
        ],
    )
    outgoing = call(
        functools.partial(project_kernel, factor, coarse, centres),
        jax.ShapeDtypeStruct((devices, 80, 128), bf16),
        (times, folded, rank, keys),
        [
            pltpu.VMEM((depth // 128, 128, 128), f32),
            pltpu.VMEM((16, depth), f32),
            pltpu.VMEM((16 * coarse, depth), f32),
            pltpu.VMEM((beam_count // (2 * centres), 2 * centres, depth), f32),
            pltpu.VMEM((devices * 8, 128), f32),
        ],
    )
    incoming = lax.all_to_all(
        outgoing, ("line", "xline"), split_axis=0, concat_axis=0, tiled=True
    )
    image = call(
        place_kernel,
        jax.ShapeDtypeStruct((depth, X), f32),
        (incoming,),
        [pltpu.VMEM((8 * devices, 128), f32)],
    )
    return image[None]


def solution(mesh):
    placed = (
        P("line", "xline", None),
        P(),
        P(),
        P("line", "xline", None),
        P("line", "xline", None),
        P("xline", None),
        P("xline", None),
    )
    return jax.shard_map(
        on_device, mesh=mesh, in_specs=placed, out_specs=P("line", None, "xline"), check_vma=False
    )
```

```python
import functools
import math

import jax
import jax.numpy as jnp
import numpy as np
from jax import lax
from jax.experimental import pallas as pl
from jax.experimental.pallas import tpu as pltpu
from jax.sharding import PartitionSpec as P

X = 128
FINE = 128
SLOTS = 9
BATCH = 8


def iota(shape, dim):
    return lax.broadcasted_iota(jnp.int32, shape, dim)


def fold_matrix():
    half = FINE // 2
    plus = np.zeros((FINE, half), np.float32)
    minus = np.zeros((FINE, half), np.float32)
    for m in range(half):
        plus[half + m, m] = plus[half - 1 - m, m] = 1.0
        minus[half + m, m], minus[half - 1 - m, m] = 1.0, -1.0
    zero = np.zeros_like(plus)
    real = np.concatenate([plus, zero, zero, -minus], 1)
    imag = np.concatenate([zero, minus, plus, zero], 1)
    return np.concatenate([real, imag], 0)


def pick_column(row, at):
    hit = iota((at.shape[0], row.shape[1]), 1) == at
    return jnp.sum(jnp.where(hit, row, 0.0), axis=1, keepdims=True)


def slant_kernel(before, own, after, taper, ray, fold, out, data, order, rows, beams):
    half = before.shape[0] * 2
    window = 2 * half
    rays = ray.shape[1]
    freqs = own.shape[1] // 2
    centres = own.shape[0] // half
    blocks = freqs // 128
    data[: half // 2] = before[...]
    data[half // 2 : half // 2 + own.shape[0]] = own[...]
    data[half // 2 + own.shape[0] :] = after[...]

    column = iota((1, order.shape[1]), 1)
    source = column // 16 % 8 * 128 + column // 128 * 16 + column % 16
    order[...] = (iota(order.shape, 0) == source).astype(jnp.bfloat16)

    weight = taper[...] * (1.0 / math.sqrt(window))
    place = iota((half, 1), 0)
    high_weight = pick_column(weight, half + place)
    low_weight = pick_column(weight, half - 1 - place)
    flip = (iota((half, half), 0) + iota((half, half), 1) == half - 1).astype(jnp.bfloat16)
    lane = iota((half, 128), 1)
    even = lane % 2 == 0
    for block in range(blocks):
        parts = [
            data[n * half : n * half + window, part * freqs + block * 128 :][:, :128]
            for n in range(centres)
            for part in range(2)
        ]
        moved = jnp.dot(
            jnp.concatenate(parts, 1), order[...], preferred_element_type=jnp.float32
        )
        low = jnp.dot(flip, moved[:half].astype(jnp.bfloat16), preferred_element_type=jnp.float32)
        low, high = low * low_weight, moved[half:] * high_weight
        total, diff = high + low, high - low
        for g in range(8):
            plus = total[:, 128 * g : 128 * (g + 1)]
            minus = diff[:, 128 * g : 128 * (g + 1)]
            minus = jnp.where(
                lane % 32 < 16, pltpu.roll(minus, 112, 1), -pltpu.roll(minus, 16, 1)
            )
            stack = [
                jnp.where(even, plus, 0.0),
                jnp.where(even, 0.0, plus),
                jnp.where(even, minus, 0.0),
                jnp.where(even, 0.0, minus),
            ]
            rows[block * 8 + g] = jnp.concatenate(stack, 0).astype(jnp.bfloat16)

    slow = pick_column(ray[...], iota((rays, 1), 0))
    lane = iota((rays, 128), 1)
    offset = (lane % half).astype(jnp.float32) + 0.5
    angle = slow * offset * (math.pi / freqs)
    c1, s1 = jnp.cos(angle), jnp.sin(angle)
    cs, ss = 1.0 - 2.0 * s1 * s1, 2.0 * s1 * c1
    first = lane < half
    pair = lane % 16 // 2

    def one_group(g, state):
        c, s = state
        total = jnp.zeros((rays, 128), jnp.float32)
        for start in range(0, 8, BATCH):
            steer = []
            for _ in range(BATCH):
                steer.append(jnp.concatenate([c, s], 1).astype(jnp.bfloat16))
                c, s = c * cs - s * ss, s * cs + c * ss
            y = jnp.dot(
                jnp.concatenate(steer, 0), rows[g], preferred_element_type=jnp.float32
            )
            for q in range(BATCH):
                total = jnp.where(pair == start + q, y[q * rays : (q + 1) * rays], total)
        beams[g] = total
        return c, s

    begin = (jnp.where(first, c1, cs), jnp.where(first, s1, ss))
    lax.fori_loop(0, 8 * blocks, one_group, begin, unroll=8)

    flat = out.reshape(rays * out.shape[1], 128)
    centre = lane // 32
    for block in range(blocks):
        fine, rest = [], []
        for g in range(8):
            value = beams[block * 8 + g]
            fine.append(value.astype(jnp.bfloat16).astype(jnp.float32))
            rest.append(value - fine[-1])
        stack = [
            jnp.concatenate([jnp.where(centre == n, v, 0.0) for v in piece], 1)
            for piece in (fine, rest)
            for n in range(centres)
        ]
        folded = jnp.dot(
            jnp.concatenate(stack, 0).astype(jnp.bfloat16),
            fold[...],
            preferred_element_type=jnp.float32,
        )
        folded = folded[: centres * rays] + folded[centres * rays :]
        for n in range(centres):
            for v in range(2):
                row = (2 * block + v) * centres + n
                value = folded[n * rays : (n + 1) * rays, 128 * v : 128 * (v + 1)]
                flat[pl.ds(row, rays, stride=out.shape[1]), :] = value


def project_kernel(factor, coarse, centres, times, folded, rank, keys, out, seed, step, outer, proj, ninth):
    half = FINE // 2
    blocks = seed.shape[0]
    bases = times.shape[0]
    upper = iota((2 * centres, 128), 0) < centres

    def one_group(base, r):
        for zb in range(blocks):
            cols = slice(zb * 128, zb * 128 + 128)
            t = times[base, pl.ds(8 * r + zb, 8, stride=32), :]
            amp = times[base, pl.ds(16 + 8 * r + zb, 8, stride=32), :] * factor
            angle = t * (math.pi / (2 * coarse * FINE))
            c0, s0 = jnp.cos(angle), jnp.sin(angle)
            c1, s1 = 1.0 - 2.0 * s0 * s0, 2.0 * s0 * c0
            c, s = c0, s0
            for m in range(8):
                seed[zb, m * 8 : m * 8 + 8, :] = c
                seed[zb, 64 + m * 8 : 72 + m * 8, :] = s
                if m < 7:
                    c, s = c * c1 - s * s1, s * c1 + c * s1
            c, s = c1, s1
            for power in range(6):
                c, s = 1.0 - 2.0 * s * s, 2.0 * s * c
                if power == 2:
                    step[0:8, cols] = c
                    step[8:16, cols] = s
            ca, sa = (c * c0 - s * s0) * amp, (s * c0 + c * s0) * amp
            cb, sb = 1.0 - 2.0 * s * s, 2.0 * s * c
            for a in range(coarse):
                outer[16 * a : 16 * a + 8, cols] = ca
                outer[16 * a + 8 : 16 * a + 16, cols] = sa
                ca, sa = ca * cb - sa * sb, sa * cb + ca * sb
        held = [None] * blocks
        for i in range(8):
            p = base * 16 + 2 * i + r
            rows = folded[p].astype(jnp.bfloat16)
            for zb in range(blocks):
                cols = slice(zb * 128, zb * 128 + 128)
                c = seed[zb, pl.ds(i, 8, stride=8), :]
                s = seed[zb, pl.ds(64 + i, 8, stride=8), :]
                cs = jnp.broadcast_to(step[i : i + 1, cols], (8, 128))
                ss = jnp.broadcast_to(step[8 + i : 9 + i, cols], (8, 128))
                real, imag = [c], [s]
                for _ in range(half // 8 - 1):
                    c, s = c * cs - s * ss, s * cs + c * ss
                    real.append(c)
                    imag.append(s)
                weights = jnp.concatenate(real + imag, 0).astype(jnp.bfloat16)
                parts = jnp.dot(rows, weights, preferred_element_type=jnp.float32)
                total = jnp.zeros(upper.shape, jnp.float32)
                for a in range(coarse):
                    turn = jnp.where(
                        upper,
                        jnp.broadcast_to(outer[16 * a + i : 16 * a + i + 1, cols], upper.shape),
                        jnp.broadcast_to(outer[16 * a + 8 + i : 16 * a + 9 + i, cols], upper.shape),
                    )
                    total = total + parts[2 * centres * a : 2 * centres * (a + 1)] * turn
                total = total + pltpu.roll(total, centres, 0)
                if i % 2 == 0:
                    held[zb] = total
                else:
                    tile = (r * bases + base) * 4 + i // 2
                    proj[tile, :, cols] = jnp.where(upper, held[zb], total)

    def one_base(base, carry):
        one_group(base, 0)
        one_group(base, 1)
        return carry

    lax.fori_loop(0, bases, one_base, 0)

    sends = proj[...].reshape(-1, 128 * blocks).astype(jnp.bfloat16)
    devices, rows = rank.shape
    ranks = jnp.broadcast_to(rank[...][:, None, :], (devices, 8, rows)).reshape(devices * 8, rows)
    lane8 = iota((devices * 8, rows), 0) % 8
    pick = (ranks == lane8.astype(jnp.float32)).astype(jnp.bfloat16)
    for k in range(4):
        y = jnp.dot(pick, sends[:, 256 * k : 256 * (k + 1)], preferred_element_type=jnp.float32)
        pair = [y[:, :128].reshape(devices, 8, 128), y[:, 128:].reshape(devices, 8, 128)]
        out[:, 16 * k : 16 * (k + 1), :] = jnp.concatenate(pair, 1).astype(jnp.bfloat16)
    last = jnp.dot(
        (rank[...] == 8.0).astype(jnp.bfloat16), sends, preferred_element_type=jnp.float32
    )
    for k in range(8):
        ninth[pl.ds(k, devices, stride=8), :] = last[:, 128 * k : 128 * (k + 1)]
    tags = jnp.broadcast_to(keys[...][:, None, :], (devices, 8, 128))
    pair = [ninth[...].reshape(devices, 8, 128), tags]
    out[:, 64:80, :] = jnp.concatenate(pair, 1).astype(jnp.bfloat16)


def open_kernel(own, times, amps, reach, landing, earlier, order, up, down, mine, rank, keys, sems):
    edge = up.shape[0]
    copies = [
        pltpu.make_async_copy(own.at[own.shape[0] - edge :], up, sems.at[0]),
        pltpu.make_async_copy(own.at[:edge], down, sems.at[1]),
    ]
    for copy in copies:
        copy.start()
    rows = [table[r : r + 1, :] for table in (times, amps) for r in range(table.shape[0])]
    lanes = range(0, times.shape[1], 128)
    tile = jnp.concatenate([row[:, at : at + 128] for row in rows for at in lanes], 0)
    mine[...] = jnp.broadcast_to(tile[None], mine.shape)

    devices, rows = rank.shape
    tile = iota((devices, rows), 0)
    named = jnp.zeros((devices, rows), jnp.float32)
    column = jnp.zeros((devices, rows), jnp.float32)
    for t in range(reach.shape[0]):
        hit = jnp.broadcast_to(reach[t : t + 1, :], (devices, rows)) == tile
        land = jnp.broadcast_to(landing[t : t + 1, :], (devices, rows)).astype(jnp.float32)
        named = named + jnp.where(hit, 1.0, 0.0)
        column = column + jnp.where(hit, land + 1.0, 0.0)
    count = jnp.dot(named.astype(jnp.bfloat16), earlier[...], preferred_element_type=jnp.float32)
    slot = jnp.where(named > 0.0, count, -1.0)
    rank[...] = jnp.dot(
        slot.astype(jnp.bfloat16), order[...], preferred_element_type=jnp.float32
    )
    lane = iota((devices, 128), 1)
    table = jnp.zeros((devices, 128), jnp.float32)
    for k in range(SLOTS):
        value = jnp.sum(jnp.where(slot == k, column, 0.0), axis=1, keepdims=True)
        table = jnp.where(lane == k, value, table)
    keys[...] = table - 1.0
    for copy in copies:
        copy.wait()


def place_kernel(incoming, image, ninth):
    devices = incoming.shape[0]
    tail = incoming[:, 64:80, :].astype(jnp.float32)
    tags = tail[:, 8:16, :]
    ninth[...] = tail[:, 0:8, :].reshape(devices * 8, 128)
    lane = iota((devices, 128), 1)
    hit9 = (tags[:, 0, :][:, 8:9] == lane.astype(jnp.float32)).astype(jnp.bfloat16)
    tags = jnp.concatenate([tags, tags], 1).reshape(devices * 16, 128)
    lane = iota((devices * 16, 128), 1)
    row = iota((devices * 16, 128), 0) % 16
    key = jnp.sum(jnp.where(lane == row % 8, tags, 0.0), axis=1, keepdims=True)
    hit = key == lane.astype(jnp.float32)
    both = jnp.concatenate(
        [
            (hit & (row < 8)).astype(jnp.bfloat16),
            (hit & (row >= 8)).astype(jnp.bfloat16),
        ],
        1,
    )
    contract = (((0,), (0,)), ((), ()))
    for k in range(4):
        rows = incoming[:, 16 * k : 16 * (k + 1), :].reshape(devices * 16, 128)
        y = lax.dot_general(rows, both, contract, preferred_element_type=jnp.float32)
        for q in range(2):
            last = ninth[pl.ds(2 * k + q, devices, stride=8), :].astype(jnp.bfloat16)
            last = lax.dot_general(last, hit9, contract, preferred_element_type=jnp.float32)
            cut = 256 * k + 128 * q
            image[cut : cut + 128, :] = y[:, 128 * q : 128 * (q + 1)] + last


def vmem(count):
    return [pl.BlockSpec(memory_space=pltpu.VMEM)] * count


def near(*arrays):
    return tuple(pltpu.with_memory_space_constraint(array, pltpu.VMEM) for array in arrays)


def call(kernel, shapes, args, scratch=(), specs=()):
    return pl.pallas_call(
        kernel,
        out_shape=shapes,
        in_specs=list(specs) + vmem(len(args) - len(specs)),
        out_specs=jax.tree.map(lambda _: pl.BlockSpec(memory_space=pltpu.VMEM), shapes),
        scratch_shapes=list(scratch),
        compiler_params=pltpu.CompilerParams(vmem_limit_bytes=56 * 1024 * 1024),
    )(*args)


def on_device(traces, taper, ray_param, reach, landing, travel_time, amplitude):
    f32, bf16 = jnp.float32, jnp.bfloat16
    freqs = traces.shape[2] // 2
    window = taper.shape[0]
    half = window // 2
    rays = ray_param.shape[0]
    rows = traces.shape[1]
    centres = rows // half
    depth = travel_time.shape[1]
    reach_count = reach.shape[2]
    line_count, size = lax.axis_size("line"), lax.axis_size("xline")
    devices = line_count * size
    coarse = freqs // FINE
    factor = 1.0 / math.sqrt(2.0 * freqs * centres * rays * reach_count / X)

    own = traces[0]
    beam_count = centres * rays
    earlier = np.triu(np.ones((beam_count, beam_count), np.float32), 1)
    order = np.arange(beam_count).reshape(centres, rays // 16, 4, 2, 2)
    order = np.eye(beam_count, dtype=np.float32)[:, order.transpose(4, 1, 2, 3, 0).reshape(-1)]
    edge = (half // 2, 2 * freqs)
    last, first, mine, rank, keys = call(
        open_kernel,
        (
            pltpu.VMEM(edge, bf16),
            pltpu.VMEM(edge, bf16),
            pltpu.VMEM((size, 4 * depth // 128, 128), f32),
            pltpu.VMEM((devices, beam_count), f32),
            pltpu.VMEM((devices, 128), f32),
        ),
        (
            own,
            travel_time,
            amplitude,
            reach[0].T,
            landing[0].T,
            jnp.asarray(earlier, bf16),
            jnp.asarray(order, bf16),
        ),
        [pltpu.SemaphoreType.DMA((2,))],
        [pl.BlockSpec(memory_space=pl.ANY)],
    )
    up = [(i, i + 1) for i in range(size - 1)]
    down = [(j, i) for i, j in up]
    before = lax.ppermute(last, "xline", up)
    after = lax.ppermute(first, "xline", down)
    times = lax.all_to_all(mine, "xline", split_axis=0, concat_axis=0, tiled=True)
    times = times.reshape(size // 8, 8 * mine.shape[1], 128)

    at = np.arange(8 * 128)
    fold = fold_matrix()[at // 16 % 2 * 128 + at // 128 * 16 + at % 16]
    folded = call(
        slant_kernel,
        pltpu.VMEM((rays, 2 * coarse * centres, FINE), f32),
        (
            *near(before),
            own,
            *near(after),
            taper[None],
            ray_param[None],
            jnp.asarray(fold, bf16),
        ),
        [
            pltpu.VMEM((rows + half, 2 * freqs), bf16),
            pltpu.VMEM((256 * centres, 256 * centres), bf16),
            pltpu.VMEM((freqs // 16, 4 * half, 128), bf16),
            pltpu.VMEM((freqs // 16, rays, 128), f32),
        ],
    )
    outgoing = call(
        functools.partial(project_kernel, factor, coarse, centres),
        pltpu.VMEM((devices, 80, 128), bf16),
        near(times, folded, rank, keys),
        [
            pltpu.VMEM((depth // 128, 128, 128), f32),
            pltpu.VMEM((16, depth), f32),
            pltpu.VMEM((16 * coarse, depth), f32),
            pltpu.VMEM((beam_count // (2 * centres), 2 * centres, depth), f32),
            pltpu.VMEM((devices * 8, 128), f32),
        ],
    )
    incoming = lax.all_to_all(
        outgoing, ("line", "xline"), split_axis=0, concat_axis=0, tiled=True
    )
    image = call(
        place_kernel,
        jax.ShapeDtypeStruct((depth, X), f32),
        near(incoming),
        [pltpu.VMEM((8 * devices, 128), f32)],
    )
    return image[None]


def solution(mesh):
    placed = (
        P("line", "xline", None),
        P(),
        P(),
        P("line", "xline", None),
        P("line", "xline", None),
        P("xline", None),
        P("xline", None),
    )
    return jax.shard_map(
        on_device, mesh=mesh, in_specs=placed, out_specs=P("line", None, "xline"), check_vma=False
    )
```

```python
import functools
import math

import jax
import jax.numpy as jnp
import numpy as np
from jax import lax
from jax.experimental import pallas as pl
from jax.experimental.pallas import tpu as pltpu
from jax.sharding import PartitionSpec as P

X = 128
FINE = 128
SLOTS = 9
BATCH = 8


def iota(shape, dim):
    return lax.broadcasted_iota(jnp.int32, shape, dim)


def fold_matrix():
    half = FINE // 2
    plus = np.zeros((FINE, half), np.float32)
    minus = np.zeros((FINE, half), np.float32)
    for m in range(half):
        plus[half + m, m] = plus[half - 1 - m, m] = 1.0
        minus[half + m, m], minus[half - 1 - m, m] = 1.0, -1.0
    zero = np.zeros_like(plus)
    real = np.concatenate([plus, zero, zero, -minus], 1)
    imag = np.concatenate([zero, minus, plus, zero], 1)
    return np.concatenate([real, imag], 0)


def pick_column(row, at):
    hit = iota((at.shape[0], row.shape[1]), 1) == at
    return jnp.sum(jnp.where(hit, row, 0.0), axis=1, keepdims=True)


def slant_kernel(before, own, after, taper, ray, fold, out, data, order, rows, beams):
    half = before.shape[0] * 2
    window = 2 * half
    rays = ray.shape[1]
    freqs = own.shape[1] // 2
    centres = own.shape[0] // half
    blocks = freqs // 128
    data[: half // 2] = before[...]
    data[half // 2 : half // 2 + own.shape[0]] = own[...]
    data[half // 2 + own.shape[0] :] = after[...]

    column = iota((1, order.shape[1]), 1)
    source = column // 16 % 8 * 128 + column // 128 * 16 + column % 16
    order[...] = (iota(order.shape, 0) == source).astype(jnp.bfloat16)

    weight = taper[...] * (1.0 / math.sqrt(window))
    place = iota((half, 1), 0)
    high_weight = pick_column(weight, half + place)
    low_weight = pick_column(weight, half - 1 - place)
    flip = (iota((half, half), 0) + iota((half, half), 1) == half - 1).astype(jnp.bfloat16)
    lane = iota((half, 128), 1)
    even = lane % 2 == 0
    for block in range(blocks):
        parts = [
            data[n * half : n * half + window, part * freqs + block * 128 :][:, :128]
            for n in range(centres)
            for part in range(2)
        ]
        moved = jnp.dot(
            jnp.concatenate(parts, 1), order[...], preferred_element_type=jnp.float32
        )
        low = jnp.dot(flip, moved[:half].astype(jnp.bfloat16), preferred_element_type=jnp.float32)
        low, high = low * low_weight, moved[half:] * high_weight
        total, diff = high + low, high - low
        for g in range(8):
            plus = total[:, 128 * g : 128 * (g + 1)]
            minus = diff[:, 128 * g : 128 * (g + 1)]
            minus = jnp.where(
                lane % 32 < 16, pltpu.roll(minus, 112, 1), -pltpu.roll(minus, 16, 1)
            )
            stack = [
                jnp.where(even, plus, 0.0),
                jnp.where(even, 0.0, plus),
                jnp.where(even, minus, 0.0),
                jnp.where(even, 0.0, minus),
            ]
            rows[block * 8 + g] = jnp.concatenate(stack, 0).astype(jnp.bfloat16)

    slow = pick_column(ray[...], iota((rays, 1), 0))
    lane = iota((rays, 128), 1)
    offset = (lane % half).astype(jnp.float32) + 0.5
    angle = slow * offset * (math.pi / freqs)
    c1, s1 = jnp.cos(angle), jnp.sin(angle)
    cs, ss = 1.0 - 2.0 * s1 * s1, 2.0 * s1 * c1
    first = lane < half
    pair = lane % 16 // 2

    def one_group(g, state):
        c, s = state
        total = jnp.zeros((rays, 128), jnp.float32)
        for start in range(0, 8, BATCH):
            steer = []
            for _ in range(BATCH):
                steer.append(jnp.concatenate([c, s], 1).astype(jnp.bfloat16))
                c, s = c * cs - s * ss, s * cs + c * ss
            y = jnp.dot(
                jnp.concatenate(steer, 0), rows[g], preferred_element_type=jnp.float32
            )
            for q in range(BATCH):
                total = jnp.where(pair == start + q, y[q * rays : (q + 1) * rays], total)
        beams[g] = total
        return c, s

    begin = (jnp.where(first, c1, cs), jnp.where(first, s1, ss))
    lax.fori_loop(0, 8 * blocks, one_group, begin, unroll=8)

    flat = out.reshape(rays * out.shape[1], 128)
    centre = lane // 32
    for block in range(blocks):
        fine, rest = [], []
        for g in range(8):
            value = beams[block * 8 + g]
            fine.append(value.astype(jnp.bfloat16).astype(jnp.float32))
            rest.append(value - fine[-1])
        stack = [
            jnp.concatenate([jnp.where(centre == n, v, 0.0) for v in piece], 1)
            for piece in (fine, rest)
            for n in range(centres)
        ]
        folded = jnp.dot(
            jnp.concatenate(stack, 0).astype(jnp.bfloat16),
            fold[...],
            preferred_element_type=jnp.float32,
        )
        folded = folded[: centres * rays] + folded[centres * rays :]
        for n in range(centres):
            for v in range(2):
                row = (2 * block + v) * centres + n
                value = folded[n * rays : (n + 1) * rays, 128 * v : 128 * (v + 1)]
                flat[pl.ds(row, rays, stride=out.shape[1]), :] = value


def project_kernel(factor, coarse, centres, times, folded, pick, pick9, keys, out, seed, step, outer, proj, ninth):
    half = FINE // 2
    blocks = seed.shape[0]
    bases = times.shape[0]
    upper = iota((2 * centres, 128), 0) < centres

    def one_group(base, r):
        for zb in range(blocks):
            cols = slice(zb * 128, zb * 128 + 128)
            t = times[base, pl.ds(8 * r + zb, 8, stride=32), :]
            amp = times[base, pl.ds(16 + 8 * r + zb, 8, stride=32), :] * factor
            angle = t * (math.pi / (2 * coarse * FINE))
            c0, s0 = jnp.cos(angle), jnp.sin(angle)
            c1, s1 = 1.0 - 2.0 * s0 * s0, 2.0 * s0 * c0
            c, s = c0, s0
            for m in range(8):
                seed[zb, m * 8 : m * 8 + 8, :] = c
                seed[zb, 64 + m * 8 : 72 + m * 8, :] = s
                if m < 7:
                    c, s = c * c1 - s * s1, s * c1 + c * s1
            c, s = c1, s1
            for power in range(6):
                c, s = 1.0 - 2.0 * s * s, 2.0 * s * c
                if power == 2:
                    step[0:8, cols] = c
                    step[8:16, cols] = s
            ca, sa = (c * c0 - s * s0) * amp, (s * c0 + c * s0) * amp
            cb, sb = 1.0 - 2.0 * s * s, 2.0 * s * c
            for a in range(coarse):
                outer[16 * a : 16 * a + 8, cols] = ca
                outer[16 * a + 8 : 16 * a + 16, cols] = sa
                ca, sa = ca * cb - sa * sb, sa * cb + ca * sb
        held = [None] * blocks
        for i in range(8):
            p = base * 16 + 2 * i + r
            rows = folded[p].astype(jnp.bfloat16)
            for zb in range(blocks):
                cols = slice(zb * 128, zb * 128 + 128)
                c = seed[zb, pl.ds(i, 8, stride=8), :]
                s = seed[zb, pl.ds(64 + i, 8, stride=8), :]
                cs = jnp.broadcast_to(step[i : i + 1, cols], (8, 128))
                ss = jnp.broadcast_to(step[8 + i : 9 + i, cols], (8, 128))
                real, imag = [c], [s]
                for _ in range(half // 8 - 1):
                    c, s = c * cs - s * ss, s * cs + c * ss
                    real.append(c)
                    imag.append(s)
                weights = jnp.concatenate(real + imag, 0).astype(jnp.bfloat16)
                parts = jnp.dot(rows, weights, preferred_element_type=jnp.float32)
                total = jnp.zeros(upper.shape, jnp.float32)
                for a in range(coarse):
                    turn = jnp.where(
                        upper,
                        jnp.broadcast_to(outer[16 * a + i : 16 * a + i + 1, cols], upper.shape),
                        jnp.broadcast_to(outer[16 * a + 8 + i : 16 * a + 9 + i, cols], upper.shape),
                    )
                    total = total + parts[2 * centres * a : 2 * centres * (a + 1)] * turn
                total = total + pltpu.roll(total, centres, 0)
                if i % 2 == 0:
                    held[zb] = total
                else:
                    tile = (r * bases + base) * 4 + i // 2
                    proj[tile, :, cols] = jnp.where(upper, held[zb], total)

    def one_base(base, carry):
        one_group(base, 0)
        one_group(base, 1)
        return carry

    lax.fori_loop(0, bases, one_base, 0)

    sends = proj[...].reshape(-1, 128 * blocks).astype(jnp.bfloat16)
    devices = keys.shape[0]
    for k in range(4):
        y = jnp.dot(pick[...], sends[:, 256 * k : 256 * (k + 1)], preferred_element_type=jnp.float32)
        pair = [y[:, :128].reshape(devices, 8, 128), y[:, 128:].reshape(devices, 8, 128)]
        out[:, 16 * k : 16 * (k + 1), :] = jnp.concatenate(pair, 1).astype(jnp.bfloat16)
    last = jnp.dot(pick9[...], sends, preferred_element_type=jnp.float32)
    for k in range(8):
        ninth[pl.ds(k, devices, stride=8), :] = last[:, 128 * k : 128 * (k + 1)]
    tags = jnp.broadcast_to(keys[...][:, None, :], (devices, 8, 128))
    pair = [ninth[...].reshape(devices, 8, 128), tags]
    out[:, 64:80, :] = jnp.concatenate(pair, 1).astype(jnp.bfloat16)


def open_kernel(own, times, amps, up, down, mine, sems):
    edge = up.shape[0]
    copies = [
        pltpu.make_async_copy(own.at[own.shape[0] - edge :], up, sems.at[0]),
        pltpu.make_async_copy(own.at[:edge], down, sems.at[1]),
    ]
    for copy in copies:
        copy.start()
    rows = [table[r : r + 1, :] for table in (times, amps) for r in range(table.shape[0])]
    lanes = range(0, times.shape[1], 128)
    tile = jnp.concatenate([row[:, at : at + 128] for row in rows for at in lanes], 0)
    mine[...] = jnp.broadcast_to(tile[None], mine.shape)
    for copy in copies:
        copy.wait()


def route_kernel(centres, reach, landing, pick, ninth, keys):
    devices, rows = ninth.shape
    tile = iota((devices, rows), 0)
    named = jnp.zeros((devices, rows), jnp.float32)
    column = jnp.zeros((devices, rows), jnp.float32)
    for t in range(reach.shape[0]):
        hit = jnp.broadcast_to(reach[t : t + 1, :], (devices, rows)) == tile
        land = jnp.broadcast_to(landing[t : t + 1, :], (devices, rows)).astype(jnp.float32)
        named = named + jnp.where(hit, 1.0, 0.0)
        column = column + jnp.where(hit, land + 1.0, 0.0)
    first, second = iota((rows, rows), 0), iota((rows, rows), 1)
    earlier = (first < second).astype(jnp.bfloat16)
    count = jnp.dot(named.astype(jnp.bfloat16), earlier, preferred_element_type=jnp.float32)
    slot = jnp.where(named > 0.0, count, -1.0)
    rays = rows // centres
    tile = second % centres * rays + second // (rays // 2 * centres)
    tile += second // (8 * centres) % (rays // 16) * 16
    tile += second // (2 * centres) % 4 * 4 + second // centres % 2 * 2
    order = (first == tile).astype(jnp.bfloat16)
    moved = jnp.dot(slot.astype(jnp.bfloat16), order, preferred_element_type=jnp.float32)
    wide = jnp.broadcast_to(moved[:, None, :], (devices, 8, rows)).reshape(devices * 8, rows)
    row = iota((devices * 8, rows), 0) % 8
    pick[...] = (wide == row.astype(jnp.float32)).astype(jnp.bfloat16)
    ninth[...] = (moved == 8.0).astype(jnp.bfloat16)
    lane = iota((devices, 128), 1)
    table = jnp.zeros((devices, 128), jnp.float32)
    for k in range(SLOTS):
        value = jnp.sum(jnp.where(slot == k, column, 0.0), axis=1, keepdims=True)
        table = jnp.where(lane == k, value, table)
    keys[...] = table - 1.0


def place_kernel(incoming, image, ninth):
    devices = incoming.shape[0]
    tail = incoming[:, 64:80, :].astype(jnp.float32)
    tags = tail[:, 8:16, :]
    ninth[...] = tail[:, 0:8, :].reshape(devices * 8, 128)
    lane = iota((devices, 128), 1)
    hit9 = (tags[:, 0, :][:, 8:9] == lane.astype(jnp.float32)).astype(jnp.bfloat16)
    tags = jnp.concatenate([tags, tags], 1).reshape(devices * 16, 128)
    lane = iota((devices * 16, 128), 1)
    row = iota((devices * 16, 128), 0) % 16
    key = jnp.sum(jnp.where(lane == row % 8, tags, 0.0), axis=1, keepdims=True)
    hit = key == lane.astype(jnp.float32)
    both = jnp.concatenate(
        [
            (hit & (row < 8)).astype(jnp.bfloat16),
            (hit & (row >= 8)).astype(jnp.bfloat16),
        ],
        1,
    )
    contract = (((0,), (0,)), ((), ()))
    for k in range(4):
        rows = incoming[:, 16 * k : 16 * (k + 1), :].reshape(devices * 16, 128)
        y = lax.dot_general(rows, both, contract, preferred_element_type=jnp.float32)
        for q in range(2):
            last = ninth[pl.ds(2 * k + q, devices, stride=8), :].astype(jnp.bfloat16)
            last = lax.dot_general(last, hit9, contract, preferred_element_type=jnp.float32)
            cut = 256 * k + 128 * q
            image[cut : cut + 128, :] = y[:, 128 * q : 128 * (q + 1)] + last


def vmem(count):
    return [pl.BlockSpec(memory_space=pltpu.VMEM)] * count


def near(*arrays):
    return tuple(pltpu.with_memory_space_constraint(array, pltpu.VMEM) for array in arrays)


def call(kernel, shapes, args, scratch=(), specs=(), flops=0):
    return pl.pallas_call(
        kernel,
        out_shape=shapes,
        in_specs=list(specs) + vmem(len(args) - len(specs)),
        out_specs=jax.tree.map(lambda _: pl.BlockSpec(memory_space=pltpu.VMEM), shapes),
        scratch_shapes=list(scratch),
        cost_estimate=pl.CostEstimate(flops=flops, bytes_accessed=0, transcendentals=0),
        compiler_params=pltpu.CompilerParams(vmem_limit_bytes=56 * 1024 * 1024),
    )(*args)


def on_device(traces, taper, ray_param, reach, landing, travel_time, amplitude):
    f32, bf16 = jnp.float32, jnp.bfloat16
    freqs = traces.shape[2] // 2
    window = taper.shape[0]
    half = window // 2
    rays = ray_param.shape[0]
    rows = traces.shape[1]
    centres = rows // half
    depth = travel_time.shape[1]
    reach_count = reach.shape[2]
    line_count, size = lax.axis_size("line"), lax.axis_size("xline")
    devices = line_count * size
    coarse = freqs // FINE
    factor = 1.0 / math.sqrt(2.0 * freqs * centres * rays * reach_count / X)

    own = traces[0]
    beam_count = centres * rays
    edge = (half // 2, 2 * freqs)
    last, first, mine = call(
        open_kernel,
        (
            pltpu.VMEM(edge, bf16),
            pltpu.VMEM(edge, bf16),
            pltpu.VMEM((size, 4 * depth // 128, 128), f32),
        ),
        (own, travel_time, amplitude),
        [pltpu.SemaphoreType.DMA((2,))],
        [pl.BlockSpec(memory_space=pl.ANY)],
    )
    pick, pick9, keys = call(
        functools.partial(route_kernel, centres),
        (
            pltpu.VMEM((8 * devices, beam_count), bf16),
            pltpu.VMEM((devices, beam_count), bf16),
            pltpu.VMEM((devices, 128), f32),
        ),
        (reach[0].T, landing[0].T),
        flops=1_000_000_000,
    )
    up = [(i, i + 1) for i in range(size - 1)]
    down = [(j, i) for i, j in up]
    before = lax.ppermute(last, "xline", up)
    after = lax.ppermute(first, "xline", down)
    times = lax.all_to_all(mine, "xline", split_axis=0, concat_axis=0, tiled=True)
    times = times.reshape(size // 8, 8 * mine.shape[1], 128)

    at = np.arange(8 * 128)
    fold = fold_matrix()[at // 16 % 2 * 128 + at // 128 * 16 + at % 16]
    folded = call(
        slant_kernel,
        pltpu.VMEM((rays, 2 * coarse * centres, FINE), f32),
        (
            *near(before),
            own,
            *near(after),
            taper[None],
            ray_param[None],
            jnp.asarray(fold, bf16),
        ),
        [
            pltpu.VMEM((rows + half, 2 * freqs), bf16),
            pltpu.VMEM((256 * centres, 256 * centres), bf16),
            pltpu.VMEM((freqs // 16, 4 * half, 128), bf16),
            pltpu.VMEM((freqs // 16, rays, 128), f32),
        ],
        flops=8_000_000_000,
    )
    outgoing = call(
        functools.partial(project_kernel, factor, coarse, centres),
        pltpu.VMEM((devices, 80, 128), bf16),
        near(times, folded, pick, pick9, keys),
        [
            pltpu.VMEM((depth // 128, 128, 128), f32),
            pltpu.VMEM((16, depth), f32),
            pltpu.VMEM((16 * coarse, depth), f32),
            pltpu.VMEM((beam_count // (2 * centres), 2 * centres, depth), f32),
            pltpu.VMEM((devices * 8, 128), f32),
        ],
    )
    incoming = lax.all_to_all(
        outgoing, ("line", "xline"), split_axis=0, concat_axis=0, tiled=True
    )
    image = call(
        place_kernel,
        jax.ShapeDtypeStruct((depth, X), f32),
        near(incoming),
        [pltpu.VMEM((8 * devices, 128), f32)],
    )
    return image[None]


def solution(mesh):
    placed = (
        P("line", "xline", None),
        P(),
        P(),
        P("line", "xline", None),
        P("line", "xline", None),
        P("xline", None),
        P("xline", None),
    )
    return jax.shard_map(
        on_device, mesh=mesh, in_specs=placed, out_specs=P("line", None, "xline"), check_vma=False
    )
```

```python
import functools
import math

import jax
import jax.numpy as jnp
import numpy as np
from jax import lax
from jax.experimental import pallas as pl
from jax.experimental.pallas import tpu as pltpu
from jax.sharding import PartitionSpec as P

X = 128
FINE = 128
SLOTS = 9
BATCH = 8


def iota(shape, dim):
    return lax.broadcasted_iota(jnp.int32, shape, dim)


def fold_matrix():
    half = FINE // 2
    plus = np.zeros((FINE, half), np.float32)
    minus = np.zeros((FINE, half), np.float32)
    for m in range(half):
        plus[half + m, m] = plus[half - 1 - m, m] = 1.0
        minus[half + m, m], minus[half - 1 - m, m] = 1.0, -1.0
    zero = np.zeros_like(plus)
    real = np.concatenate([plus, zero, zero, -minus], 1)
    imag = np.concatenate([zero, minus, plus, zero], 1)
    return np.concatenate([real, imag], 0)


def pick_column(row, at):
    hit = iota((at.shape[0], row.shape[1]), 1) == at
    return jnp.sum(jnp.where(hit, row, 0.0), axis=1, keepdims=True)


def slant_kernel(before, own, after, taper, ray, fold, order, out, data, rows, beams):
    half = before.shape[0] * 2
    window = 2 * half
    rays = ray.shape[1]
    freqs = own.shape[1] // 2
    centres = own.shape[0] // half
    blocks = freqs // 128
    data[: half // 2] = before[...]
    data[half // 2 : half // 2 + own.shape[0]] = own[...]
    data[half // 2 + own.shape[0] :] = after[...]

    weight = taper[...] * (1.0 / math.sqrt(window))
    place = iota((half, 1), 0)
    high_weight = pick_column(weight, half + place)
    low_weight = pick_column(weight, half - 1 - place)
    flip = (iota((half, half), 0) + iota((half, half), 1) == half - 1).astype(jnp.bfloat16)
    lane = iota((half, 128), 1)
    even = lane % 2 == 0
    side = lane % 32 < 16
    def prepare(block):
        parts = [
            data[n * half : n * half + window, part * freqs + block * 128 :][:, :128]
            for n in range(centres)
            for part in range(2)
        ]
        moved = jnp.dot(
            jnp.concatenate(parts, 1), order[...], preferred_element_type=jnp.float32
        )
        low = jnp.dot(flip, moved[:half].astype(jnp.bfloat16), preferred_element_type=jnp.float32)
        low, high = low * low_weight, moved[half:] * high_weight
        total, diff = high + low, high - low
        for g in range(8):
            plus = total[:, 128 * g : 128 * (g + 1)]
            minus = diff[:, 128 * g : 128 * (g + 1)]
            minus = jnp.where(
                side, pltpu.roll(minus, 112, 1), -pltpu.roll(minus, 16, 1)
            )
            stack = [
                jnp.where(even, plus, 0.0),
                jnp.where(even, 0.0, plus),
                jnp.where(even, minus, 0.0),
                jnp.where(even, 0.0, minus),
            ]
            rows[block * 8 + g] = jnp.concatenate(stack, 0).astype(jnp.bfloat16)

    slow = pick_column(ray[...], iota((rays, 1), 0))
    lane = iota((rays, 128), 1)
    offset = (lane % half).astype(jnp.float32) + 0.5
    angle = slow * offset * (math.pi / freqs)
    c1, s1 = jnp.cos(angle), jnp.sin(angle)
    cs, ss = 1.0 - 2.0 * s1 * s1, 2.0 * s1 * c1
    first = lane < half
    pair = lane % 16 // 2

    def one_group(g, state):
        c, s = state
        total = jnp.zeros((rays, 128), jnp.float32)
        for start in range(0, 8, BATCH):
            steer = []
            for _ in range(BATCH):
                steer.append(jnp.concatenate([c, s], 1).astype(jnp.bfloat16))
                c, s = c * cs - s * ss, s * cs + c * ss
            y = jnp.dot(
                jnp.concatenate(steer, 0), rows[g], preferred_element_type=jnp.float32
            )
            for q in range(BATCH):
                total = jnp.where(pair == start + q, y[q * rays : (q + 1) * rays], total)
        beams[g] = total
        return c, s

    flat = out.reshape(rays * out.shape[1], 128)
    centre = lane // 32
    def finish(block):
        fine, rest = [], []
        for g in range(8):
            value = beams[block * 8 + g]
            fine.append(value.astype(jnp.bfloat16).astype(jnp.float32))
            rest.append(value - fine[-1])
        stack = [
            jnp.concatenate([jnp.where(centre == n, v, 0.0) for v in piece], 1)
            for piece in (fine, rest)
            for n in range(centres)
        ]
        folded = jnp.dot(
            jnp.concatenate(stack, 0).astype(jnp.bfloat16),
            fold[...],
            preferred_element_type=jnp.float32,
        )
        folded = folded[: centres * rays] + folded[centres * rays :]
        for n in range(centres):
            for v in range(2):
                row = (2 * block + v) * centres + n
                value = folded[n * rays : (n + 1) * rays, 128 * v : 128 * (v + 1)]
                flat[pl.ds(row, rays, stride=out.shape[1]), :] = value

    state = (jnp.where(first, c1, cs), jnp.where(first, s1, ss))
    prepare(0)
    for block in range(blocks):
        if block + 1 < blocks:
            prepare(block + 1)
        for g in range(8):
            state = one_group(block * 8 + g, state)
        if block > 0:
            finish(block - 1)
    finish(blocks - 1)


def project_kernel(coarse, centres, times, folded, pick, pick9, keys, out, seed, step, outer, proj, ninth):
    half = FINE // 2
    blocks = seed.shape[0]
    bases = times.shape[0]
    upper = iota((2 * centres, 128), 0) < centres

    def one_group(base, r):
        for zb in range(blocks):
            cols = slice(zb * 128, zb * 128 + 128)
            s0 = times[base, pl.ds(8 * r + zb, 8, stride=32), :]
            amp = times[base, pl.ds(16 + 8 * r + zb, 8, stride=32), :]
            c0 = jnp.sqrt(1.0 - s0 * s0)
            c1, s1 = 1.0 - 2.0 * s0 * s0, 2.0 * s0 * c0
            c, s = c0, s0
            for m in range(8):
                seed[zb, m * 8 : m * 8 + 8, :] = c
                seed[zb, 64 + m * 8 : 72 + m * 8, :] = s
                if m < 7:
                    c, s = c * c1 - s * s1, s * c1 + c * s1
            c, s = c1, s1
            for power in range(6):
                c, s = 1.0 - 2.0 * s * s, 2.0 * s * c
                if power == 2:
                    step[0:8, cols] = c
                    step[8:16, cols] = s
            ca, sa = (c * c0 - s * s0) * amp, (s * c0 + c * s0) * amp
            cb, sb = 1.0 - 2.0 * s * s, 2.0 * s * c
            for a in range(coarse):
                outer[16 * a : 16 * a + 8, cols] = ca
                outer[16 * a + 8 : 16 * a + 16, cols] = sa
                ca, sa = ca * cb - sa * sb, sa * cb + ca * sb
        held = [None] * blocks
        for i in range(8):
            p = base * 16 + 2 * i + r
            rows = folded[p].astype(jnp.bfloat16)
            for zb in range(blocks):
                cols = slice(zb * 128, zb * 128 + 128)
                c = seed[zb, pl.ds(i, 8, stride=8), :]
                s = seed[zb, pl.ds(64 + i, 8, stride=8), :]
                cs = jnp.broadcast_to(step[i : i + 1, cols], (8, 128))
                ss = jnp.broadcast_to(step[8 + i : 9 + i, cols], (8, 128))
                real, imag = [c], [s]
                for _ in range(half // 8 - 1):
                    c, s = c * cs - s * ss, s * cs + c * ss
                    real.append(c)
                    imag.append(s)
                weights = jnp.concatenate(real + imag, 0).astype(jnp.bfloat16)
                parts = jnp.dot(rows, weights, preferred_element_type=jnp.float32)
                total = jnp.zeros(upper.shape, jnp.float32)
                for a in range(coarse):
                    turn = jnp.where(
                        upper,
                        jnp.broadcast_to(outer[16 * a + i : 16 * a + i + 1, cols], upper.shape),
                        jnp.broadcast_to(outer[16 * a + 8 + i : 16 * a + 9 + i, cols], upper.shape),
                    )
                    total = total + parts[2 * centres * a : 2 * centres * (a + 1)] * turn
                total = total + pltpu.roll(total, centres, 0)
                if i % 2 == 0:
                    held[zb] = total
                else:
                    tile = (r * bases + base) * 4 + i // 2
                    proj[tile, :, cols] = jnp.where(upper, held[zb], total)

    def one_base(base, carry):
        one_group(base, 0)
        one_group(base, 1)
        return carry

    lax.fori_loop(0, bases, one_base, 0)

    sends = proj[...].reshape(-1, 128 * blocks).astype(jnp.bfloat16)
    devices = keys.shape[0]
    for k in range(4):
        y = jnp.dot(pick[...], sends[:, 256 * k : 256 * (k + 1)], preferred_element_type=jnp.float32)
        pair = [y[:, :128].reshape(devices, 8, 128), y[:, 128:].reshape(devices, 8, 128)]
        out[:, 16 * k : 16 * (k + 1), :] = jnp.concatenate(pair, 1).astype(jnp.bfloat16)
    last = jnp.dot(pick9[...], sends, preferred_element_type=jnp.float32)
    for k in range(8):
        ninth[pl.ds(k, devices, stride=8), :] = last[:, 128 * k : 128 * (k + 1)]
    tags = jnp.broadcast_to(keys[...][:, None, :], (devices, 8, 128))
    pair = [ninth[...].reshape(devices, 8, 128), tags]
    out[:, 64:80, :] = jnp.concatenate(pair, 1).astype(jnp.bfloat16)


def open_kernel(scale, factor, own, times, amps, up, down, mine, held, sems):
    edge = up.shape[0]
    pairs = [
        (times, held.at[0]),
        (amps, held.at[1]),
        (own.at[own.shape[0] - edge :], up),
        (own.at[:edge], down),
    ]
    copies = [pltpu.make_async_copy(x, y, sems.at[k]) for k, (x, y) in enumerate(pairs)]
    for copy in copies:
        copy.start()
    copies[0].wait()
    copies[1].wait()
    tables = (jnp.sin(held[0] * scale), held[1] * factor)
    rows = [table[r : r + 1, :] for table in tables for r in range(held.shape[1])]
    lanes = range(0, held.shape[2], 128)
    tile = jnp.concatenate([row[:, at : at + 128] for row in rows for at in lanes], 0)
    mine[...] = jnp.broadcast_to(tile[None], mine.shape)
    copies[2].wait()
    copies[3].wait()


def route_kernel(centres, reach, landing, pick, ninth, keys, lanes):
    devices, rows = ninth.shape
    tile = iota((devices, rows), 0)
    named = jnp.zeros((devices, rows), jnp.float32)
    column = jnp.zeros((devices, rows), jnp.float32)
    for t in range(reach.shape[0]):
        hit = jnp.broadcast_to(reach[t : t + 1, :], (devices, rows)) == tile
        land = jnp.broadcast_to(landing[t : t + 1, :], (devices, rows)).astype(jnp.float32)
        named = named + jnp.where(hit, 1.0, 0.0)
        column = column + jnp.where(hit, land + 1.0, 0.0)
    first, second = iota((rows, rows), 0), iota((rows, rows), 1)
    earlier = (first < second).astype(jnp.bfloat16)
    count = jnp.dot(named.astype(jnp.bfloat16), earlier, preferred_element_type=jnp.float32)
    slot = jnp.where(named > 0.0, count, -1.0)
    rays = rows // centres
    tile = second % centres * rays + second // (rays // 2 * centres)
    tile += second // (8 * centres) % (rays // 16) * 16
    tile += second // (2 * centres) % 4 * 4 + second // centres % 2 * 2
    order = (first == tile).astype(jnp.bfloat16)
    moved = jnp.dot(slot.astype(jnp.bfloat16), order, preferred_element_type=jnp.float32)
    wide = jnp.broadcast_to(moved[:, None, :], (devices, 8, rows)).reshape(devices * 8, rows)
    row = iota((devices * 8, rows), 0) % 8
    pick[...] = (wide == row.astype(jnp.float32)).astype(jnp.bfloat16)
    ninth[...] = (moved == 8.0).astype(jnp.bfloat16)
    lane = iota((devices, 128), 1)
    table = jnp.zeros((devices, 128), jnp.float32)
    for k in range(SLOTS):
        value = jnp.sum(jnp.where(slot == k, column, 0.0), axis=1, keepdims=True)
        table = jnp.where(lane == k, value, table)
    keys[...] = table - 1.0
    column = iota((1, lanes.shape[1]), 1)
    source = column // 16 % 8 * 128 + column // 128 * 16 + column % 16
    lanes[...] = (iota(lanes.shape, 0) == source).astype(jnp.bfloat16)


def place_kernel(incoming, image, ninth):
    devices = incoming.shape[0]
    tail = incoming[:, 64:80, :].astype(jnp.float32)
    tags = tail[:, 8:16, :]
    ninth[...] = tail[:, 0:8, :].reshape(devices * 8, 128)
    lane = iota((devices, 128), 1)
    hit9 = (tags[:, 0, :][:, 8:9] == lane.astype(jnp.float32)).astype(jnp.bfloat16)
    tags = jnp.concatenate([tags, tags], 1).reshape(devices * 16, 128)
    lane = iota((devices * 16, 128), 1)
    row = iota((devices * 16, 128), 0) % 16
    key = jnp.sum(jnp.where(lane == row % 8, tags, 0.0), axis=1, keepdims=True)
    hit = key == lane.astype(jnp.float32)
    both = jnp.concatenate(
        [
            (hit & (row < 8)).astype(jnp.bfloat16),
            (hit & (row >= 8)).astype(jnp.bfloat16),
        ],
        1,
    )
    contract = (((0,), (0,)), ((), ()))
    for k in range(4):
        rows = incoming[:, 16 * k : 16 * (k + 1), :].reshape(devices * 16, 128)
        y = lax.dot_general(rows, both, contract, preferred_element_type=jnp.float32)
        for q in range(2):
            last = ninth[pl.ds(2 * k + q, devices, stride=8), :].astype(jnp.bfloat16)
            last = lax.dot_general(last, hit9, contract, preferred_element_type=jnp.float32)
            cut = 256 * k + 128 * q
            image[cut : cut + 128, :] = y[:, 128 * q : 128 * (q + 1)] + last


def vmem(count):
    return [pl.BlockSpec(memory_space=pltpu.VMEM)] * count


def near(*arrays):
    return tuple(pltpu.with_memory_space_constraint(array, pltpu.VMEM) for array in arrays)


def call(kernel, shapes, args, scratch=(), specs=(), flops=0):
    return pl.pallas_call(
        kernel,
        out_shape=shapes,
        in_specs=list(specs) + vmem(len(args) - len(specs)),
        out_specs=jax.tree.map(lambda _: pl.BlockSpec(memory_space=pltpu.VMEM), shapes),
        scratch_shapes=list(scratch),
        cost_estimate=pl.CostEstimate(flops=flops, bytes_accessed=0, transcendentals=0),
        compiler_params=pltpu.CompilerParams(vmem_limit_bytes=56 * 1024 * 1024),
    )(*args)


def on_device(traces, taper, ray_param, reach, landing, travel_time, amplitude):
    f32, bf16 = jnp.float32, jnp.bfloat16
    freqs = traces.shape[2] // 2
    window = taper.shape[0]
    half = window // 2
    rays = ray_param.shape[0]
    rows = traces.shape[1]
    centres = rows // half
    depth = travel_time.shape[1]
    reach_count = reach.shape[2]
    line_count, size = lax.axis_size("line"), lax.axis_size("xline")
    devices = line_count * size
    coarse = freqs // FINE
    factor = 1.0 / math.sqrt(2.0 * freqs * centres * rays * reach_count / X)

    own = traces[0]
    beam_count = centres * rays
    edge = (half // 2, 2 * freqs)
    last, first, mine = call(
        functools.partial(open_kernel, math.pi / (2 * freqs), factor),
        (
            pltpu.VMEM(edge, bf16),
            pltpu.VMEM(edge, bf16),
            pltpu.VMEM((size, 4 * depth // 128, 128), f32),
        ),
        (own, travel_time, amplitude),
        [pltpu.VMEM((2,) + travel_time.shape, f32), pltpu.SemaphoreType.DMA((4,))],
        [pl.BlockSpec(memory_space=pl.ANY)] * 3,
    )
    pick, pick9, keys, order = call(
        functools.partial(route_kernel, centres),
        (
            pltpu.VMEM((8 * devices, beam_count), bf16),
            pltpu.VMEM((devices, beam_count), bf16),
            pltpu.VMEM((devices, 128), f32),
            pltpu.VMEM((256 * centres, 256 * centres), bf16),
        ),
        (reach[0].T, landing[0].T),
        flops=1_000_000_000,
    )
    up = [(i, i + 1) for i in range(size - 1)]
    down = [(j, i) for i, j in up]
    before = lax.ppermute(last, "xline", up)
    after = lax.ppermute(first, "xline", down)
    times = lax.all_to_all(mine, "xline", split_axis=0, concat_axis=0, tiled=True)
    times = times.reshape(size // 8, 8 * mine.shape[1], 128)

    at = np.arange(8 * 128)
    fold = fold_matrix()[at // 16 % 2 * 128 + at // 128 * 16 + at % 16]
    folded = call(
        slant_kernel,
        pltpu.VMEM((rays, 2 * coarse * centres, FINE), f32),
        (
            *near(before),
            own,
            *near(after),
            taper[None],
            ray_param[None],
            jnp.asarray(fold, bf16),
            *near(order),
        ),
        [
            pltpu.VMEM((rows + half, 2 * freqs), bf16),
            pltpu.VMEM((freqs // 16, 4 * half, 128), bf16),
            pltpu.VMEM((freqs // 16, rays, 128), f32),
        ],
        flops=8_000_000_000,
    )
    outgoing = call(
        functools.partial(project_kernel, coarse, centres),
        pltpu.VMEM((devices, 80, 128), bf16),
        near(times, folded, pick, pick9, keys),
        [
            pltpu.VMEM((depth // 128, 128, 128), f32),
            pltpu.VMEM((16, depth), f32),
            pltpu.VMEM((16 * coarse, depth), f32),
            pltpu.VMEM((beam_count // (2 * centres), 2 * centres, depth), f32),
            pltpu.VMEM((devices * 8, 128), f32),
        ],
    )
    incoming = lax.all_to_all(
        outgoing, ("line", "xline"), split_axis=0, concat_axis=0, tiled=True
    )
    image = call(
        place_kernel,
        jax.ShapeDtypeStruct((depth, X), f32),
        near(incoming),
        [pltpu.VMEM((8 * devices, 128), f32)],
    )
    return image[None]


def solution(mesh):
    placed = (
        P("line", "xline", None),
        P(),
        P(),
        P("line", "xline", None),
        P("line", "xline", None),
        P("xline", None),
        P("xline", None),
    )
    return jax.shard_map(
        on_device, mesh=mesh, in_specs=placed, out_specs=P("line", None, "xline"), check_vma=False
    )
```

```python
import functools
import math

import jax
import jax.numpy as jnp
import numpy as np
from jax import lax
from jax.experimental import pallas as pl
from jax.experimental.pallas import tpu as pltpu
from jax.sharding import PartitionSpec as P

X = 128
FINE = 128
SLOTS = 9
BATCH = 8


def iota(shape, dim):
    return lax.broadcasted_iota(jnp.int32, shape, dim)


def fold_matrix():
    half = FINE // 2
    plus = np.zeros((FINE, half), np.float32)
    minus = np.zeros((FINE, half), np.float32)
    for m in range(half):
        plus[half + m, m] = plus[half - 1 - m, m] = 1.0
        minus[half + m, m], minus[half - 1 - m, m] = 1.0, -1.0
    zero = np.zeros_like(plus)
    real = np.concatenate([plus, zero, zero, -minus], 1)
    imag = np.concatenate([zero, minus, plus, zero], 1)
    return np.concatenate([real, imag], 0)


def pick_column(row, at):
    hit = iota((at.shape[0], row.shape[1]), 1) == at
    return jnp.sum(jnp.where(hit, row, 0.0), axis=1, keepdims=True)


def slant_kernel(before, own, after, taper, ray, fold, out, data, rows, beams):
    half = before.shape[0] * 2
    window = 2 * half
    rays = ray.shape[1]
    freqs = own.shape[1] // 2
    centres = own.shape[0] // half
    blocks = freqs // 128
    data[: half // 2] = before[...]
    data[half // 2 : half // 2 + own.shape[0]] = own[...]
    data[half // 2 + own.shape[0] :] = after[...]

    weight = taper[...] * (1.0 / math.sqrt(window))
    place = iota((half, 1), 0)
    high_weight = pick_column(weight, half + place)
    low_weight = pick_column(weight, half - 1 - place)
    flip = (iota((half, half), 0) + iota((half, half), 1) == half - 1).astype(jnp.bfloat16)
    lane = iota((half, 128), 1)
    even = lane % 2 == 0
    side = lane % 32 < 16
    column = iota((1, 256), 1)
    source = column // 16 % 2 * 128 + column // 32 * 16 + column % 16
    order = (iota((256, 256), 0) == source).astype(jnp.bfloat16)

    def prepare(block):
        sums, turns = [], []
        for n in range(centres):
            parts = [
                data[n * half : n * half + window, part * freqs + block * 128 :][:, :128]
                for part in range(2)
            ]
            moved = jnp.dot(
                jnp.concatenate(parts, 1), order, preferred_element_type=jnp.float32
            )
            low = moved[:half].astype(jnp.bfloat16)
            low = jnp.dot(flip, low, preferred_element_type=jnp.float32) * low_weight
            high = moved[half:] * high_weight
            for value, into in ((high + low, sums), (high - low, turns)):
                for cut in (0, 128):
                    tile = value[:, cut : cut + 128]
                    if into is turns:
                        tile = jnp.where(side, pltpu.roll(tile, 112, 1), -pltpu.roll(tile, 16, 1))
                    into.append(pltpu.roll(tile, 32 * n, 1) if n else tile)
        for g in range(8):
            plus, minus = (
                functools.reduce(
                    lambda x, c: jnp.where(lane // 32 == c, table[(c - g) % centres * 2 + g // 4], x),
                    range(1, centres),
                    table[-g % centres * 2 + g // 4],
                )
                for table in (sums, turns)
            )
            stack = [
                jnp.where(even, plus, 0.0),
                jnp.where(even, 0.0, plus),
                jnp.where(even, minus, 0.0),
                jnp.where(even, 0.0, minus),
            ]
            rows[block * 8 + g] = jnp.concatenate(stack, 0).astype(jnp.bfloat16)

    slow = pick_column(ray[...], iota((rays, 1), 0))
    lanes = iota((rays, 128), 1)
    offset = (lanes % half).astype(jnp.float32) + 0.5
    angle = slow * offset * (math.pi / freqs)
    c1, s1 = jnp.cos(angle), jnp.sin(angle)
    cs, ss = 1.0 - 2.0 * s1 * s1, 2.0 * s1 * c1
    first = lanes < half
    pair = lanes % 16 // 2

    def one_group(g, state):
        c, s = state
        total = jnp.zeros((rays, 128), jnp.float32)
        for start in range(0, 8, BATCH):
            steer = []
            for _ in range(BATCH):
                steer.append(jnp.concatenate([c, s], 1).astype(jnp.bfloat16))
                c, s = c * cs - s * ss, s * cs + c * ss
            y = jnp.dot(
                jnp.concatenate(steer, 0), rows[g], preferred_element_type=jnp.float32
            )
            for q in range(BATCH):
                total = jnp.where(pair == start + q, y[q * rays : (q + 1) * rays], total)
        beams[g] = total
        return c, s

    flat = out.reshape(rays * out.shape[1], 128)
    def finish(block):
        fine, rest = [], []
        for n in range(centres):
            tiles = []
            for first_group in (block * 8, block * 8 + 4):
                tile = beams[first_group + -n % centres]
                for c in range(1, centres):
                    tile = jnp.where(lanes // 32 == c, beams[first_group + (c - n) % centres], tile)
                tiles.append(pltpu.roll(tile, 128 - 32 * n, 1) if n else tile)
            value = jnp.concatenate(tiles, 1)
            fine.append(value.astype(jnp.bfloat16).astype(jnp.float32))
            rest.append(value - fine[-1])
        folded = jnp.dot(
            jnp.concatenate(fine + rest, 0).astype(jnp.bfloat16),
            fold[...],
            preferred_element_type=jnp.float32,
        )
        folded = folded[: centres * rays] + folded[centres * rays :]
        for n in range(centres):
            for v in range(2):
                row = (2 * block + v) * centres + n
                value = folded[n * rays : (n + 1) * rays, 128 * v : 128 * (v + 1)]
                flat[pl.ds(row, rays, stride=out.shape[1]), :] = value

    state = (jnp.where(first, c1, cs), jnp.where(first, s1, ss))
    prepare(0)
    for block in range(blocks):
        if block + 1 < blocks:
            prepare(block + 1)
        for g in range(8):
            state = one_group(block * 8 + g, state)
        if block > 0:
            finish(block - 1)
    finish(blocks - 1)


def project_kernel(coarse, centres, times, folded, pick, pick9, keys, out, seed, step, outer, proj, ninth):
    half = FINE // 2
    blocks = seed.shape[0]
    bases = times.shape[0]
    upper = iota((2 * centres, 128), 0) < centres

    def one_group(base, r):
        for zb in range(blocks):
            cols = slice(zb * 128, zb * 128 + 128)
            s0 = times[base, pl.ds(8 * r + zb, 8, stride=32), :]
            amp = times[base, pl.ds(16 + 8 * r + zb, 8, stride=32), :]
            c0 = jnp.sqrt(1.0 - s0 * s0)
            c1, s1 = 1.0 - 2.0 * s0 * s0, 2.0 * s0 * c0
            c, s = c0, s0
            for m in range(8):
                seed[zb, m * 8 : m * 8 + 8, :] = c
                seed[zb, 64 + m * 8 : 72 + m * 8, :] = s
                if m < 7:
                    c, s = c * c1 - s * s1, s * c1 + c * s1
            c, s = c1, s1
            for power in range(6):
                c, s = 1.0 - 2.0 * s * s, 2.0 * s * c
                if power == 2:
                    step[0:8, cols] = c
                    step[8:16, cols] = s
            ca, sa = (c * c0 - s * s0) * amp, (s * c0 + c * s0) * amp
            cb, sb = 1.0 - 2.0 * s * s, 2.0 * s * c
            for a in range(coarse):
                outer[16 * a : 16 * a + 8, cols] = ca
                outer[16 * a + 8 : 16 * a + 16, cols] = sa
                ca, sa = ca * cb - sa * sb, sa * cb + ca * sb
        held = [None] * blocks
        for i in range(8):
            p = base * 16 + 2 * i + r
            rows = folded[p].astype(jnp.bfloat16)
            for zb in range(blocks):
                cols = slice(zb * 128, zb * 128 + 128)
                c = seed[zb, pl.ds(i, 8, stride=8), :]
                s = seed[zb, pl.ds(64 + i, 8, stride=8), :]
                cs = jnp.broadcast_to(step[i : i + 1, cols], (8, 128))
                ss = jnp.broadcast_to(step[8 + i : 9 + i, cols], (8, 128))
                real, imag = [c], [s]
                for _ in range(half // 8 - 1):
                    c, s = c * cs - s * ss, s * cs + c * ss
                    real.append(c)
                    imag.append(s)
                weights = jnp.concatenate(real + imag, 0).astype(jnp.bfloat16)
                parts = jnp.dot(rows, weights, preferred_element_type=jnp.float32)
                total = jnp.zeros(upper.shape, jnp.float32)
                for a in range(coarse):
                    turn = jnp.where(
                        upper,
                        jnp.broadcast_to(outer[16 * a + i : 16 * a + i + 1, cols], upper.shape),
                        jnp.broadcast_to(outer[16 * a + 8 + i : 16 * a + 9 + i, cols], upper.shape),
                    )
                    total = total + parts[2 * centres * a : 2 * centres * (a + 1)] * turn
                total = total + pltpu.roll(total, centres, 0)
                if i % 2 == 0:
                    held[zb] = total
                else:
                    tile = (r * bases + base) * 4 + i // 2
                    proj[tile, :, cols] = jnp.where(upper, held[zb], total)

    def one_base(base, carry):
        one_group(base, 0)
        one_group(base, 1)
        return carry

    lax.fori_loop(0, bases, one_base, 0)

    sends = proj[...].reshape(-1, 128 * blocks).astype(jnp.bfloat16)
    devices = keys.shape[0]
    for k in range(4):
        y = jnp.dot(pick[...], sends[:, 256 * k : 256 * (k + 1)], preferred_element_type=jnp.float32)
        pair = [y[:, :128].reshape(devices, 8, 128), y[:, 128:].reshape(devices, 8, 128)]
        out[:, 16 * k : 16 * (k + 1), :] = jnp.concatenate(pair, 1).astype(jnp.bfloat16)
    last = jnp.dot(pick9[...], sends, preferred_element_type=jnp.float32)
    for k in range(8):
        ninth[pl.ds(k, devices, stride=8), :] = last[:, 128 * k : 128 * (k + 1)]
    tags = jnp.broadcast_to(keys[...][:, None, :], (devices, 8, 128))
    pair = [ninth[...].reshape(devices, 8, 128), tags]
    out[:, 64:80, :] = jnp.concatenate(pair, 1).astype(jnp.bfloat16)


def open_kernel(scale, factor, own, times, amps, up, down, mine, held, sems):
    edge = up.shape[0]
    pairs = [
        (times, held.at[0]),
        (amps, held.at[1]),
        (own.at[own.shape[0] - edge :], up),
        (own.at[:edge], down),
    ]
    copies = [pltpu.make_async_copy(x, y, sems.at[k]) for k, (x, y) in enumerate(pairs)]
    for copy in copies:
        copy.start()
    copies[0].wait()
    copies[1].wait()
    tables = (jnp.sin(held[0] * scale), held[1] * factor)
    rows = [table[r : r + 1, :] for table in tables for r in range(held.shape[1])]
    lanes = range(0, held.shape[2], 128)
    tile = jnp.concatenate([row[:, at : at + 128] for row in rows for at in lanes], 0)
    mine[...] = jnp.broadcast_to(tile[None], mine.shape)
    copies[2].wait()
    copies[3].wait()


def route_kernel(centres, reach, landing, pick, ninth, keys):
    devices, rows = ninth.shape
    tile = iota((devices, rows), 0)
    named = jnp.zeros((devices, rows), jnp.float32)
    column = jnp.zeros((devices, rows), jnp.float32)
    for t in range(reach.shape[0]):
        hit = jnp.broadcast_to(reach[t : t + 1, :], (devices, rows)) == tile
        land = jnp.broadcast_to(landing[t : t + 1, :], (devices, rows)).astype(jnp.float32)
        named = named + jnp.where(hit, 1.0, 0.0)
        column = column + jnp.where(hit, land + 1.0, 0.0)
    first, second = iota((rows, rows), 0), iota((rows, rows), 1)
    earlier = (first < second).astype(jnp.bfloat16)
    count = jnp.dot(named.astype(jnp.bfloat16), earlier, preferred_element_type=jnp.float32)
    slot = jnp.where(named > 0.0, count, -1.0)
    rays = rows // centres
    tile = second % centres * rays + second // (rays // 2 * centres)
    tile += second // (8 * centres) % (rays // 16) * 16
    tile += second // (2 * centres) % 4 * 4 + second // centres % 2 * 2
    order = (first == tile).astype(jnp.bfloat16)
    moved = jnp.dot(slot.astype(jnp.bfloat16), order, preferred_element_type=jnp.float32)
    wide = jnp.broadcast_to(moved[:, None, :], (devices, 8, rows)).reshape(devices * 8, rows)
    row = iota((devices * 8, rows), 0) % 8
    pick[...] = (wide == row.astype(jnp.float32)).astype(jnp.bfloat16)
    ninth[...] = (moved == 8.0).astype(jnp.bfloat16)
    lane = iota((devices, 128), 1)
    table = jnp.zeros((devices, 128), jnp.float32)
    for k in range(SLOTS):
        value = jnp.sum(jnp.where(slot == k, column, 0.0), axis=1, keepdims=True)
        table = jnp.where(lane == k, value, table)
    keys[...] = table - 1.0


def place_kernel(incoming, image, ninth):
    devices = incoming.shape[0]
    tail = incoming[:, 64:80, :].astype(jnp.float32)
    tags = tail[:, 8:16, :]
    ninth[...] = tail[:, 0:8, :].reshape(devices * 8, 128)
    lane = iota((devices, 128), 1)
    hit9 = (tags[:, 0, :][:, 8:9] == lane.astype(jnp.float32)).astype(jnp.bfloat16)
    tags = jnp.concatenate([tags, tags], 1).reshape(devices * 16, 128)
    lane = iota((devices * 16, 128), 1)
    row = iota((devices * 16, 128), 0) % 16
    key = jnp.sum(jnp.where(lane == row % 8, tags, 0.0), axis=1, keepdims=True)
    hit = key == lane.astype(jnp.float32)
    both = jnp.concatenate(
        [
            (hit & (row < 8)).astype(jnp.bfloat16),
            (hit & (row >= 8)).astype(jnp.bfloat16),
        ],
        1,
    )
    contract = (((0,), (0,)), ((), ()))
    for k in range(4):
        rows = incoming[:, 16 * k : 16 * (k + 1), :].reshape(devices * 16, 128)
        y = lax.dot_general(rows, both, contract, preferred_element_type=jnp.float32)
        for q in range(2):
            last = ninth[pl.ds(2 * k + q, devices, stride=8), :].astype(jnp.bfloat16)
            last = lax.dot_general(last, hit9, contract, preferred_element_type=jnp.float32)
            cut = 256 * k + 128 * q
            image[cut : cut + 128, :] = y[:, 128 * q : 128 * (q + 1)] + last


def vmem(count):
    return [pl.BlockSpec(memory_space=pltpu.VMEM)] * count


def near(*arrays):
    return tuple(pltpu.with_memory_space_constraint(array, pltpu.VMEM) for array in arrays)


def call(kernel, shapes, args, scratch=(), specs=(), flops=0):
    return pl.pallas_call(
        kernel,
        out_shape=shapes,
        in_specs=list(specs) + vmem(len(args) - len(specs)),
        out_specs=jax.tree.map(lambda _: pl.BlockSpec(memory_space=pltpu.VMEM), shapes),
        scratch_shapes=list(scratch),
        cost_estimate=pl.CostEstimate(flops=flops, bytes_accessed=0, transcendentals=0),
        compiler_params=pltpu.CompilerParams(vmem_limit_bytes=56 * 1024 * 1024),
    )(*args)


def on_device(traces, taper, ray_param, reach, landing, travel_time, amplitude):
    f32, bf16 = jnp.float32, jnp.bfloat16
    freqs = traces.shape[2] // 2
    window = taper.shape[0]
    half = window // 2
    rays = ray_param.shape[0]
    rows = traces.shape[1]
    centres = rows // half
    depth = travel_time.shape[1]
    reach_count = reach.shape[2]
    line_count, size = lax.axis_size("line"), lax.axis_size("xline")
    devices = line_count * size
    coarse = freqs // FINE
    factor = 1.0 / math.sqrt(2.0 * freqs * centres * rays * reach_count / X)

    own = traces[0]
    beam_count = centres * rays
    edge = (half // 2, 2 * freqs)
    last, first, mine = call(
        functools.partial(open_kernel, math.pi / (2 * freqs), factor),
        (
            pltpu.VMEM(edge, bf16),
            pltpu.VMEM(edge, bf16),
            pltpu.VMEM((size, 4 * depth // 128, 128), f32),
        ),
        (own, travel_time, amplitude),
        [pltpu.VMEM((2,) + travel_time.shape, f32), pltpu.SemaphoreType.DMA((4,))],
        [pl.BlockSpec(memory_space=pl.ANY)] * 3,
    )
    pick, pick9, keys = call(
        functools.partial(route_kernel, centres),
        (
            pltpu.VMEM((8 * devices, beam_count), bf16),
            pltpu.VMEM((devices, beam_count), bf16),
            pltpu.VMEM((devices, 128), f32),
        ),
        (reach[0].T, landing[0].T),
        flops=1_000_000_000,
    )
    up = [(i, i + 1) for i in range(size - 1)]
    down = [(j, i) for i, j in up]
    before = lax.ppermute(last, "xline", up)
    after = lax.ppermute(first, "xline", down)
    times = lax.all_to_all(mine, "xline", split_axis=0, concat_axis=0, tiled=True)
    times = times.reshape(size // 8, 8 * mine.shape[1], 128)

    at = np.arange(256)
    fold = fold_matrix()[at // 16 % 2 * 128 + at // 32 * 16 + at % 16]
    folded = call(
        slant_kernel,
        pltpu.VMEM((rays, 2 * coarse * centres, FINE), f32),
        (
            *near(before),
            own,
            *near(after),
            taper[None],
            ray_param[None],
            jnp.asarray(fold, bf16),
        ),
        [
            pltpu.VMEM((rows + half, 2 * freqs), bf16),
            pltpu.VMEM((freqs // 16, 4 * half, 128), bf16),
            pltpu.VMEM((freqs // 16, rays, 128), f32),
        ],
        flops=8_000_000_000,
    )
    outgoing = call(
        functools.partial(project_kernel, coarse, centres),
        pltpu.VMEM((devices, 80, 128), bf16),
        near(times, folded, pick, pick9, keys),
        [
            pltpu.VMEM((depth // 128, 128, 128), f32),
            pltpu.VMEM((16, depth), f32),
            pltpu.VMEM((16 * coarse, depth), f32),
            pltpu.VMEM((beam_count // (2 * centres), 2 * centres, depth), f32),
            pltpu.VMEM((devices * 8, 128), f32),
        ],
    )
    incoming = lax.all_to_all(
        outgoing, ("line", "xline"), split_axis=0, concat_axis=0, tiled=True
    )
    image = call(
        place_kernel,
        jax.ShapeDtypeStruct((depth, X), f32),
        near(incoming),
        [pltpu.VMEM((8 * devices, 128), f32)],
    )
    return image[None]


def solution(mesh):
    placed = (
        P("line", "xline", None),
        P(),
        P(),
        P("line", "xline", None),
        P("line", "xline", None),
        P("xline", None),
        P("xline", None),
    )
    return jax.shard_map(
        on_device, mesh=mesh, in_specs=placed, out_specs=P("line", None, "xline"), check_vma=False
    )
```

```python
import functools
import math

import jax
import jax.numpy as jnp
import numpy as np
from jax import lax
from jax.experimental import pallas as pl
from jax.experimental.pallas import tpu as pltpu
from jax.sharding import PartitionSpec as P

X = 128
FINE = 128
SLOTS = 9
BATCH = 8


def iota(shape, dim):
    return lax.broadcasted_iota(jnp.int32, shape, dim)


def fold_matrix():
    half = FINE // 2
    plus = np.zeros((FINE, half), np.float32)
    minus = np.zeros((FINE, half), np.float32)
    for m in range(half):
        plus[half + m, m] = plus[half - 1 - m, m] = 1.0
        minus[half + m, m], minus[half - 1 - m, m] = 1.0, -1.0
    zero = np.zeros_like(plus)
    real = np.concatenate([plus, zero, zero, -minus], 1)
    imag = np.concatenate([zero, minus, plus, zero], 1)
    return np.concatenate([real, imag], 0)


def pick_column(row, at):
    hit = iota((at.shape[0], row.shape[1]), 1) == at
    return jnp.sum(jnp.where(hit, row, 0.0), axis=1, keepdims=True)


def slant_kernel(before, own, after, taper, ray, fold, out, data, rows, beams):
    half = before.shape[0] * 2
    window = 2 * half
    rays = ray.shape[1]
    freqs = own.shape[1] // 2
    centres = own.shape[0] // half
    blocks = freqs // 128
    data[: half // 2] = before[...]
    data[half // 2 : half // 2 + own.shape[0]] = own[...]
    data[half // 2 + own.shape[0] :] = after[...]

    weight = taper[...] * (1.0 / math.sqrt(window))
    place = iota((half, 1), 0)
    high_weight = pick_column(weight, half + place)
    low_weight = pick_column(weight, half - 1 - place)
    flip = (iota((half, half), 0) + iota((half, half), 1) == half - 1).astype(jnp.bfloat16)
    lane = iota((half, 128), 1)
    even = lane % 2 == 0
    side = lane % 32 < 16
    column = iota((1, 256), 1)
    source = column // 16 % 2 * 128 + column // 32 * 16 + column % 16
    order = (iota((256, 256), 0) == source).astype(jnp.bfloat16)

    def prepare(block):
        sums, turns = [], []
        for n in range(centres):
            parts = [
                data[n * half : n * half + window, part * freqs + block * 128 :][:, :128]
                for part in range(2)
            ]
            moved = jnp.dot(
                jnp.concatenate(parts, 1), order, preferred_element_type=jnp.float32
            )
            low = moved[:half].astype(jnp.bfloat16)
            low = jnp.dot(flip, low, preferred_element_type=jnp.float32) * low_weight
            high = moved[half:] * high_weight
            for value, into in ((high + low, sums), (high - low, turns)):
                for cut in (0, 128):
                    tile = value[:, cut : cut + 128]
                    if into is turns:
                        tile = jnp.where(side, pltpu.roll(tile, 112, 1), -pltpu.roll(tile, 16, 1))
                    into.append(pltpu.roll(tile, 32 * n, 1) if n else tile)
        for g in range(8):
            plus, minus = (
                functools.reduce(
                    lambda x, c: jnp.where(lane // 32 == c, table[(c - g) % centres * 2 + g // 4], x),
                    range(1, centres),
                    table[-g % centres * 2 + g // 4],
                )
                for table in (sums, turns)
            )
            stack = [
                jnp.where(even, plus, 0.0),
                jnp.where(even, 0.0, plus),
                jnp.where(even, minus, 0.0),
                jnp.where(even, 0.0, minus),
            ]
            rows[block * 8 + g] = jnp.concatenate(stack, 0).astype(jnp.bfloat16)

    slow = pick_column(ray[...], iota((rays, 1), 0))
    lanes = iota((rays, 128), 1)
    offset = (lanes % half).astype(jnp.float32) + 0.5
    angle = slow * offset * (math.pi / freqs)
    c1, s1 = jnp.cos(angle), jnp.sin(angle)
    cs, ss = 1.0 - 2.0 * s1 * s1, 2.0 * s1 * c1
    first = lanes < half
    pair = lanes % 16 // 2

    def one_group(g, state):
        c, s = state
        total = jnp.zeros((rays, 128), jnp.float32)
        for start in range(0, 8, BATCH):
            steer = []
            for _ in range(BATCH):
                steer.append(jnp.concatenate([c, s], 1).astype(jnp.bfloat16))
                c, s = c * cs - s * ss, s * cs + c * ss
            y = jnp.dot(
                jnp.concatenate(steer, 0), rows[g], preferred_element_type=jnp.float32
            )
            for q in range(BATCH):
                total = jnp.where(pair == start + q, y[q * rays : (q + 1) * rays], total)
        beams[g] = total
        return c, s

    flat = out.reshape(rays * out.shape[1], 128)
    def finish(block):
        fine, rest = [], []
        for n in range(centres):
            tiles = []
            for first_group in (block * 8, block * 8 + 4):
                tile = beams[first_group + -n % centres]
                for c in range(1, centres):
                    tile = jnp.where(lanes // 32 == c, beams[first_group + (c - n) % centres], tile)
                tiles.append(pltpu.roll(tile, 128 - 32 * n, 1) if n else tile)
            value = jnp.concatenate(tiles, 1)
            fine.append(value.astype(jnp.bfloat16).astype(jnp.float32))
            rest.append(value - fine[-1])
        folded = jnp.dot(
            jnp.concatenate(fine + rest, 0).astype(jnp.bfloat16),
            fold[...],
            preferred_element_type=jnp.float32,
        )
        folded = folded[: centres * rays] + folded[centres * rays :]
        for n in range(centres):
            for v in range(2):
                row = (2 * block + v) * centres + n
                value = folded[n * rays : (n + 1) * rays, 128 * v : 128 * (v + 1)]
                flat[pl.ds(row, rays, stride=out.shape[1]), :] = value

    state = (jnp.where(first, c1, cs), jnp.where(first, s1, ss))
    prepare(0)
    for block in range(blocks):
        if block + 1 < blocks:
            prepare(block + 1)
        for g in range(8):
            state = one_group(block * 8 + g, state)
        if block > 0:
            finish(block - 1)
    finish(blocks - 1)


def project_kernel(coarse, centres, times, folded, pick, pick9, keys, out, seed, step, outer, proj, ninth):
    half = FINE // 2
    blocks = seed.shape[0]
    bases = times.shape[0]
    upper = iota((2 * centres, 128), 0) < centres

    def one_group(base, r):
        for zb in range(blocks):
            cols = slice(zb * 128, zb * 128 + 128)
            s0 = times[base, pl.ds(8 * r + zb, 8, stride=32), :]
            amp = times[base, pl.ds(16 + 8 * r + zb, 8, stride=32), :]
            c0 = jnp.sqrt(1.0 - s0 * s0)
            c1, s1 = 1.0 - 2.0 * s0 * s0, 2.0 * s0 * c0
            c, s = c0, s0
            for m in range(8):
                seed[zb, m * 8 : m * 8 + 8, :] = c
                seed[zb, 64 + m * 8 : 72 + m * 8, :] = s
                if m < 7:
                    c, s = c * c1 - s * s1, s * c1 + c * s1
            c, s = c1, s1
            for power in range(6):
                c, s = 1.0 - 2.0 * s * s, 2.0 * s * c
                if power == 2:
                    step[0:8, cols] = c
                    step[8:16, cols] = s
            ca, sa = (c * c0 - s * s0) * amp, (s * c0 + c * s0) * amp
            cb, sb = 1.0 - 2.0 * s * s, 2.0 * s * c
            for a in range(coarse):
                outer[16 * a : 16 * a + 8, cols] = ca
                outer[16 * a + 8 : 16 * a + 16, cols] = sa
                ca, sa = ca * cb - sa * sb, sa * cb + ca * sb
        held = [None] * blocks
        for i in range(8):
            p = base * 16 + 2 * i + r
            rows = folded[p].astype(jnp.bfloat16)
            for zb in range(blocks):
                cols = slice(zb * 128, zb * 128 + 128)
                c = seed[zb, pl.ds(i, 8, stride=8), :]
                s = seed[zb, pl.ds(64 + i, 8, stride=8), :]
                cs = jnp.broadcast_to(step[i : i + 1, cols], (8, 128))
                ss = jnp.broadcast_to(step[8 + i : 9 + i, cols], (8, 128))
                real, imag = [c], [s]
                for _ in range(half // 8 - 1):
                    c, s = c * cs - s * ss, s * cs + c * ss
                    real.append(c)
                    imag.append(s)
                weights = jnp.concatenate(real + imag, 0).astype(jnp.bfloat16)
                parts = jnp.dot(rows, weights, preferred_element_type=jnp.float32)
                total = jnp.zeros(upper.shape, jnp.float32)
                for a in range(coarse):
                    turn = jnp.where(
                        upper,
                        jnp.broadcast_to(outer[16 * a + i : 16 * a + i + 1, cols], upper.shape),
                        jnp.broadcast_to(outer[16 * a + 8 + i : 16 * a + 9 + i, cols], upper.shape),
                    )
                    total = total + parts[2 * centres * a : 2 * centres * (a + 1)] * turn
                total = total + pltpu.roll(total, centres, 0)
                if i % 2 == 0:
                    held[zb] = total
                else:
                    tile = (r * bases + base) * 4 + i // 2
                    proj[tile, :, cols] = jnp.where(upper, held[zb], total)

    def one_base(base, carry):
        one_group(base, 0)
        one_group(base, 1)
        return carry

    lax.fori_loop(0, bases, one_base, 0)

    sends = proj[...].reshape(-1, 128 * blocks).astype(jnp.bfloat16)
    devices = keys.shape[0]
    for k in range(4):
        y = jnp.dot(pick[...], sends[:, 256 * k : 256 * (k + 1)], preferred_element_type=jnp.float32)
        pair = [y[:, :128].reshape(devices, 8, 128), y[:, 128:].reshape(devices, 8, 128)]
        out[:, 16 * k : 16 * (k + 1), :] = jnp.concatenate(pair, 1).astype(jnp.bfloat16)
    last = jnp.dot(pick9[...], sends, preferred_element_type=jnp.float32)
    for k in range(8):
        ninth[pl.ds(k, devices, stride=8), :] = last[:, 128 * k : 128 * (k + 1)]
    tags = jnp.broadcast_to(keys[...][:, None, :], (devices, 8, 128))
    pair = [ninth[...].reshape(devices, 8, 128), tags]
    out[:, 64:80, :] = jnp.concatenate(pair, 1).astype(jnp.bfloat16)


def open_kernel(scale, factor, own, times, amps, up, down, mine, held, sems):
    edge = up.shape[0]
    pairs = [
        (times, held.at[0]),
        (amps, held.at[1]),
        (own.at[own.shape[0] - edge :], up),
        (own.at[:edge], down),
    ]
    copies = [pltpu.make_async_copy(x, y, sems.at[k]) for k, (x, y) in enumerate(pairs)]
    for copy in copies:
        copy.start()
    copies[0].wait()
    copies[1].wait()
    tables = (jnp.sin(held[0] * scale), held[1] * factor)
    rows = [table[r : r + 1, :] for table in tables for r in range(held.shape[1])]
    lanes = range(0, held.shape[2], 128)
    tile = jnp.concatenate([row[:, at : at + 128] for row in rows for at in lanes], 0)
    mine[...] = jnp.broadcast_to(tile[None], mine.shape)
    copies[2].wait()
    copies[3].wait()


def route_kernel(centres, reach, landing, pick, ninth, keys):
    devices, rows = ninth.shape
    tile = iota((devices, rows), 0)
    named = jnp.zeros((devices, rows), jnp.float32)
    column = jnp.zeros((devices, rows), jnp.float32)
    for t in range(reach.shape[0]):
        hit = jnp.broadcast_to(reach[t : t + 1, :], (devices, rows)) == tile
        land = jnp.broadcast_to(landing[t : t + 1, :], (devices, rows)).astype(jnp.float32)
        named = named + jnp.where(hit, 1.0, 0.0)
        column = column + jnp.where(hit, land + 1.0, 0.0)
    first, second = iota((rows, rows), 0), iota((rows, rows), 1)
    earlier = (first < second).astype(jnp.bfloat16)
    count = jnp.dot(named.astype(jnp.bfloat16), earlier, preferred_element_type=jnp.float32)
    slot = jnp.where(named > 0.0, count, -1.0)
    rays = rows // centres
    tile = second % centres * rays + second // (rays // 2 * centres)
    tile += second // (8 * centres) % (rays // 16) * 16
    tile += second // (2 * centres) % 4 * 4 + second // centres % 2 * 2
    order = (first == tile).astype(jnp.bfloat16)
    moved = jnp.dot(slot.astype(jnp.bfloat16), order, preferred_element_type=jnp.float32)
    wide = jnp.broadcast_to(moved[:, None, :], (devices, 8, rows)).reshape(devices * 8, rows)
    row = iota((devices * 8, rows), 0) % 8
    pick[...] = (wide == row.astype(jnp.float32)).astype(jnp.bfloat16)
    ninth[...] = (moved == 8.0).astype(jnp.bfloat16)
    lane = iota((devices, 128), 1)
    table = jnp.zeros((devices, 128), jnp.float32)
    for k in range(SLOTS):
        value = jnp.sum(jnp.where(slot == k, column, 0.0), axis=1, keepdims=True)
        table = jnp.where(lane == k, value, table)
    keys[...] = table - 1.0


def place_kernel(incoming, image, ninth):
    devices = incoming.shape[0]
    tail = incoming[:, 64:80, :].astype(jnp.float32)
    tags = tail[:, 8:16, :]
    ninth[...] = tail[:, 0:8, :].reshape(devices * 8, 128)
    lane = iota((devices, 128), 1)
    hit9 = (tags[:, 0, :][:, 8:9] == lane.astype(jnp.float32)).astype(jnp.bfloat16)
    tags = jnp.concatenate([tags, tags], 1).reshape(devices * 16, 128)
    lane = iota((devices * 16, 128), 1)
    row = iota((devices * 16, 128), 0) % 16
    key = jnp.sum(jnp.where(lane == row % 8, tags, 0.0), axis=1, keepdims=True)
    hit = key == lane.astype(jnp.float32)
    both = jnp.concatenate(
        [
            (hit & (row < 8)).astype(jnp.bfloat16),
            (hit & (row >= 8)).astype(jnp.bfloat16),
        ],
        1,
    )
    contract = (((0,), (0,)), ((), ()))
    for k in range(4):
        rows = incoming[:, 16 * k : 16 * (k + 1), :].reshape(devices * 16, 128)
        y = lax.dot_general(rows, both, contract, preferred_element_type=jnp.float32)
        for q in range(2):
            last = ninth[pl.ds(2 * k + q, devices, stride=8), :].astype(jnp.bfloat16)
            last = lax.dot_general(last, hit9, contract, preferred_element_type=jnp.float32)
            cut = 256 * k + 128 * q
            image[cut : cut + 128, :] = y[:, 128 * q : 128 * (q + 1)] + last


def vmem(count):
    return [pl.BlockSpec(memory_space=pltpu.VMEM)] * count


def near(*arrays):
    return tuple(pltpu.with_memory_space_constraint(array, pltpu.VMEM) for array in arrays)


def call(kernel, shapes, args, scratch=(), specs=(), flops=0):
    return pl.pallas_call(
        kernel,
        out_shape=shapes,
        in_specs=list(specs) + vmem(len(args) - len(specs)),
        out_specs=jax.tree.map(lambda _: pl.BlockSpec(memory_space=pltpu.VMEM), shapes),
        scratch_shapes=list(scratch),
        cost_estimate=pl.CostEstimate(flops=flops, bytes_accessed=0, transcendentals=0),
        compiler_params=pltpu.CompilerParams(vmem_limit_bytes=56 * 1024 * 1024),
    )(*args)


def on_device(traces, taper, ray_param, reach, landing, travel_time, amplitude):
    f32, bf16 = jnp.float32, jnp.bfloat16
    freqs = traces.shape[2] // 2
    window = taper.shape[0]
    half = window // 2
    rays = ray_param.shape[0]
    rows = traces.shape[1]
    centres = rows // half
    depth = travel_time.shape[1]
    reach_count = reach.shape[2]
    line_count, size = lax.axis_size("line"), lax.axis_size("xline")
    devices = line_count * size
    coarse = freqs // FINE
    factor = 1.0 / math.sqrt(2.0 * freqs * centres * rays * reach_count / X)

    own = traces[0]
    beam_count = centres * rays
    edge = (half // 2, 2 * freqs)
    last, first, mine = call(
        functools.partial(open_kernel, math.pi / (2 * freqs), factor),
        (
            pltpu.VMEM(edge, bf16),
            pltpu.VMEM(edge, bf16),
            pltpu.VMEM((size, 4 * depth // 128, 128), f32),
        ),
        (own, travel_time, amplitude),
        [pltpu.VMEM((2,) + travel_time.shape, f32), pltpu.SemaphoreType.DMA((4,))],
        [pl.BlockSpec(memory_space=pl.ANY)] * 3,
    )
    pick, pick9, keys = call(
        functools.partial(route_kernel, centres),
        (
            pltpu.VMEM((8 * devices, beam_count), bf16),
            pltpu.VMEM((devices, beam_count), bf16),
            pltpu.VMEM((devices, 128), f32),
        ),
        (reach[0].T, landing[0].T),
        flops=100_000_000,
    )
    up = [(i, i + 1) for i in range(size - 1)]
    down = [(j, i) for i, j in up]
    before = lax.ppermute(last, "xline", up)
    after = lax.ppermute(first, "xline", down)
    times = lax.all_to_all(mine, "xline", split_axis=0, concat_axis=0, tiled=True)
    times = times.reshape(size // 8, 8 * mine.shape[1], 128)

    at = np.arange(256)
    fold = fold_matrix()[at // 16 % 2 * 128 + at // 32 * 16 + at % 16]
    folded = call(
        slant_kernel,
        pltpu.VMEM((rays, 2 * coarse * centres, FINE), f32),
        (
            *near(before),
            own,
            *near(after),
            taper[None],
            ray_param[None],
            jnp.asarray(fold, bf16),
        ),
        [
            pltpu.VMEM((rows + half, 2 * freqs), bf16),
            pltpu.VMEM((freqs // 16, 4 * half, 128), bf16),
            pltpu.VMEM((freqs // 16, rays, 128), f32),
        ],
        flops=8_000_000_000,
    )
    outgoing = call(
        functools.partial(project_kernel, coarse, centres),
        pltpu.VMEM((devices, 80, 128), bf16),
        near(times, folded, pick, pick9, keys),
        [
            pltpu.VMEM((depth // 128, 128, 128), f32),
            pltpu.VMEM((16, depth), f32),
            pltpu.VMEM((16 * coarse, depth), f32),
            pltpu.VMEM((beam_count // (2 * centres), 2 * centres, depth), f32),
            pltpu.VMEM((devices * 8, 128), f32),
        ],
    )
    incoming = lax.all_to_all(
        outgoing, ("line", "xline"), split_axis=0, concat_axis=0, tiled=True
    )
    image = call(
        place_kernel,
        jax.ShapeDtypeStruct((depth, X), f32),
        near(incoming),
        [pltpu.VMEM((8 * devices, 128), f32)],
    )
    return image[None]


def solution(mesh):
    placed = (
        P("line", "xline", None),
        P(),
        P(),
        P("line", "xline", None),
        P("line", "xline", None),
        P("xline", None),
        P("xline", None),
    )
    return jax.shard_map(
        on_device, mesh=mesh, in_specs=placed, out_specs=P("line", None, "xline"), check_vma=False
    )
```

```python
import functools
import math

import jax
import jax.numpy as jnp
import numpy as np
from jax import lax
from jax.experimental import pallas as pl
from jax.experimental.pallas import tpu as pltpu
from jax.sharding import PartitionSpec as P

X = 128
FINE = 128
SLOTS = 9
BATCH = 8


def iota(shape, dim):
    return lax.broadcasted_iota(jnp.int32, shape, dim)


def fold_matrix():
    half = FINE // 2
    plus = np.zeros((FINE, half), np.float32)
    minus = np.zeros((FINE, half), np.float32)
    for m in range(half):
        plus[half + m, m] = plus[half - 1 - m, m] = 1.0
        minus[half + m, m], minus[half - 1 - m, m] = 1.0, -1.0
    zero = np.zeros_like(plus)
    real = np.concatenate([plus, zero, zero, -minus], 1)
    imag = np.concatenate([zero, minus, plus, zero], 1)
    return np.concatenate([real, imag], 0)


def pick_column(row, at):
    hit = iota((at.shape[0], row.shape[1]), 1) == at
    return jnp.sum(jnp.where(hit, row, 0.0), axis=1, keepdims=True)


def slant_kernel(before, own, after, taper, ray, fold, out, data, rows, beams):
    half = before.shape[0] * 2
    window = 2 * half
    rays = ray.shape[1]
    freqs = own.shape[1] // 2
    centres = own.shape[0] // half
    blocks = freqs // 128
    data[: half // 2] = before[...]
    data[half // 2 : half // 2 + own.shape[0]] = own[...]
    data[half // 2 + own.shape[0] :] = after[...]

    weight = taper[...] * (1.0 / math.sqrt(window))
    place = iota((half, 1), 0)
    high_weight = pick_column(weight, half + place)
    low_weight = pick_column(weight, half - 1 - place)
    flip = (iota((half, half), 0) + iota((half, half), 1) == half - 1).astype(jnp.bfloat16)
    lane = iota((half, 128), 1)
    even = lane % 2 == 0
    side = lane % 32 < 16
    column = iota((1, 256), 1)
    source = column // 16 % 2 * 128 + column // 32 * 16 + column % 16
    order = (iota((256, 256), 0) == source).astype(jnp.bfloat16)

    def prepare(block):
        sums, turns = [], []
        for n in range(centres):
            parts = [
                data[n * half : n * half + window, part * freqs + block * 128 :][:, :128]
                for part in range(2)
            ]
            moved = jnp.dot(
                jnp.concatenate(parts, 1), order, preferred_element_type=jnp.float32
            )
            low = moved[:half].astype(jnp.bfloat16)
            low = jnp.dot(flip, low, preferred_element_type=jnp.float32) * low_weight
            high = moved[half:] * high_weight
            for value, into in ((high + low, sums), (high - low, turns)):
                for cut in (0, 128):
                    tile = value[:, cut : cut + 128]
                    if into is turns:
                        tile = jnp.where(side, pltpu.roll(tile, 112, 1), -pltpu.roll(tile, 16, 1))
                    into.append(pltpu.roll(tile, 32 * n, 1) if n else tile)
        for g in range(8):
            plus, minus = (
                functools.reduce(
                    lambda x, c: jnp.where(lane // 32 == c, table[(c - g) % centres * 2 + g // 4], x),
                    range(1, centres),
                    table[-g % centres * 2 + g // 4],
                )
                for table in (sums, turns)
            )
            stack = [
                jnp.where(even, plus, 0.0),
                jnp.where(even, 0.0, plus),
                jnp.where(even, minus, 0.0),
                jnp.where(even, 0.0, minus),
            ]
            rows[block * 8 + g] = jnp.concatenate(stack, 0).astype(jnp.bfloat16)

    slow = pick_column(ray[...], iota((rays, 1), 0))
    lanes = iota((rays, 128), 1)
    offset = (lanes % half).astype(jnp.float32) + 0.5
    angle = slow * offset * (math.pi / freqs)
    c1, s1 = jnp.cos(angle), jnp.sin(angle)
    cs, ss = 1.0 - 2.0 * s1 * s1, 2.0 * s1 * c1
    first = lanes < half
    pair = lanes % 16 // 2

    def one_group(g, state):
        c, s = state
        total = jnp.zeros((rays, 128), jnp.float32)
        for start in range(0, 8, BATCH):
            steer = []
            for _ in range(BATCH):
                steer.append(jnp.concatenate([c, s], 1).astype(jnp.bfloat16))
                c, s = c * cs - s * ss, s * cs + c * ss
            y = jnp.dot(
                jnp.concatenate(steer, 0), rows[g], preferred_element_type=jnp.float32
            )
            for q in range(BATCH):
                total = jnp.where(pair == start + q, y[q * rays : (q + 1) * rays], total)
        beams[g] = total
        return c, s

    flat = out.reshape(rays * out.shape[1], 128)
    def finish(block):
        fine, rest = [], []
        for n in range(centres):
            tiles = []
            for first_group in (block * 8, block * 8 + 4):
                tile = beams[first_group + -n % centres]
                for c in range(1, centres):
                    tile = jnp.where(lanes // 32 == c, beams[first_group + (c - n) % centres], tile)
                tiles.append(pltpu.roll(tile, 128 - 32 * n, 1) if n else tile)
            value = jnp.concatenate(tiles, 1)
            fine.append(value.astype(jnp.bfloat16).astype(jnp.float32))
            rest.append(value - fine[-1])
        folded = jnp.dot(
            jnp.concatenate(fine + rest, 0).astype(jnp.bfloat16),
            fold[...],
            preferred_element_type=jnp.float32,
        )
        folded = folded[: centres * rays] + folded[centres * rays :]
        for n in range(centres):
            for v in range(2):
                row = (2 * block + v) * centres + n
                value = folded[n * rays : (n + 1) * rays, 128 * v : 128 * (v + 1)]
                flat[pl.ds(row, rays, stride=out.shape[1]), :] = value

    state = (jnp.where(first, c1, cs), jnp.where(first, s1, ss))
    prepare(0)
    for block in range(blocks):
        if block + 1 < blocks:
            prepare(block + 1)
        for g in range(8):
            state = one_group(block * 8 + g, state)
        if block > 0:
            finish(block - 1)
    finish(blocks - 1)


def project_kernel(coarse, centres, times, folded, pick, pick9, keys, out, seed, step, outer, proj, ninth):
    half = FINE // 2
    blocks = seed.shape[1]
    bases = times.shape[0]
    upper = iota((2 * centres, 128), 0) < centres

    def one_group(base, r):
        for zb in range(blocks):
            cols = slice(zb * 128, zb * 128 + 128)
            s0 = times[base, pl.ds(8 * r + zb, 8, stride=32), :]
            amp = times[base, pl.ds(16 + 8 * r + zb, 8, stride=32), :]
            c0 = jnp.sqrt(1.0 - s0 * s0)
            c1, s1 = 1.0 - 2.0 * s0 * s0, 2.0 * s0 * c0
            c, s = c0, s0
            for m in range(8):
                seed[r, zb, m * 8 : m * 8 + 8, :] = c
                seed[r, zb, 64 + m * 8 : 72 + m * 8, :] = s
                if m < 7:
                    c, s = c * c1 - s * s1, s * c1 + c * s1
            c, s = c1, s1
            for power in range(6):
                c, s = 1.0 - 2.0 * s * s, 2.0 * s * c
                if power == 2:
                    step[r, 0:8, cols] = c
                    step[r, 8:16, cols] = s
            ca, sa = (c * c0 - s * s0) * amp, (s * c0 + c * s0) * amp
            cb, sb = 1.0 - 2.0 * s * s, 2.0 * s * c
            for a in range(coarse):
                outer[r, 16 * a : 16 * a + 8, cols] = ca
                outer[r, 16 * a + 8 : 16 * a + 16, cols] = sa
                ca, sa = ca * cb - sa * sb, sa * cb + ca * sb
        held = [None] * blocks
        for i in range(8):
            p = base * 16 + 2 * i + r
            rows = folded[p].astype(jnp.bfloat16)
            for zb in range(blocks):
                cols = slice(zb * 128, zb * 128 + 128)
                c = seed[r, zb, pl.ds(i, 8, stride=8), :]
                s = seed[r, zb, pl.ds(64 + i, 8, stride=8), :]
                cs = jnp.broadcast_to(step[r, i : i + 1, cols], (8, 128))
                ss = jnp.broadcast_to(step[r, 8 + i : 9 + i, cols], (8, 128))
                real, imag = [c], [s]
                for _ in range(half // 8 - 1):
                    c, s = c * cs - s * ss, s * cs + c * ss
                    real.append(c)
                    imag.append(s)
                weights = jnp.concatenate(real + imag, 0).astype(jnp.bfloat16)
                parts = jnp.dot(rows, weights, preferred_element_type=jnp.float32)
                total = jnp.zeros(upper.shape, jnp.float32)
                for a in range(coarse):
                    turn = jnp.where(
                        upper,
                        jnp.broadcast_to(outer[r, 16 * a + i : 16 * a + i + 1, cols], upper.shape),
                        jnp.broadcast_to(outer[r, 16 * a + 8 + i : 16 * a + 9 + i, cols], upper.shape),
                    )
                    total = total + parts[2 * centres * a : 2 * centres * (a + 1)] * turn
                total = total + pltpu.roll(total, centres, 0)
                if i % 2 == 0:
                    held[zb] = total
                else:
                    tile = (r * bases + base) * 4 + i // 2
                    proj[tile, :, cols] = jnp.where(upper, held[zb], total)

    def one_base(base, carry):
        one_group(base, 0)
        one_group(base, 1)
        return carry

    lax.fori_loop(0, bases, one_base, 0)

    sends = proj[...].reshape(-1, 128 * blocks).astype(jnp.bfloat16)
    devices = keys.shape[0]
    for k in range(4):
        y = jnp.dot(pick[...], sends[:, 256 * k : 256 * (k + 1)], preferred_element_type=jnp.float32)
        pair = [y[:, :128].reshape(devices, 8, 128), y[:, 128:].reshape(devices, 8, 128)]
        out[:, 16 * k : 16 * (k + 1), :] = jnp.concatenate(pair, 1).astype(jnp.bfloat16)
    last = jnp.dot(pick9[...], sends, preferred_element_type=jnp.float32)
    for k in range(8):
        ninth[pl.ds(k, devices, stride=8), :] = last[:, 128 * k : 128 * (k + 1)]
    tags = jnp.broadcast_to(keys[...][:, None, :], (devices, 8, 128))
    pair = [ninth[...].reshape(devices, 8, 128), tags]
    out[:, 64:80, :] = jnp.concatenate(pair, 1).astype(jnp.bfloat16)


def open_kernel(scale, factor, own, times, amps, up, down, mine, held, sems):
    edge = up.shape[0]
    pairs = [
        (times, held.at[0]),
        (amps, held.at[1]),
        (own.at[own.shape[0] - edge :], up),
        (own.at[:edge], down),
    ]
    copies = [pltpu.make_async_copy(x, y, sems.at[k]) for k, (x, y) in enumerate(pairs)]
    for copy in copies:
        copy.start()
    copies[0].wait()
    copies[1].wait()
    tables = (jnp.sin(held[0] * scale), held[1] * factor)
    rows = [table[r : r + 1, :] for table in tables for r in range(held.shape[1])]
    lanes = range(0, held.shape[2], 128)
    tile = jnp.concatenate([row[:, at : at + 128] for row in rows for at in lanes], 0)
    mine[...] = jnp.broadcast_to(tile[None], mine.shape)
    copies[2].wait()
    copies[3].wait()


def route_kernel(centres, reach, landing, pick, ninth, keys):
    devices, rows = ninth.shape
    tile = iota((devices, rows), 0)
    named = jnp.zeros((devices, rows), jnp.float32)
    column = jnp.zeros((devices, rows), jnp.float32)
    for t in range(reach.shape[0]):
        hit = jnp.broadcast_to(reach[t : t + 1, :], (devices, rows)) == tile
        land = jnp.broadcast_to(landing[t : t + 1, :], (devices, rows)).astype(jnp.float32)
        named = named + jnp.where(hit, 1.0, 0.0)
        column = column + jnp.where(hit, land + 1.0, 0.0)
    first, second = iota((rows, rows), 0), iota((rows, rows), 1)
    earlier = (first < second).astype(jnp.bfloat16)
    count = jnp.dot(named.astype(jnp.bfloat16), earlier, preferred_element_type=jnp.float32)
    slot = jnp.where(named > 0.0, count, -1.0)
    rays = rows // centres
    tile = second % centres * rays + second // (rays // 2 * centres)
    tile += second // (8 * centres) % (rays // 16) * 16
    tile += second // (2 * centres) % 4 * 4 + second // centres % 2 * 2
    order = (first == tile).astype(jnp.bfloat16)
    moved = jnp.dot(slot.astype(jnp.bfloat16), order, preferred_element_type=jnp.float32)
    wide = jnp.broadcast_to(moved[:, None, :], (devices, 8, rows)).reshape(devices * 8, rows)
    row = iota((devices * 8, rows), 0) % 8
    pick[...] = (wide == row.astype(jnp.float32)).astype(jnp.bfloat16)
    ninth[...] = (moved == 8.0).astype(jnp.bfloat16)
    lane = iota((devices, 128), 1)
    table = jnp.zeros((devices, 128), jnp.float32)
    for k in range(SLOTS):
        value = jnp.sum(jnp.where(slot == k, column, 0.0), axis=1, keepdims=True)
        table = jnp.where(lane == k, value, table)
    keys[...] = table - 1.0


def place_kernel(incoming, image, ninth):
    devices = incoming.shape[0]
    tail = incoming[:, 64:80, :].astype(jnp.float32)
    tags = tail[:, 8:16, :]
    ninth[...] = tail[:, 0:8, :].reshape(devices * 8, 128)
    lane = iota((devices, 128), 1)
    hit9 = (tags[:, 0, :][:, 8:9] == lane.astype(jnp.float32)).astype(jnp.bfloat16)
    tags = jnp.concatenate([tags, tags], 1).reshape(devices * 16, 128)
    lane = iota((devices * 16, 128), 1)
    row = iota((devices * 16, 128), 0) % 16
    key = jnp.sum(jnp.where(lane == row % 8, tags, 0.0), axis=1, keepdims=True)
    hit = key == lane.astype(jnp.float32)
    both = jnp.concatenate(
        [
            (hit & (row < 8)).astype(jnp.bfloat16),
            (hit & (row >= 8)).astype(jnp.bfloat16),
        ],
        1,
    )
    contract = (((0,), (0,)), ((), ()))
    for k in range(4):
        rows = incoming[:, 16 * k : 16 * (k + 1), :].reshape(devices * 16, 128)
        y = lax.dot_general(rows, both, contract, preferred_element_type=jnp.float32)
        for q in range(2):
            last = ninth[pl.ds(2 * k + q, devices, stride=8), :].astype(jnp.bfloat16)
            last = lax.dot_general(last, hit9, contract, preferred_element_type=jnp.float32)
            cut = 256 * k + 128 * q
            image[cut : cut + 128, :] = y[:, 128 * q : 128 * (q + 1)] + last


def vmem(count):
    return [pl.BlockSpec(memory_space=pltpu.VMEM)] * count


def near(*arrays):
    return tuple(pltpu.with_memory_space_constraint(array, pltpu.VMEM) for array in arrays)


def call(kernel, shapes, args, scratch=(), specs=(), flops=0):
    return pl.pallas_call(
        kernel,
        out_shape=shapes,
        in_specs=list(specs) + vmem(len(args) - len(specs)),
        out_specs=jax.tree.map(lambda _: pl.BlockSpec(memory_space=pltpu.VMEM), shapes),
        scratch_shapes=list(scratch),
        cost_estimate=pl.CostEstimate(flops=flops, bytes_accessed=0, transcendentals=0),
        compiler_params=pltpu.CompilerParams(vmem_limit_bytes=56 * 1024 * 1024),
    )(*args)


def on_device(traces, taper, ray_param, reach, landing, travel_time, amplitude):
    f32, bf16 = jnp.float32, jnp.bfloat16
    freqs = traces.shape[2] // 2
    window = taper.shape[0]
    half = window // 2
    rays = ray_param.shape[0]
    rows = traces.shape[1]
    centres = rows // half
    depth = travel_time.shape[1]
    reach_count = reach.shape[2]
    line_count, size = lax.axis_size("line"), lax.axis_size("xline")
    devices = line_count * size
    coarse = freqs // FINE
    factor = 1.0 / math.sqrt(2.0 * freqs * centres * rays * reach_count / X)

    own = traces[0]
    beam_count = centres * rays
    edge = (half // 2, 2 * freqs)
    last, first, mine = call(
        functools.partial(open_kernel, math.pi / (2 * freqs), factor),
        (
            pltpu.VMEM(edge, bf16),
            pltpu.VMEM(edge, bf16),
            pltpu.VMEM((size, 4 * depth // 128, 128), f32),
        ),
        (own, travel_time, amplitude),
        [pltpu.VMEM((2,) + travel_time.shape, f32), pltpu.SemaphoreType.DMA((4,))],
        [pl.BlockSpec(memory_space=pl.ANY)] * 3,
    )
    pick, pick9, keys = call(
        functools.partial(route_kernel, centres),
        (
            pltpu.VMEM((8 * devices, beam_count), bf16),
            pltpu.VMEM((devices, beam_count), bf16),
            pltpu.VMEM((devices, 128), f32),
        ),
        (reach[0].T, landing[0].T),
        flops=100_000_000,
    )
    up = [(i, i + 1) for i in range(size - 1)]
    down = [(j, i) for i, j in up]
    before = lax.ppermute(last, "xline", up)
    after = lax.ppermute(first, "xline", down)
    times = lax.all_to_all(mine, "xline", split_axis=0, concat_axis=0, tiled=True)
    times = times.reshape(size // 8, 8 * mine.shape[1], 128)

    at = np.arange(256)
    fold = fold_matrix()[at // 16 % 2 * 128 + at // 32 * 16 + at % 16]
    folded = call(
        slant_kernel,
        pltpu.VMEM((rays, 2 * coarse * centres, FINE), f32),
        (
            *near(before),
            own,
            *near(after),
            taper[None],
            ray_param[None],
            jnp.asarray(fold, bf16),
        ),
        [
            pltpu.VMEM((rows + half, 2 * freqs), bf16),
            pltpu.VMEM((freqs // 16, 4 * half, 128), bf16),
            pltpu.VMEM((freqs // 16, rays, 128), f32),
        ],
        flops=8_000_000_000,
    )
    outgoing = call(
        functools.partial(project_kernel, coarse, centres),
        pltpu.VMEM((devices, 80, 128), bf16),
        near(times, folded, pick, pick9, keys),
        [
            pltpu.VMEM((2, depth // 128, 128, 128), f32),
            pltpu.VMEM((2, 16, depth), f32),
            pltpu.VMEM((2, 16 * coarse, depth), f32),
            pltpu.VMEM((beam_count // (2 * centres), 2 * centres, depth), f32),
            pltpu.VMEM((devices * 8, 128), f32),
        ],
    )
    incoming = lax.all_to_all(
        outgoing, ("line", "xline"), split_axis=0, concat_axis=0, tiled=True
    )
    image = call(
        place_kernel,
        jax.ShapeDtypeStruct((depth, X), f32),
        near(incoming),
        [pltpu.VMEM((8 * devices, 128), f32)],
    )
    return image[None]


def solution(mesh):
    placed = (
        P("line", "xline", None),
        P(),
        P(),
        P("line", "xline", None),
        P("line", "xline", None),
        P("xline", None),
        P("xline", None),
    )
    return jax.shard_map(
        on_device, mesh=mesh, in_specs=placed, out_specs=P("line", None, "xline"), check_vma=False
    )
```

```python
import functools
import math

import jax
import jax.numpy as jnp
import numpy as np
from jax import lax
from jax.experimental import pallas as pl
from jax.experimental.pallas import tpu as pltpu
from jax.sharding import PartitionSpec as P

X = 128
FINE = 128
SLOTS = 9
BATCH = 8


def iota(shape, dim):
    return lax.broadcasted_iota(jnp.int32, shape, dim)


def fold_matrix():
    half = FINE // 2
    plus = np.zeros((FINE, half), np.float32)
    minus = np.zeros((FINE, half), np.float32)
    for m in range(half):
        plus[half + m, m] = plus[half - 1 - m, m] = 1.0
        minus[half + m, m], minus[half - 1 - m, m] = 1.0, -1.0
    zero = np.zeros_like(plus)
    real = np.concatenate([plus, zero, zero, -minus], 1)
    imag = np.concatenate([zero, minus, plus, zero], 1)
    return np.concatenate([real, imag], 0)


def pick_column(row, at):
    hit = iota((at.shape[0], row.shape[1]), 1) == at
    return jnp.sum(jnp.where(hit, row, 0.0), axis=1, keepdims=True)


def slant_kernel(before, own, after, taper, ray, fold, out, data, rows, beams):
    half = before.shape[0] * 2
    window = 2 * half
    rays = ray.shape[1]
    freqs = own.shape[1] // 2
    centres = own.shape[0] // half
    blocks = freqs // 128
    data[: half // 2] = before[...]
    data[half // 2 : half // 2 + own.shape[0]] = own[...]
    data[half // 2 + own.shape[0] :] = after[...]

    weight = taper[...] * (1.0 / math.sqrt(window))
    place = iota((half, 1), 0)
    high_weight = pick_column(weight, half + place)
    low_weight = pick_column(weight, half - 1 - place)
    flip = (iota((half, half), 0) + iota((half, half), 1) == half - 1).astype(jnp.bfloat16)
    lane = iota((half, 128), 1)
    even = lane % 2 == 0
    side = lane % 32 < 16
    column = iota((1, 256), 1)
    source = column // 16 % 2 * 128 + column // 32 * 16 + column % 16
    order = (iota((256, 256), 0) == source).astype(jnp.bfloat16)

    def prepare(block):
        sums, turns = [], []
        for n in range(centres):
            parts = [
                data[n * half : n * half + window, part * freqs + block * 128 :][:, :128]
                for part in range(2)
            ]
            moved = jnp.dot(
                jnp.concatenate(parts, 1), order, preferred_element_type=jnp.float32
            )
            low = moved[:half].astype(jnp.bfloat16)
            low = jnp.dot(flip, low, preferred_element_type=jnp.float32) * low_weight
            high = moved[half:] * high_weight
            for value, into in ((high + low, sums), (high - low, turns)):
                for cut in (0, 128):
                    tile = value[:, cut : cut + 128]
                    if into is turns:
                        tile = jnp.where(side, pltpu.roll(tile, 112, 1), -pltpu.roll(tile, 16, 1))
                    into.append(pltpu.roll(tile, 32 * n, 1) if n else tile)
        for g in range(8):
            plus, minus = (
                functools.reduce(
                    lambda x, c: jnp.where(lane // 32 == c, table[(c - g) % centres * 2 + g // 4], x),
                    range(1, centres),
                    table[-g % centres * 2 + g // 4],
                )
                for table in (sums, turns)
            )
            stack = [
                jnp.where(even, plus, 0.0),
                jnp.where(even, 0.0, plus),
                jnp.where(even, minus, 0.0),
                jnp.where(even, 0.0, minus),
            ]
            rows[block * 8 + g] = jnp.concatenate(stack, 0).astype(jnp.bfloat16)

    slow = pick_column(ray[...], iota((rays, 1), 0))
    lanes = iota((rays, 128), 1)
    offset = (lanes % half).astype(jnp.float32) + 0.5
    angle = slow * offset * (math.pi / freqs)
    c1, s1 = jnp.cos(angle), jnp.sin(angle)
    cs, ss = 1.0 - 2.0 * s1 * s1, 2.0 * s1 * c1
    first = lanes < half
    pair = lanes % 16 // 2

    def one_group(g, state):
        c, s = state
        total = jnp.zeros((rays, 128), jnp.float32)
        for start in range(0, 8, BATCH):
            steer = []
            for _ in range(BATCH):
                steer.append(jnp.concatenate([c, s], 1).astype(jnp.bfloat16))
                c, s = c * cs - s * ss, s * cs + c * ss
            y = jnp.dot(
                jnp.concatenate(steer, 0), rows[g], preferred_element_type=jnp.float32
            )
            for q in range(BATCH):
                total = jnp.where(pair == start + q, y[q * rays : (q + 1) * rays], total)
        beams[g] = total
        return c, s

    flat = out.reshape(rays * out.shape[1], 128)
    def finish(block):
        fine, rest = [], []
        for n in range(centres):
            tiles = []
            for first_group in (block * 8, block * 8 + 4):
                tile = beams[first_group + -n % centres]
                for c in range(1, centres):
                    tile = jnp.where(lanes // 32 == c, beams[first_group + (c - n) % centres], tile)
                tiles.append(pltpu.roll(tile, 128 - 32 * n, 1) if n else tile)
            value = jnp.concatenate(tiles, 1)
            fine.append(value.astype(jnp.bfloat16).astype(jnp.float32))
            rest.append(value - fine[-1])
        folded = jnp.dot(
            jnp.concatenate(fine + rest, 0).astype(jnp.bfloat16),
            fold[...],
            preferred_element_type=jnp.float32,
        )
        folded = folded[: centres * rays] + folded[centres * rays :]
        for n in range(centres):
            for v in range(2):
                row = (2 * block + v) * centres + n
                value = folded[n * rays : (n + 1) * rays, 128 * v : 128 * (v + 1)]
                flat[pl.ds(row, rays, stride=out.shape[1]), :] = value

    state = (jnp.where(first, c1, cs), jnp.where(first, s1, ss))
    prepare(0)
    for block in range(blocks):
        if block + 1 < blocks:
            prepare(block + 1)
        for g in range(8):
            state = one_group(block * 8 + g, state)
        if block > 0:
            finish(block - 1)
    finish(blocks - 1)


def project_kernel(coarse, centres, times, folded, pick, pick9, keys, out, seed, step, outer, proj, ninth):
    half = FINE // 2
    blocks = seed.shape[0]
    bases = times.shape[0]
    upper = iota((2 * centres, 128), 0) < centres

    def one_group(base, r):
        for zb in range(blocks):
            cols = slice(zb * 128, zb * 128 + 128)
            s0 = times[base, pl.ds(8 * r + zb, 8, stride=32), :]
            amp = times[base, pl.ds(16 + 8 * r + zb, 8, stride=32), :]
            c0 = jnp.sqrt(1.0 - s0 * s0)
            c1, s1 = 1.0 - 2.0 * s0 * s0, 2.0 * s0 * c0
            c, s = c0, s0
            for m in range(8):
                seed[zb, m * 8 : m * 8 + 8, :] = c
                seed[zb, 64 + m * 8 : 72 + m * 8, :] = s
                if m < 7:
                    c, s = c * c1 - s * s1, s * c1 + c * s1
            c, s = c1, s1
            for power in range(6):
                c, s = 1.0 - 2.0 * s * s, 2.0 * s * c
                if power == 2:
                    step[0:8, cols] = c
                    step[8:16, cols] = s
            ca, sa = (c * c0 - s * s0) * amp, (s * c0 + c * s0) * amp
            cb, sb = 1.0 - 2.0 * s * s, 2.0 * s * c
            for a in range(coarse):
                outer[16 * a : 16 * a + 8, cols] = ca
                outer[16 * a + 8 : 16 * a + 16, cols] = sa
                ca, sa = ca * cb - sa * sb, sa * cb + ca * sb
        held = [None] * blocks
        for i in range(8):
            p = base * 16 + 2 * i + r
            rows = folded[p].astype(jnp.bfloat16)
            for zb in range(blocks):
                cols = slice(zb * 128, zb * 128 + 128)
                c = seed[zb, pl.ds(i, 8, stride=8), :]
                s = seed[zb, pl.ds(64 + i, 8, stride=8), :]
                cs = jnp.broadcast_to(step[i : i + 1, cols], (8, 128))
                ss = jnp.broadcast_to(step[8 + i : 9 + i, cols], (8, 128))
                real, imag = [c], [s]
                for _ in range(half // 8 - 1):
                    c, s = c * cs - s * ss, s * cs + c * ss
                    real.append(c)
                    imag.append(s)
                weights = jnp.concatenate(real + imag, 0).astype(jnp.bfloat16)
                parts = jnp.dot(rows, weights, preferred_element_type=jnp.float32)
                total = jnp.zeros(upper.shape, jnp.float32)
                for a in range(coarse):
                    turn = jnp.where(
                        upper,
                        jnp.broadcast_to(outer[16 * a + i : 16 * a + i + 1, cols], upper.shape),
                        jnp.broadcast_to(outer[16 * a + 8 + i : 16 * a + 9 + i, cols], upper.shape),
                    )
                    total = total + parts[2 * centres * a : 2 * centres * (a + 1)] * turn
                total = total + pltpu.roll(total, centres, 0)
                if i % 2 == 0:
                    held[zb] = total
                else:
                    tile = (r * bases + base) * 4 + i // 2
                    proj[tile, :, cols] = jnp.where(upper, held[zb], total)

    def one_base(base, carry):
        one_group(base, 0)
        one_group(base, 1)
        return carry

    lax.fori_loop(0, bases, one_base, 0, unroll=4)

    sends = proj[...].reshape(-1, 128 * blocks).astype(jnp.bfloat16)
    devices = keys.shape[0]
    for k in range(4):
        y = jnp.dot(pick[...], sends[:, 256 * k : 256 * (k + 1)], preferred_element_type=jnp.float32)
        pair = [y[:, :128].reshape(devices, 8, 128), y[:, 128:].reshape(devices, 8, 128)]
        out[:, 16 * k : 16 * (k + 1), :] = jnp.concatenate(pair, 1).astype(jnp.bfloat16)
    last = jnp.dot(pick9[...], sends, preferred_element_type=jnp.float32)
    for k in range(8):
        ninth[pl.ds(k, devices, stride=8), :] = last[:, 128 * k : 128 * (k + 1)]
    tags = jnp.broadcast_to(keys[...][:, None, :], (devices, 8, 128))
    pair = [ninth[...].reshape(devices, 8, 128), tags]
    out[:, 64:80, :] = jnp.concatenate(pair, 1).astype(jnp.bfloat16)


def open_kernel(scale, factor, own, times, amps, up, down, mine, held, sems):
    edge = up.shape[0]
    pairs = [
        (times, held.at[0]),
        (amps, held.at[1]),
        (own.at[own.shape[0] - edge :], up),
        (own.at[:edge], down),
    ]
    copies = [pltpu.make_async_copy(x, y, sems.at[k]) for k, (x, y) in enumerate(pairs)]
    for copy in copies:
        copy.start()
    copies[0].wait()
    copies[1].wait()
    tables = (jnp.sin(held[0] * scale), held[1] * factor)
    rows = [table[r : r + 1, :] for table in tables for r in range(held.shape[1])]
    lanes = range(0, held.shape[2], 128)
    tile = jnp.concatenate([row[:, at : at + 128] for row in rows for at in lanes], 0)
    mine[...] = jnp.broadcast_to(tile[None], mine.shape)
    copies[2].wait()
    copies[3].wait()


def route_kernel(centres, reach, landing, pick, ninth, keys):
    devices, rows = ninth.shape
    tile = iota((devices, rows), 0)
    named = jnp.zeros((devices, rows), jnp.float32)
    column = jnp.zeros((devices, rows), jnp.float32)
    for t in range(reach.shape[0]):
        hit = jnp.broadcast_to(reach[t : t + 1, :], (devices, rows)) == tile
        land = jnp.broadcast_to(landing[t : t + 1, :], (devices, rows)).astype(jnp.float32)
        named = named + jnp.where(hit, 1.0, 0.0)
        column = column + jnp.where(hit, land + 1.0, 0.0)
    first, second = iota((rows, rows), 0), iota((rows, rows), 1)
    earlier = (first < second).astype(jnp.bfloat16)
    count = jnp.dot(named.astype(jnp.bfloat16), earlier, preferred_element_type=jnp.float32)
    slot = jnp.where(named > 0.0, count, -1.0)
    rays = rows // centres
    tile = second % centres * rays + second // (rays // 2 * centres)
    tile += second // (8 * centres) % (rays // 16) * 16
    tile += second // (2 * centres) % 4 * 4 + second // centres % 2 * 2
    order = (first == tile).astype(jnp.bfloat16)
    moved = jnp.dot(slot.astype(jnp.bfloat16), order, preferred_element_type=jnp.float32)
    wide = jnp.broadcast_to(moved[:, None, :], (devices, 8, rows)).reshape(devices * 8, rows)
    row = iota((devices * 8, rows), 0) % 8
    pick[...] = (wide == row.astype(jnp.float32)).astype(jnp.bfloat16)
    ninth[...] = (moved == 8.0).astype(jnp.bfloat16)
    lane = iota((devices, 128), 1)
    table = jnp.zeros((devices, 128), jnp.float32)
    for k in range(SLOTS):
        value = jnp.sum(jnp.where(slot == k, column, 0.0), axis=1, keepdims=True)
        table = jnp.where(lane == k, value, table)
    keys[...] = table - 1.0


def place_kernel(incoming, image, ninth):
    devices = incoming.shape[0]
    tail = incoming[:, 64:80, :].astype(jnp.float32)
    tags = tail[:, 8:16, :]
    ninth[...] = tail[:, 0:8, :].reshape(devices * 8, 128)
    lane = iota((devices, 128), 1)
    hit9 = (tags[:, 0, :][:, 8:9] == lane.astype(jnp.float32)).astype(jnp.bfloat16)
    tags = jnp.concatenate([tags, tags], 1).reshape(devices * 16, 128)
    lane = iota((devices * 16, 128), 1)
    row = iota((devices * 16, 128), 0) % 16
    key = jnp.sum(jnp.where(lane == row % 8, tags, 0.0), axis=1, keepdims=True)
    hit = key == lane.astype(jnp.float32)
    both = jnp.concatenate(
        [
            (hit & (row < 8)).astype(jnp.bfloat16),
            (hit & (row >= 8)).astype(jnp.bfloat16),
        ],
        1,
    )
    contract = (((0,), (0,)), ((), ()))
    for k in range(4):
        rows = incoming[:, 16 * k : 16 * (k + 1), :].reshape(devices * 16, 128)
        y = lax.dot_general(rows, both, contract, preferred_element_type=jnp.float32)
        for q in range(2):
            last = ninth[pl.ds(2 * k + q, devices, stride=8), :].astype(jnp.bfloat16)
            last = lax.dot_general(last, hit9, contract, preferred_element_type=jnp.float32)
            cut = 256 * k + 128 * q
            image[cut : cut + 128, :] = y[:, 128 * q : 128 * (q + 1)] + last


def vmem(count):
    return [pl.BlockSpec(memory_space=pltpu.VMEM)] * count


def near(*arrays):
    return tuple(pltpu.with_memory_space_constraint(array, pltpu.VMEM) for array in arrays)


def call(kernel, shapes, args, scratch=(), specs=(), flops=0):
    return pl.pallas_call(
        kernel,
        out_shape=shapes,
        in_specs=list(specs) + vmem(len(args) - len(specs)),
        out_specs=jax.tree.map(lambda _: pl.BlockSpec(memory_space=pltpu.VMEM), shapes),
        scratch_shapes=list(scratch),
        cost_estimate=pl.CostEstimate(flops=flops, bytes_accessed=0, transcendentals=0),
        compiler_params=pltpu.CompilerParams(vmem_limit_bytes=56 * 1024 * 1024),
    )(*args)


def on_device(traces, taper, ray_param, reach, landing, travel_time, amplitude):
    f32, bf16 = jnp.float32, jnp.bfloat16
    freqs = traces.shape[2] // 2
    window = taper.shape[0]
    half = window // 2
    rays = ray_param.shape[0]
    rows = traces.shape[1]
    centres = rows // half
    depth = travel_time.shape[1]
    reach_count = reach.shape[2]
    line_count, size = lax.axis_size("line"), lax.axis_size("xline")
    devices = line_count * size
    coarse = freqs // FINE
    factor = 1.0 / math.sqrt(2.0 * freqs * centres * rays * reach_count / X)

    own = traces[0]
    beam_count = centres * rays
    edge = (half // 2, 2 * freqs)
    last, first, mine = call(
        functools.partial(open_kernel, math.pi / (2 * freqs), factor),
        (
            pltpu.VMEM(edge, bf16),
            pltpu.VMEM(edge, bf16),
            pltpu.VMEM((size, 4 * depth // 128, 128), f32),
        ),
        (own, travel_time, amplitude),
        [pltpu.VMEM((2,) + travel_time.shape, f32), pltpu.SemaphoreType.DMA((4,))],
        [pl.BlockSpec(memory_space=pl.ANY)] * 3,
    )
    pick, pick9, keys = call(
        functools.partial(route_kernel, centres),
        (
            pltpu.VMEM((8 * devices, beam_count), bf16),
            pltpu.VMEM((devices, beam_count), bf16),
            pltpu.VMEM((devices, 128), f32),
        ),
        (reach[0].T, landing[0].T),
        flops=100_000_000,
    )
    up = [(i, i + 1) for i in range(size - 1)]
    down = [(j, i) for i, j in up]
    before = lax.ppermute(last, "xline", up)
    after = lax.ppermute(first, "xline", down)
    times = lax.all_to_all(mine, "xline", split_axis=0, concat_axis=0, tiled=True)
    times = times.reshape(size // 8, 8 * mine.shape[1], 128)

    at = np.arange(256)
    fold = fold_matrix()[at // 16 % 2 * 128 + at // 32 * 16 + at % 16]
    folded = call(
        slant_kernel,
        pltpu.VMEM((rays, 2 * coarse * centres, FINE), f32),
        (
            *near(before),
            own,
            *near(after),
            taper[None],
            ray_param[None],
            jnp.asarray(fold, bf16),
        ),
        [
            pltpu.VMEM((rows + half, 2 * freqs), bf16),
            pltpu.VMEM((freqs // 16, 4 * half, 128), bf16),
            pltpu.VMEM((freqs // 16, rays, 128), f32),
        ],
        flops=8_000_000_000,
    )
    outgoing = call(
        functools.partial(project_kernel, coarse, centres),
        pltpu.VMEM((devices, 80, 128), bf16),
        near(times, folded, pick, pick9, keys),
        [
            pltpu.VMEM((depth // 128, 128, 128), f32),
            pltpu.VMEM((16, depth), f32),
            pltpu.VMEM((16 * coarse, depth), f32),
            pltpu.VMEM((beam_count // (2 * centres), 2 * centres, depth), f32),
            pltpu.VMEM((devices * 8, 128), f32),
        ],
    )
    incoming = lax.all_to_all(
        outgoing, ("line", "xline"), split_axis=0, concat_axis=0, tiled=True
    )
    image = call(
        place_kernel,
        jax.ShapeDtypeStruct((depth, X), f32),
        near(incoming),
        [pltpu.VMEM((8 * devices, 128), f32)],
    )
    return image[None]


def solution(mesh):
    placed = (
        P("line", "xline", None),
        P(),
        P(),
        P("line", "xline", None),
        P("line", "xline", None),
        P("xline", None),
        P("xline", None),
    )
    return jax.shard_map(
        on_device, mesh=mesh, in_specs=placed, out_specs=P("line", None, "xline"), check_vma=False
    )
```
